128 devices in a mesh: section: 2 (over y_hi), expert: 8 (over z, core), hid: 8 (over x, y_lo).
Axes of the slice: x: 4, y: 4 (y_hi: 2, y_lo: 2; y = y_hi * 2 + y_lo), z: 4, core: 2. Of those that a mesh axis runs over, the one named last changes fastest.
Arguments:
- saved_input: bfloat16 [2, 1024, 4096], P('section', 'expert', 'hid'), may hold values from -6 to 6
- cotangent: bfloat16 [2, 1024, 4096], P('section', 'expert', 'hid'), may hold values from -6 to 6
- next_input: bfloat16 [2, 1024, 4096], P('section', 'expert', 'hid'), may hold values from -6 to 6
- routes_saved: int32 [2, 1024, 2], P('section', 'expert'), may hold values from 0 to 7, all different within a row; in each aligned block of 128 rows (0 to 127, 128 to 255, ..., all dimensions but the last counted through in order) at most 48 rows name the same one
- routes_next: int32 [2, 1024, 2], P('section', 'expert'), may hold values from 0 to 7, all different within a row; in each aligned block of 128 rows (0 to 127, 128 to 255, ..., all dimensions but the last counted through in order) at most 48 rows name the same one
- norm_gain: float32 [2, 4096], P('section', 'hid'), may hold values from 0.1 to 1.9
- router: float32 [2, 4096, 8], P('section', 'hid'), may hold values from -0.18 to 0.18
- expert_gate: bfloat16 [2, 8, 4096, 7168], P('section', 'expert', None, 'hid'), may hold values from -0.09375 to 0.09375
- expert_up: bfloat16 [2, 8, 4096, 7168], P('section', 'expert', None, 'hid'), may hold values from -0.09375 to 0.09375
- expert_down: bfloat16 [2, 8, 7168, 4096], P('section', 'expert', 'hid'), may hold values from -0.0625 to 0.0625
Outputs:
- leaving: bfloat16 [2, 1024, 4096], P('section', 'expert', 'hid')
- arriving: bfloat16 [2, 1024, 4096], P('section', 'expert', 'hid')
The draws below stay inside these ranges and needn't reach their ends.
Inputs may be any that keep to these rules, and one draw needn't show every extreme that they name: `routes_saved`: A token's two ids differ. In each aligned block of 128 tokens of a section no expert is named by more than 48 tokens, and some block names some expert exactly 48 times. `routes_next`: A token's two ids differ. In each aligned block of 128 tokens of a section no expert is named by more than 48 tokens, and some block names some expert exactly 48 times.
All inputs are finite; a program needn't handle non-finite values.
Results may differ from the reference program's by a relative error of at most 0.0052.
Values may be sent and summed in bfloat16 or wider, within the bound.
No kernel may reach another device: no remote copies, remote signals or barrier semaphores. Data moves between devices by JAX's collectives and lax.ppermute only.
A program may use at most 128 MiB of HBM per device.

```python
import math
import jax
import jax.numpy as jnp
import numpy as np
from jax import lax

D = 4096
FF = 7168
TOK_DEV = 128
EXPERTS = 8
CAP = 48
TOKENS = 1024
N_SECTION = 2
N_EXPERT = 8


def block_levels(key, shape, split, low, top_value):
    factor_of, own = 1.0, jax.random.fold_in(key, 6)
    for position, blocks in split:
        heights = jnp.exp(jax.random.uniform(jax.random.fold_in(own, position), (blocks,), jnp.float32, low / len(split), top_value / len(split)))
        factor_of = factor_of * jnp.repeat(heights, shape[position] // blocks).reshape([-1 if axis == position else 1 for axis in range(len(shape))])
    return factor_of


def shared_out(rng, own, number, rows, count, top, reach, lean):
    ranking = jax.random.permutation(rng, count)
    crowded, ordinary = portions_of(count, rows * top, reach, lean, True), portions_of(count, rows * top, reach, lean, False)
    places = jnp.arange(count)

    def named(tallies, offset_by):
        used = int((tallies > 0).sum())
        fixed = max(1, used // 4)
        passed = fixed + (places - fixed + offset_by * (used - fixed)) % max(1, count - fixed)
        return jnp.zeros((count,), jnp.int32).at[ranking[jnp.where(places < fixed, places, passed)]].set(jnp.asarray(tallies, jnp.int32))

    tallies = jnp.where(number % 4 == 0, named(crowded, number // 4), named(ordinary, number - number // 4 - 1))
    mixed = jax.random.permutation(jax.random.fold_in(own, 3), count)
    source_of, taker = mixed[0:count // 2 * 2:2], mixed[1:count // 2 * 2:2]
    margin = jnp.minimum(tallies[source_of] - 1, reach - tallies[taker]) // 2
    margin = jnp.where((source_of == ranking[0]) | (taker == ranking[0]) | (tallies[taker] == 0), 0, jnp.maximum(margin, 0))
    passed = jax.random.randint(jax.random.fold_in(own, 4), (count // 2,), 0, 1 << 20) % (margin + 1)
    tallies = tallies.at[source_of].add(-passed).at[taker].add(passed)
    items = jnp.searchsorted(jnp.cumsum(tallies), jnp.arange(rows * top), side="right").astype(jnp.int32)
    table = items.reshape(top, rows).T
    table = table[jax.random.permutation(jax.random.fold_in(own, 1), rows)]
    offset_by = jax.random.randint(jax.random.fold_in(own, 2), (rows, 1), 0, top)
    return jnp.take_along_axis(table, (jnp.arange(top)[None, :] + offset_by) % top, axis=1)


def portions_of(amount, total, reach, slope, full):
    weights = [(1 << 20) // math.isqrt(grade ** slope) + 1 for grade in range(1, amount + 1)]
    largest = reach if full else min(reach, max(-(-total // amount), total * weights[0] // sum(weights)))
    least = 1 if total - largest >= amount - 1 else 0
    holding, spare = [largest] + [least] * (amount - 1), total - largest - least * (amount - 1)
    while spare > 0:
        candidates = [i for i in range(1, amount) if holding[i] < largest] or [i for i in range(1, amount) if holding[i] < reach]
        pool, left = sum([weights[i] for i in candidates]), spare
        for i in candidates:
            more = min(reach - holding[i], max(1, left * weights[i] // pool), spare)
            holding[i] = holding[i] + more
            spare = spare - more
    return np.array(holding)


def normal_values(stream_key, extent, spread, limit, pieces=(), kind=jnp.bfloat16):
    drawn = jax.random.normal(stream_key, extent, jnp.float32) * spread
    if len(pieces) > 0:
        drawn = block_levels(stream_key, extent, pieces, -0.22, 0.18) * drawn
    return jnp.clip(drawn, min=-limit, max=limit).astype(kind)


def setup_inputs(seed: int = 0) -> dict:
    key_of = jax.random.split(jax.random.key(seed), 11)
    saved_input = normal_values(key_of[0], (N_SECTION, TOKENS, D), 1.0, 6.0, ((0, 2), (1, 8), (2, 8)))
    cotangent = normal_values(key_of[1], (N_SECTION, TOKENS, D), 1.0, 6.0, ((0, 2), (1, 8), (2, 8)))
    next_input = normal_values(key_of[2], (N_SECTION, TOKENS, D), 1.0, 6.0, ((0, 2), (1, 8), (2, 8)))
    routes_saved_keys = jax.random.split(jax.random.fold_in(key_of[3], 1), N_SECTION * TOKENS // TOK_DEV)
    routes_saved_turns = jax.random.permutation(jax.random.fold_in(key_of[3], 3), N_SECTION * TOKENS // TOK_DEV)
    routes_saved = jax.vmap(lambda own, number: shared_out(jax.random.fold_in(key_of[3], 2), own, number, TOK_DEV, EXPERTS, 2, CAP, 1))(routes_saved_keys, routes_saved_turns).reshape((N_SECTION, TOKENS, 2))
    routes_next_keys = jax.random.split(jax.random.fold_in(key_of[4], 1), N_SECTION * TOKENS // TOK_DEV)
    routes_next_turns = jax.random.permutation(jax.random.fold_in(key_of[4], 3), N_SECTION * TOKENS // TOK_DEV)
    routes_next = jax.vmap(lambda own, number: shared_out(jax.random.fold_in(key_of[4], 2), own, number, TOK_DEV, EXPERTS, 2, CAP, 1))(routes_next_keys, routes_next_turns).reshape((N_SECTION, TOKENS, 2))
    norm_gain = jnp.clip(1.0 + 0.18 * jax.random.normal(key_of[5], (N_SECTION, D), jnp.float32), 0.1, 1.9)
    router = normal_values(key_of[6], (N_SECTION, D, EXPERTS), 0.03, 0.18, ((0, 2), (1, 8)), jnp.float32)
    expert_gate = normal_values(key_of[7], (N_SECTION, EXPERTS, D, FF), D ** -0.5, 0.09375, ((0, 2), (1, 8), (3, 8)))
    expert_up = normal_values(key_of[8], (N_SECTION, EXPERTS, D, FF), D ** -0.5, 0.09375, ((0, 2), (1, 8), (3, 8)))
    expert_down = normal_values(key_of[9], (N_SECTION, EXPERTS, FF, D), FF ** -0.5, 0.0625, ((0, 2), (1, 8), (2, 8)))
    return {"saved_input": saved_input, "cotangent": cotangent, "next_input": next_input, "routes_saved": routes_saved, "routes_next": routes_next, "norm_gain": norm_gain, "router": router, "expert_gate": expert_gate, "expert_up": expert_up, "expert_down": expert_down}


EPSILON = 1e-05
HIGHEST = lax.Precision.HIGHEST

def norm_stats(inputs, gain, table):
    values = inputs.astype(jnp.float32)
    scale = lax.rsqrt(lax.optimization_barrier(jnp.sum(values * values, axis=1)) / D + EPSILON)
    scaled = values * scale[:, None] * gain[None, :]
    logits = jnp.dot(scaled, table, precision=HIGHEST)
    return (values, scale, scaled.astype(jnp.bfloat16), logits)

def placing(routes, logits):
    labels = jnp.arange(EXPERTS, dtype=jnp.int32)
    blocks = routes.reshape(N_EXPERT, TOK_DEV * 2).astype(jnp.int32)
    onehot = (blocks[:, :, None] == labels[None, None, :]).astype(jnp.int32)
    ranked = (jnp.cumsum(onehot, axis=1) - onehot).astype(jnp.int32)
    places = lax.optimization_barrier(jnp.sum(ranked * onehot, axis=2)).astype(jnp.int32)
    anchor = jnp.arange(N_EXPERT, dtype=jnp.int32)[:, None]
    targets = (blocks * (N_EXPERT * CAP) + anchor * CAP + places).astype(jnp.int32).reshape(TOKENS, 2)
    first_hit = (routes[:, 0:1] == labels[None, :]).astype(jnp.float32)
    second_hit = (routes[:, 1:2] == labels[None, :]).astype(jnp.float32)
    first_logit = lax.optimization_barrier(jnp.sum(logits * first_hit, axis=1))
    second_logit = lax.optimization_barrier(jnp.sum(logits * second_hit, axis=1))
    first_prob = jax.nn.sigmoid(first_logit - second_logit)
    second_prob = jax.nn.sigmoid(second_logit - first_logit)
    return (targets, first_prob, second_prob, first_hit - second_hit)

def spread_rows(targets, rows):
    total = EXPERTS * N_EXPERT * CAP
    doubled = jnp.repeat(rows, 2, axis=0)
    filled = jnp.zeros((total, rows.shape[1]), rows.dtype).at[targets.reshape(-1)].set(doubled)
    return filled.reshape(EXPERTS, N_EXPERT * CAP, rows.shape[1])

def blend(rows, targets, first_prob, second_prob):
    return first_prob[:, None] * rows[targets[:, 0]] + second_prob[:, None] * rows[targets[:, 1]]

def expert_rows(packed):
    saved_rows, cot_rows, next_rows, gate_matrix, up_matrix, down_matrix = packed
    gate_saved = jnp.dot(saved_rows, gate_matrix, preferred_element_type=jnp.float32)
    up_saved = jnp.dot(saved_rows, up_matrix, preferred_element_type=jnp.float32)
    grad_hidden = jnp.dot(cot_rows, down_matrix.T, preferred_element_type=jnp.float32)
    sig_saved = jax.nn.sigmoid(gate_saved)
    silu_saved = gate_saved * sig_saved
    hidden_saved = (silu_saved * up_saved).astype(jnp.bfloat16)
    row_dots = lax.optimization_barrier(jnp.sum(grad_hidden * hidden_saved.astype(jnp.float32), axis=1))
    grad_gate = (grad_hidden * up_saved * (sig_saved * (1.0 + gate_saved * (1.0 - sig_saved)))).astype(jnp.bfloat16)
    grad_up = (grad_hidden * silu_saved).astype(jnp.bfloat16)
    back_rows = jnp.dot(grad_gate, gate_matrix.T, preferred_element_type=jnp.float32) + jnp.dot(grad_up, up_matrix.T, preferred_element_type=jnp.float32)
    gate_next = jnp.dot(next_rows, gate_matrix, preferred_element_type=jnp.float32)
    up_next = jnp.dot(next_rows, up_matrix, preferred_element_type=jnp.float32)
    silu_next = gate_next * jax.nn.sigmoid(gate_next)
    hidden_next = (silu_next * up_next).astype(jnp.bfloat16)
    out_rows = jnp.dot(hidden_next, down_matrix, preferred_element_type=jnp.float32)
    return (back_rows, row_dots, out_rows)

def section_pass(saved, cotangent, upcoming, routes_saved, routes_next, gain, table, gate_all, up_all, down_all):
    values_saved, scale_saved, normed_saved, logits_saved = norm_stats(saved, gain, table)
    values_next, scale_next, normed_next, logits_next = norm_stats(upcoming, gain, table)
    targets_saved, first_saved, second_saved, diff_saved = placing(routes_saved, logits_saved)
    targets_next, first_next, second_next, diff_next = placing(routes_next, logits_next)
    buffer_saved = spread_rows(targets_saved, normed_saved)
    buffer_cot = spread_rows(targets_saved, cotangent)
    buffer_next = spread_rows(targets_next, normed_next)
    back_rows, row_dots, out_rows = lax.map(expert_rows, (buffer_saved, buffer_cot, buffer_next, gate_all, up_all, down_all))
    total = EXPERTS * N_EXPERT * CAP
    back_rows = back_rows.reshape(total, D)
    row_dots = row_dots.reshape(total)
    out_rows = out_rows.reshape(total, D)
    branch_next = blend(out_rows, targets_next, first_next, second_next)
    forward_out = (values_next + branch_next).astype(jnp.bfloat16)
    mixed_saved = blend(back_rows, targets_saved, first_saved, second_saved)
    grad_logit = (row_dots[targets_saved[:, 0]] - row_dots[targets_saved[:, 1]]) * first_saved * second_saved
    grad_normed = mixed_saved + jnp.dot(grad_logit[:, None] * diff_saved, table.T, precision=HIGHEST)
    scaled_grad = grad_normed * gain[None, :]
    inner = lax.optimization_barrier(jnp.sum(scaled_grad * values_saved, axis=1))
    cube = scale_saved * scale_saved * scale_saved
    grad_input = cotangent.astype(jnp.float32) + scale_saved[:, None] * scaled_grad - values_saved * cube[:, None] * (inner / D)[:, None]
    return (forward_out, grad_input.astype(jnp.bfloat16))

def reference(saved_input, cotangent, next_input, routes_saved, routes_next, norm_gain, router, expert_gate, expert_up, expert_down):
    forward_outs = []
    grad_inputs = []
    for section_index in range(N_SECTION):
        forward_out, grad_input = section_pass(saved_input[section_index], cotangent[section_index], next_input[section_index], routes_saved[section_index], routes_next[section_index], norm_gain[section_index], router[section_index], expert_gate[section_index], expert_up[section_index], expert_down[section_index])
        forward_outs.append(forward_out)
        grad_inputs.append(grad_input)
    leaving = jnp.stack([grad_inputs[0], forward_outs[1]])
    arriving = jnp.stack([grad_inputs[1], forward_outs[0]])
    return (leaving, arriving)
```

```python
import jax
import jax.numpy as jnp
from jax import lax
from jax.sharding import PartitionSpec as P

EPSILON = 1e-05
HIGHEST = lax.Precision.HIGHEST
CONTRACT = (((1,), (1,)), ((), ()))
BOTH = ("expert", "hid")


def partner(block, axis, bit):
    count = lax.axis_size(axis)
    route = []
    for low in range(count):
        high = low | 1 << bit
        if high != low and high < count:
            route += [(low, high), (high, low)]
    return lax.ppermute(block, axis, route)


def swap(block, axes):
    return lax.all_to_all(block, axes, split_axis=0, concat_axis=0, tiled=True)


def placing(routes, experts, capacity):
    tokens = routes.shape[0]
    labels = jnp.arange(experts, dtype=jnp.int32)
    onehot = (routes.reshape(-1)[:, None] == labels[None, :]).astype(jnp.bfloat16)
    order = jnp.arange(2 * tokens, dtype=jnp.int32)
    earlier = (order[None, :] < order[:, None]).astype(jnp.bfloat16)
    ranked = jnp.dot(earlier, onehot, preferred_element_type=jnp.float32)
    places = jnp.sum(ranked * onehot.astype(jnp.float32), axis=1).astype(jnp.int32)
    targets = routes * capacity + places.reshape(tokens, 2)
    slots = jnp.arange(experts * capacity, dtype=jnp.int32)
    first = targets[:, 0:1] == slots[None, :]
    second = targets[:, 1:2] == slots[None, :]
    hits = (routes[:, 0:1] == labels[None, :]).astype(jnp.float32) - (
        routes[:, 1:2] == labels[None, :]
    ).astype(jnp.float32)
    slot_map = ((targets[:, 0][None, :] == slots[:, None]) | (targets[:, 1][None, :] == slots[:, None])).astype(jnp.bfloat16)
    return (first.astype(jnp.float32), second.astype(jnp.float32), hits, slot_map)


def dispatch(slot_map, rows):
    experts, hids = lax.axis_size("expert"), lax.axis_size("hid")
    filled = jnp.dot(slot_map, rows, preferred_element_type=jnp.float32).astype(jnp.bfloat16)
    capacity, part = filled.shape[0] // experts, filled.shape[1]
    copies = jnp.broadcast_to(
        filled.reshape(experts, 1, capacity, part), (experts, hids, capacity, part)
    )
    moved = swap(copies.reshape(experts * hids, capacity, part), BOTH)
    return moved.reshape(experts, hids, capacity, part)


def flatten_rows(moved):
    blocks, groups, capacity, part = moved.shape
    return moved.transpose(0, 2, 1, 3).reshape(blocks * capacity, groups * part)


def normalise(moved, gains, column, width):
    values = moved.astype(jnp.float32)
    squares = jnp.sum(values * values, axis=(1, 3))
    scale = lax.rsqrt(squares / width + EPSILON)
    scaled = values * scale[:, None, :, None] * gains[None, :, None, :]
    logits = jnp.sum(scaled * column[None, :, None, :], axis=(1, 3))
    return (squares, logits, flatten_rows(scaled.astype(jnp.bfloat16)))


def send_back(rows):
    experts, hids = lax.axis_size("expert"), lax.axis_size("hid")
    capacity, part = rows.shape[0] // experts, rows.shape[1] // hids
    pieces = rows.reshape(experts, capacity, hids, part).transpose(0, 2, 1, 3)
    home = swap(pieces.reshape(experts * hids, capacity, part), BOTH)
    home = home.reshape(experts, hids, capacity, part).astype(jnp.float32)
    return jnp.sum(home, axis=1).reshape(experts * capacity, part)


def pick(selection, table):
    return jnp.dot(selection, table, precision=HIGHEST)


def per_device(
    saved_input,
    cotangent,
    next_input,
    routes_saved,
    routes_next,
    norm_gain,
    router,
    expert_gate,
    expert_up,
    expert_down,
):
    gain = norm_gain[0]
    table = router[0]
    gate_matrix = expert_gate[0, 0]
    up_matrix = expert_up[0, 0]
    down_matrix = expert_down[0, 0]
    width = gate_matrix.shape[0]
    tokens = saved_input.shape[1]
    experts, hids = lax.axis_size("expert"), lax.axis_size("hid")
    capacity = 3 * tokens // experts
    own = lax.axis_index("expert")

    first_next, second_next, hits_next, map_next = placing(routes_next[0], experts, capacity)
    first_saved, second_saved, hits_saved, map_saved = placing(routes_saved[0], experts, capacity)

    column = lax.dynamic_index_in_dim(table, own, 1, keepdims=False)
    params = jnp.broadcast_to(jnp.stack([gain, column])[None], (hids, 2, gain.shape[0]))
    params = swap(params, "hid")
    gains, column = params[:, 0], params[:, 1]

    moved_next = dispatch(map_next, next_input[0])
    moved_saved = dispatch(map_saved, saved_input[0])
    moved_cot = dispatch(map_saved, cotangent[0])

    _, logits_next, rows_next = normalise(moved_next, gains, column, width)
    gate_next = jnp.dot(rows_next, gate_matrix, preferred_element_type=jnp.float32)
    up_next = jnp.dot(rows_next, up_matrix, preferred_element_type=jnp.float32)
    hidden_next = (gate_next * jax.nn.sigmoid(gate_next) * up_next).astype(jnp.bfloat16)
    out_part = jnp.dot(hidden_next, down_matrix, preferred_element_type=jnp.float32)
    out_home = send_back(out_part.astype(jnp.bfloat16))

    squares_saved, logits_saved, rows_saved = normalise(moved_saved, gains, column, width)
    gate_saved = jnp.dot(rows_saved, gate_matrix, preferred_element_type=jnp.float32)
    up_saved = jnp.dot(rows_saved, up_matrix, preferred_element_type=jnp.float32)
    grad_hidden = lax.dot_general(
        flatten_rows(moved_cot), down_matrix, CONTRACT, preferred_element_type=jnp.float32
    )
    sig_saved = jax.nn.sigmoid(gate_saved)
    silu_saved = gate_saved * sig_saved
    hidden_saved = (silu_saved * up_saved).astype(jnp.bfloat16)
    row_dots = jnp.sum(grad_hidden * hidden_saved.astype(jnp.float32), axis=1)
    grad_gate = (
        grad_hidden * up_saved * (sig_saved * (1.0 + gate_saved * (1.0 - sig_saved)))
    ).astype(jnp.bfloat16)
    grad_up = (grad_hidden * silu_saved).astype(jnp.bfloat16)
    norm_dots = jnp.sum(
        grad_gate.astype(jnp.float32) * gate_saved + grad_up.astype(jnp.float32) * up_saved,
        axis=1,
    )
    scalars = jnp.stack(
        [
            row_dots.reshape(experts, capacity),
            norm_dots.reshape(experts, capacity),
            logits_saved,
            squares_saved,
            logits_next,
        ],
        axis=1,
    )
    count = scalars.shape[1]
    scalars = jnp.broadcast_to(scalars[:, None], (experts, hids, count, capacity))
    scalars = swap(scalars.reshape(experts * hids, count * capacity), BOTH)
    scalars = scalars.reshape(experts, hids, count, capacity)
    summed = jnp.sum(scalars[:, :, :2], axis=1)
    scalars = jnp.concatenate([summed, scalars[:, 0, 2:]], axis=1)
    scalars = scalars.transpose(0, 2, 1).reshape(experts * capacity, count)

    back_part = lax.dot_general(
        grad_gate, gate_matrix, CONTRACT, preferred_element_type=jnp.float32
    ) + lax.dot_general(grad_up, up_matrix, CONTRACT, preferred_element_type=jnp.float32)
    back_home = send_back(back_part.astype(jnp.bfloat16))

    one, two = pick(first_next, scalars[:, 4:5]), pick(second_next, scalars[:, 4:5])
    weights = jax.nn.sigmoid(one - two) * first_next + jax.nn.sigmoid(two - one) * second_next
    values_next = next_input[0].astype(jnp.float32)
    forward_out = (values_next + pick(weights, out_home)).astype(jnp.bfloat16)

    one, two = pick(first_saved, scalars), pick(second_saved, scalars)
    prob_one = jax.nn.sigmoid(one[:, 2] - two[:, 2])
    prob_two = jax.nn.sigmoid(two[:, 2] - one[:, 2])
    scale = lax.rsqrt(one[:, 3] / width + EPSILON)
    grad_logit = (one[:, 0] - two[:, 0]) * prob_one * prob_two
    weights = prob_one[:, None] * first_saved + prob_two[:, None] * second_saved
    grad_normed = pick(weights, back_home) + jnp.dot(
        grad_logit[:, None] * hits_saved, table.T, precision=HIGHEST
    )
    inner = prob_one * one[:, 1] + prob_two * two[:, 1] + grad_logit * (one[:, 2] - two[:, 2])
    values_saved = saved_input[0].astype(jnp.float32)
    grad_input = (
        cotangent[0].astype(jnp.float32)
        + scale[:, None] * (grad_normed * gain[None, :])
        - values_saved * (scale * scale * (inner / width))[:, None]
    ).astype(jnp.bfloat16)

    first_section = lax.axis_index("section") == 0
    outgoing = jnp.where(first_section, forward_out, grad_input)
    leaving = jnp.where(first_section, grad_input, forward_out)
    arriving = partner(outgoing, "section", 0)
    return (leaving[None], arriving[None])


def solution(mesh):
    placed = (
        P("section", "expert", "hid"),
        P("section", "expert", "hid"),
        P("section", "expert", "hid"),
        P("section", "expert", None),
        P("section", "expert", None),
        P("section", "hid"),
        P("section", "hid", None),
        P("section", "expert", None, "hid"),
        P("section", "expert", None, "hid"),
        P("section", "expert", "hid", None),
    )
    return jax.shard_map(
        per_device,
        mesh=mesh,
        in_specs=placed,
        out_specs=(P("section", "expert", "hid"), P("section", "expert", "hid")),
        check_vma=False,
    )
```

```python
import functools

import jax
import jax.numpy as jnp
from jax import lax
from jax.experimental import pallas as pl
from jax.experimental.pallas import tpu as pltpu
from jax.sharding import PartitionSpec as P

EPSILON = 1e-05
HIGHEST = lax.Precision.HIGHEST
CONTRACT = (((1,), (1,)), ((), ()))
BOTH = ("expert", "hid")
STEP = 48
LIMIT = 48 * 1024 * 1024


def partner(block, axis, bit):
    count = lax.axis_size(axis)
    route = []
    for low in range(count):
        high = low | 1 << bit
        if high != low and high < count:
            route += [(low, high), (high, low)]
    return lax.ppermute(block, axis, route)


def swap(block, axes):
    return lax.all_to_all(block, axes, split_axis=0, concat_axis=0, tiled=True)


def shift(block, along, across):
    count = lax.axis_size("hid")
    route = []
    for source in range(count):
        x, y = source // 2, source % 2
        route.append((source, (x + along) % (count // 2) * 2 + (y ^ across)))
    return lax.ppermute(block, "hid", route)


def gather_groups(block):
    other = shift(block, 0, 1)
    right, left = shift(block, 1, 0), shift(block, -1, 0)
    right_other, left_other = shift(other, 1, 0), shift(other, -1, 0)
    far, far_other = shift(right, 1, 0), shift(left_other, -1, 0)
    return jnp.stack([block, other, right, right_other, left, left_other, far, far_other])


def arrival_order():
    own = lax.axis_index("hid")
    half = lax.axis_size("hid") // 2
    x, y = own // 2, own % 2
    places = []
    for along in (0, -1, 1, 2):
        row = (x + along + half) % half * 2
        places += [row + y, row + 1 - y]
    return jnp.stack(places).astype(jnp.int32)


def placing(routes, experts, capacity):
    tokens = routes.shape[0]
    labels = jnp.arange(experts, dtype=jnp.int32)
    onehot = (routes.reshape(-1)[:, None] == labels[None, :]).astype(jnp.bfloat16)
    order = jnp.arange(2 * tokens, dtype=jnp.int32)
    earlier = (order[None, :] < order[:, None]).astype(jnp.bfloat16)
    ranked = jnp.dot(earlier, onehot, preferred_element_type=jnp.float32)
    places = jnp.sum(ranked * onehot.astype(jnp.float32), axis=1).astype(jnp.int32)
    targets = routes * capacity + places.reshape(tokens, 2)
    slots = jnp.arange(experts * capacity, dtype=jnp.int32)
    first = targets[:, 0:1] == slots[None, :]
    second = targets[:, 1:2] == slots[None, :]
    hits = (routes[:, 0:1] == labels[None, :]).astype(jnp.float32) - (
        routes[:, 1:2] == labels[None, :]
    ).astype(jnp.float32)
    slot_map = (
        (targets[:, 0][None, :] == slots[:, None]) | (targets[:, 1][None, :] == slots[:, None])
    ).astype(jnp.bfloat16)
    return (first.astype(jnp.float32), second.astype(jnp.float32), hits, slot_map)


def fill(slot_map, rows):
    return jnp.dot(slot_map, rows, preferred_element_type=jnp.float32).astype(jnp.bfloat16)


def lanes(value):
    total = value[:, 0:128]
    for start in range(128, value.shape[1], 128):
        total = total + value[:, start : start + 128]
    return total


def project_kernel(
    forward, blocked, order, rows_ref, gain_ref, column_ref, gate_w, up_w, *rest
):
    if forward:
        hidden_ref, info_ref, gate_ref, up_ref, normed, scales, sums = rest
    else:
        gate_ref, up_ref, info_ref, normed, scales, sums = rest
    step, steps = pl.program_id(0), pl.num_programs(0)
    blocks = rows_ref.shape[0] if blocked else rows_ref.shape[1] // STEP
    part = gain_ref.shape[2]

    def piece(group, block):
        if blocked:
            return rows_ref[block, group].astype(jnp.float32)
        return rows_ref[group, pl.ds(block * STEP, STEP), :].astype(jnp.float32)

    @pl.when(step == 0)
    def _():
        @pl.loop(0, blocks)
        def _(block):
            total = jnp.zeros((STEP, 128), jnp.float32)
            for group in range(8):
                values = piece(group, block)
                total = total + lanes(values * values)
            squares = jnp.sum(total, axis=1, keepdims=True)
            at = pl.ds(pl.multiple_of(block * STEP, STEP), STEP)
            scales[at, :] = jnp.broadcast_to(
                lax.rsqrt(squares / (8.0 * part) + EPSILON), (STEP, 128)
            )
            info_ref[at, :] = jnp.broadcast_to(squares, (STEP, 128))
            sums[at, :] = jnp.zeros((STEP, 128), jnp.float32)

    gains, column = gain_ref[0], column_ref[0]

    @pl.loop(0, blocks)
    def _(block):
        at = pl.ds(pl.multiple_of(block * STEP, STEP), STEP)
        scaled = piece(step, block) * scales[at, 0:1] * gains
        normed[at, :] = scaled.astype(jnp.bfloat16)
        sums[at, :] += lanes(scaled * column)

    gate = jnp.dot(normed[...], gate_w[...], preferred_element_type=jnp.float32)
    up = jnp.dot(normed[...], up_w[...], preferred_element_type=jnp.float32)

    @pl.when(step == 0)
    def _():
        gate_ref[...] = gate
        up_ref[...] = up

    @pl.when(step > 0)
    def _():
        gate_ref[...] += gate
        up_ref[...] += up

    @pl.when(step == steps - 1)
    def _():
        @pl.loop(0, blocks)
        def _(block):
            at = pl.ds(pl.multiple_of(block * STEP, STEP), STEP)
            logits = jnp.sum(sums[at, :], axis=1, keepdims=True)
            place = lax.broadcasted_iota(jnp.int32, (STEP, 128), 1)
            info_ref[at, :] = jnp.where(place == 0, logits, info_ref[at, :])
            if forward:
                value = gate_ref[at, :]
                hidden_ref[at, :] = (value * jax.nn.sigmoid(value) * up_ref[at, :]).astype(
                    jnp.bfloat16
                )


def project(forward, order, rows, gains, column, gate_w, up_w):
    blocked = rows.ndim == 4
    groups = rows.shape[1] if blocked else rows.shape[0]
    total = rows.shape[0] * rows.shape[2] if blocked else rows.shape[1]
    part, units = rows.shape[-1], gate_w.shape[1]
    whole = tuple(0 for _ in rows.shape)
    scratch = [
        pltpu.VMEM((total, part), jnp.bfloat16),
        pltpu.VMEM((total, 128), jnp.float32),
        pltpu.VMEM((total, 128), jnp.float32),
    ]
    wide = jax.ShapeDtypeStruct((total, units), jnp.float32)
    info = jax.ShapeDtypeStruct((total, 128), jnp.float32)
    wide_spec = pl.BlockSpec((total, units), lambda i, order: (0, 0))
    info_spec = pl.BlockSpec((total, 128), lambda i, order: (0, 0))
    if forward:
        shapes = (jax.ShapeDtypeStruct((total, units), jnp.bfloat16), info)
        specs = (wide_spec, info_spec)
        scratch = [pltpu.VMEM((total, units), jnp.float32)] * 2 + scratch
    else:
        shapes = (wide, wide, info)
        specs = (wide_spec, wide_spec, info_spec)
    pick_w = pl.BlockSpec((part, units), lambda i, order: (order[i], 0))
    pick_row = pl.BlockSpec((1, 1, part), lambda i, order: (order[i], 0, 0))
    return pl.pallas_call(
        functools.partial(project_kernel, forward, blocked),
        out_shape=shapes,
        grid_spec=pltpu.PrefetchScalarGridSpec(
            num_scalar_prefetch=1,
            grid=(groups,),
            in_specs=[
                pl.BlockSpec(rows.shape, lambda i, order: whole),
                pick_row,
                pick_row,
                pick_w,
                pick_w,
            ],
            out_specs=specs,
            scratch_shapes=scratch,
        ),
        compiler_params=pltpu.CompilerParams(
            dimension_semantics=("arbitrary",), vmem_limit_bytes=LIMIT
        ),
        cost_estimate=pl.CostEstimate(
            flops=4 * total * groups * part * units,
            bytes_accessed=4 * groups * part * units + 2 * total * groups * part,
            transcendentals=total * units,
        ),
    )(order, rows, gains, column, gate_w, up_w)


def down_kernel(hidden_ref, down_w, out_ref):
    blocks, _, capacity, part = out_ref.shape
    out = jnp.dot(hidden_ref[...], down_w[...], preferred_element_type=jnp.float32)
    out_ref[...] = out.astype(jnp.bfloat16).reshape(blocks, 1, capacity, part)


def down(hidden, down_w, blocks, groups):
    total, units = hidden.shape
    width = down_w.shape[1]
    part, capacity = width // groups, total // blocks
    return pl.pallas_call(
        down_kernel,
        out_shape=jax.ShapeDtypeStruct((blocks, groups, capacity, part), jnp.bfloat16),
        grid=(groups,),
        in_specs=[
            pl.BlockSpec((total, units), lambda i: (0, 0)),
            pl.BlockSpec((units, part), lambda i: (0, i)),
        ],
        out_specs=pl.BlockSpec((blocks, 1, capacity, part), lambda i: (0, i, 0, 0)),
        compiler_params=pltpu.CompilerParams(
            dimension_semantics=("arbitrary",), vmem_limit_bytes=LIMIT
        ),
        cost_estimate=pl.CostEstimate(
            flops=2 * total * units * width,
            bytes_accessed=2 * units * width + 2 * total * width,
            transcendentals=0,
        ),
    )(hidden, down_w)


def through_kernel(order, rows_ref, gate_ref, up_ref, down_w, gg_ref, gu_ref, info_ref, total):
    step, steps = pl.program_id(0), pl.num_programs(0)
    grad = lax.dot_general(
        rows_ref[0], down_w[...], CONTRACT, preferred_element_type=jnp.float32
    )

    @pl.when(step == 0)
    def _():
        total[...] = grad

    @pl.when(step > 0)
    def _():
        total[...] += grad

    @pl.when(step == steps - 1)
    def _():
        @pl.loop(0, total.shape[0] // STEP)
        def _(block):
            at = pl.ds(pl.multiple_of(block * STEP, STEP), STEP)
            grad_hidden, gate, up = total[at, :], gate_ref[at, :], up_ref[at, :]
            sig = jax.nn.sigmoid(gate)
            silu = gate * sig
            hidden = (silu * up).astype(jnp.bfloat16).astype(jnp.float32)
            grad_gate = (grad_hidden * up * (sig * (1.0 + gate * (1.0 - sig)))).astype(jnp.bfloat16)
            grad_up = (grad_hidden * silu).astype(jnp.bfloat16)
            gg_ref[at, :] = grad_gate
            gu_ref[at, :] = grad_up
            row_dot = jnp.sum(lanes(grad_hidden * hidden), axis=1, keepdims=True)
            norm_dot = jnp.sum(
                lanes(grad_gate.astype(jnp.float32) * gate + grad_up.astype(jnp.float32) * up),
                axis=1,
                keepdims=True,
            )
            place = lax.broadcasted_iota(jnp.int32, (STEP, 128), 1)
            info_ref[at, :] = jnp.where(place == 0, row_dot, norm_dot)


def through(order, rows, gate, up, down_w):
    groups, total, part = rows.shape
    units = gate.shape[1]
    wide = jax.ShapeDtypeStruct((total, units), jnp.bfloat16)
    whole = pl.BlockSpec((total, units), lambda i, order: (0, 0))
    return pl.pallas_call(
        through_kernel,
        out_shape=(wide, wide, jax.ShapeDtypeStruct((total, 128), jnp.float32)),
        grid_spec=pltpu.PrefetchScalarGridSpec(
            num_scalar_prefetch=1,
            grid=(groups,),
            in_specs=[
                pl.BlockSpec((1, total, part), lambda i, order: (i, 0, 0)),
                whole,
                whole,
                pl.BlockSpec((units, part), lambda i, order: (0, order[i])),
            ],
            out_specs=(whole, whole, pl.BlockSpec((total, 128), lambda i, order: (0, 0))),
            scratch_shapes=[pltpu.VMEM((total, units), jnp.float32)],
        ),
        compiler_params=pltpu.CompilerParams(
            dimension_semantics=("arbitrary",), vmem_limit_bytes=LIMIT
        ),
        cost_estimate=pl.CostEstimate(
            flops=2 * total * groups * part * units,
            bytes_accessed=2 * groups * part * (units + total),
            transcendentals=total * units,
        ),
    )(order, rows, gate, up, down_w)


def back_kernel(gg_ref, gu_ref, gate_w, up_w, out_ref):
    blocks, _, capacity, part = out_ref.shape
    out = lax.dot_general(gg_ref[...], gate_w[...], CONTRACT, preferred_element_type=jnp.float32)
    out = out + lax.dot_general(gu_ref[...], up_w[...], CONTRACT, preferred_element_type=jnp.float32)
    out_ref[...] = out.astype(jnp.bfloat16).reshape(blocks, 1, capacity, part)


def back(grad_gate, grad_up, gate_w, up_w, blocks, groups):
    total, units = grad_gate.shape
    width = gate_w.shape[0]
    part, capacity = width // groups, total // blocks
    whole = pl.BlockSpec((total, units), lambda i: (0, 0))
    pick_w = pl.BlockSpec((part, units), lambda i: (i, 0))
    return pl.pallas_call(
        back_kernel,
        out_shape=jax.ShapeDtypeStruct((blocks, groups, capacity, part), jnp.bfloat16),
        grid=(groups,),
        in_specs=[whole, whole, pick_w, pick_w],
        out_specs=pl.BlockSpec((blocks, 1, capacity, part), lambda i: (0, i, 0, 0)),
        compiler_params=pltpu.CompilerParams(
            dimension_semantics=("arbitrary",), vmem_limit_bytes=LIMIT
        ),
        cost_estimate=pl.CostEstimate(
            flops=4 * total * units * width,
            bytes_accessed=4 * units * width + 2 * total * width,
            transcendentals=0,
        ),
    )(grad_gate, grad_up, gate_w, up_w)


def send_back(pieces):
    experts, hids, capacity, part = pieces.shape
    home = swap(pieces.reshape(experts * hids, capacity, part), BOTH)
    home = home.reshape(experts, hids, capacity, part).astype(jnp.float32)
    return jnp.sum(home, axis=1).reshape(experts * capacity, part)


def pick(selection, table):
    return jnp.dot(selection, table, precision=HIGHEST)


def per_device(
    saved_input,
    cotangent,
    next_input,
    routes_saved,
    routes_next,
    norm_gain,
    router,
    expert_gate,
    expert_up,
    expert_down,
):
    gain = norm_gain[0]
    table = router[0]
    gate_w = expert_gate[0, 0]
    up_w = expert_up[0, 0]
    down_w = expert_down[0, 0]
    width = gate_w.shape[0]
    tokens = saved_input.shape[1]
    experts, hids = lax.axis_size("expert"), lax.axis_size("hid")
    capacity = 3 * tokens // experts
    own = lax.axis_index("expert")
    order = arrival_order()

    tokens_next = gather_groups(next_input[0])

    first_saved, second_saved, hits_saved, map_saved = placing(routes_saved[0], experts, capacity)
    part = saved_input.shape[2]
    packed = jnp.concatenate(
        [
            fill(map_saved, saved_input[0]).reshape(experts, capacity, part),
            fill(map_saved, cotangent[0]).reshape(experts, capacity, part),
        ],
        axis=1,
    )
    packed = swap(packed, "expert")
    moved_saved = gather_groups(packed[:, :capacity].reshape(experts * capacity, part))
    moved_cot = gather_groups(packed[:, capacity:].reshape(experts * capacity, part))

    first_next, second_next, hits_next, map_next = placing(routes_next[0], experts, capacity)
    moved_next = jnp.einsum(
        "ect,htf->ehcf",
        map_next.reshape(experts, capacity, tokens),
        tokens_next,
        preferred_element_type=jnp.float32,
    ).astype(jnp.bfloat16)
    moved_next = swap(moved_next, "expert")

    column = lax.dynamic_index_in_dim(table, own, 1, keepdims=False)
    params = jnp.broadcast_to(jnp.stack([gain, column])[None], (hids, 2, gain.shape[0]))
    params = swap(params, "hid")
    gains, column = params[:, 0:1], params[:, 1:2]

    hidden_next, info_next = project(True, order, moved_next, gains, column, gate_w, up_w)
    out_home = send_back(down(hidden_next, down_w, experts, hids))

    gate_saved, up_saved, info_saved = project(
        False, order, moved_saved, gains, column, gate_w, up_w
    )
    grad_gate, grad_up, info_grad = through(order, moved_cot, gate_saved, up_saved, down_w)
    scalars = jnp.concatenate([info_grad[:, :2], info_saved[:, :2], info_next[:, :1]], axis=1)
    count = scalars.shape[1]
    scalars = scalars.reshape(experts, 1, capacity * count)
    scalars = jnp.broadcast_to(scalars, (experts, hids, capacity * count))
    scalars = swap(scalars.reshape(experts * hids, capacity * count), BOTH)
    scalars = scalars.reshape(experts, hids, capacity * count)
    summed = jnp.sum(scalars, axis=1).reshape(experts * capacity, count)
    single = scalars[:, 0].reshape(experts * capacity, count)
    scalars = jnp.concatenate([summed[:, :2], single[:, 2:]], axis=1)

    back_home = send_back(back(grad_gate, grad_up, gate_w, up_w, experts, hids))

    one, two = pick(first_next, scalars[:, 4:5]), pick(second_next, scalars[:, 4:5])
    weights = jax.nn.sigmoid(one - two) * first_next + jax.nn.sigmoid(two - one) * second_next
    values_next = next_input[0].astype(jnp.float32)
    forward_out = (values_next + pick(weights, out_home)).astype(jnp.bfloat16)

    one, two = pick(first_saved, scalars), pick(second_saved, scalars)
    prob_one = jax.nn.sigmoid(one[:, 2] - two[:, 2])
    prob_two = jax.nn.sigmoid(two[:, 2] - one[:, 2])
    scale = lax.rsqrt(one[:, 3] / width + EPSILON)
    grad_logit = (one[:, 0] - two[:, 0]) * prob_one * prob_two
    weights = prob_one[:, None] * first_saved + prob_two[:, None] * second_saved
    grad_normed = pick(weights, back_home) + jnp.dot(
        grad_logit[:, None] * hits_saved, table.T, precision=HIGHEST
    )
    inner = prob_one * one[:, 1] + prob_two * two[:, 1] + grad_logit * (one[:, 2] - two[:, 2])
    values_saved = saved_input[0].astype(jnp.float32)
    grad_input = (
        cotangent[0].astype(jnp.float32)
        + scale[:, None] * (grad_normed * gain[None, :])
        - values_saved * (scale * scale * (inner / width))[:, None]
    ).astype(jnp.bfloat16)

    first_section = lax.axis_index("section") == 0
    outgoing = jnp.where(first_section, forward_out, grad_input)
    leaving = jnp.where(first_section, grad_input, forward_out)
    arriving = partner(outgoing, "section", 0)
    return (leaving[None], arriving[None])


def solution(mesh):
    placed = (
        P("section", "expert", "hid"),
        P("section", "expert", "hid"),
        P("section", "expert", "hid"),
        P("section", "expert", None),
        P("section", "expert", None),
        P("section", "hid"),
        P("section", "hid", None),
        P("section", "expert", None, "hid"),
        P("section", "expert", None, "hid"),
        P("section", "expert", "hid", None),
    )
    return jax.shard_map(
        per_device,
        mesh=mesh,
        in_specs=placed,
        out_specs=(P("section", "expert", "hid"), P("section", "expert", "hid")),
        check_vma=False,
    )
```

```python
import functools

import jax
import jax.numpy as jnp
from jax import lax
from jax.experimental import pallas as pl
from jax.experimental.pallas import tpu as pltpu
from jax.sharding import PartitionSpec as P

EPSILON = 1e-05
INNER = (((1,), (0,)), ((), ()))
CONTRACT = (((1,), (1,)), ((), ()))
LEADING = (((0,), (0,)), ((), ()))
BOTH = ("expert", "hid")
STEP = 48
GROUPS = 8
TABLE = 32
LIMIT = 56 * 1024 * 1024
VMEM = pl.BlockSpec(memory_space=pltpu.VMEM)
SMEM = pl.BlockSpec(memory_space=pltpu.SMEM)
PLACE = pl.BlockSpec(memory_space=pl.ANY)


def product(left, right, dims):
    return lax.dot_general(left, right, dims, preferred_element_type=jnp.float32)


def partner(block, axis, bit):
    count = lax.axis_size(axis)
    route = []
    for low in range(count):
        high = low | 1 << bit
        if high != low and high < count:
            route += [(low, high), (high, low)]
    return lax.ppermute(block, axis, route)


def swap(block, axes):
    return lax.all_to_all(block, axes, split_axis=0, concat_axis=0, tiled=True)


def shift(block, along, across):
    count = lax.axis_size("hid")
    route = []
    for source in range(count):
        x, y = source // 2, source % 2
        route.append((source, (x + along) % (count // 2) * 2 + (y ^ across)))
    return lax.ppermute(block, "hid", route)


def gather_groups(block):
    other = shift(block, 0, 1)
    right, left = shift(block, 1, 0), shift(block, -1, 0)
    right_other, left_other = shift(other, 1, 0), shift(other, -1, 0)
    far, far_other = shift(right, 1, 0), shift(left_other, -1, 0)
    return [block, other, right, right_other, left, left_other, far, far_other]


def arrival_order():
    own = lax.axis_index("hid")
    half = lax.axis_size("hid") // 2
    x, y = own // 2, own % 2
    places = []
    for along in (0, -1, 1, 2):
        row = (x + along + half) % half * 2
        places += [row + y, row + 1 - y]
    return jnp.stack(places).astype(jnp.int32)


def three_parts(value):
    high = value.astype(jnp.bfloat16)
    rest = value - high.astype(jnp.float32)
    middle = rest.astype(jnp.bfloat16)
    low = (rest - middle.astype(jnp.float32)).astype(jnp.bfloat16)
    return high, middle, low


def pack_kernel(
    capacity, routes_s, routes_n, saved, cot, upcoming, gain, router, packed, tokens_out, sel_s, sel_n
):
    tokens, part = saved.shape
    experts = router.shape[0]
    tokens_out[0:tokens, :] = upcoming[...]
    gains = gain[...]
    scaled = router[...] * gains
    rows = [p.astype(jnp.float32) for p in three_parts(scaled)]
    rows += [p.astype(jnp.float32) for p in three_parts(gains)]
    rows.append(jnp.zeros((TABLE - 3 * experts - 3, part), jnp.float32))
    tokens_out[tokens : tokens + TABLE, :] = jnp.concatenate(rows, axis=0).astype(jnp.bfloat16)

    row = lax.broadcasted_iota(jnp.int32, (tokens, tokens), 0)
    lane = lax.broadcasted_iota(jnp.int32, (tokens, tokens), 1)
    earlier = jnp.where(lane < row, 1.0, 0.0).astype(jnp.bfloat16)
    wide = lax.broadcasted_iota(jnp.int32, (tokens, 128), 1)
    slots = lax.broadcasted_iota(jnp.int32, (tokens, experts * capacity), 1)

    def select(routes):
        ids = routes[...]
        one, two = ids[:, 0:1], ids[:, 1:2]
        hit_one = jnp.where(wide == one, 1.0, 0.0)
        hit_two = jnp.where(wide == two, 1.0, 0.0)
        counts = product(earlier, (hit_one + hit_two).astype(jnp.bfloat16), INNER)
        rank_one = jnp.sum(counts * hit_one, axis=1, keepdims=True).astype(jnp.int32)
        rank_two = jnp.sum(counts * hit_two, axis=1, keepdims=True).astype(jnp.int32)
        first = jnp.where(slots == one * capacity + rank_one, 1.0, 0.0)
        second = jnp.where(slots == two * capacity + rank_two, 1.0, 0.0)
        inside = wide < 3 * experts
        wide_one = jnp.where(inside & (lax.rem(wide, experts) == one), 1.0, 0.0).astype(jnp.bfloat16)
        wide_two = jnp.where(inside & (lax.rem(wide, experts) == two), 1.0, 0.0).astype(jnp.bfloat16)
        other = product(first.astype(jnp.bfloat16), wide_two, LEADING)
        other = other + product(second.astype(jnp.bfloat16), wide_one, LEADING)
        return (first + second).astype(jnp.bfloat16), other.astype(jnp.bfloat16)

    def put(start, lanes, width, value):
        packed[:, start : start + capacity, lanes : lanes + width] = value.reshape(
            experts, capacity, width
        )

    both, other = select(routes_s)
    sel_s[...] = both
    put(0, 0, part, product(both, saved[...], LEADING).astype(jnp.bfloat16))
    put(capacity, 0, part, product(both, cot[...], LEADING).astype(jnp.bfloat16))
    put(0, part, 128, other)
    both, other = select(routes_n)
    sel_n[...] = both
    put(capacity, part, 128, other)


def pack(routes_s, routes_n, saved, cot, upcoming, gain, router, capacity):
    tokens, part = saved.shape
    experts = router.shape[0]
    total = experts * capacity
    shapes = [
        (experts, 2 * capacity, part + 128),
        (tokens + TABLE, part),
        (tokens, total),
        (tokens, total),
    ]
    return pl.pallas_call(
        functools.partial(pack_kernel, capacity),
        out_shape=[jax.ShapeDtypeStruct(s, jnp.bfloat16) for s in shapes],
        in_specs=[VMEM] * 7,
        out_specs=[VMEM] * 4,
        compiler_params=pltpu.CompilerParams(vmem_limit_bytes=LIMIT // 2),
    )(routes_s, routes_n, saved, cot, upcoming, gain, router)


def spread_kernel(sel, *refs):
    pieces, (moved, table) = refs[:GROUPS], refs[GROUPS:]
    tokens = sel.shape[0]
    blocks, _, capacity, part = moved.shape
    for group, piece in enumerate(pieces):
        rows = product(sel[...], piece[0:tokens, :], LEADING).astype(jnp.bfloat16)
        moved[:, group] = rows.reshape(blocks, capacity, part)
        table[group] = piece[tokens : tokens + TABLE, :]


def spread(sel, pieces, blocks):
    part = pieces[0].shape[1]
    capacity = sel.shape[1] // blocks
    return pl.pallas_call(
        spread_kernel,
        out_shape=(
            jax.ShapeDtypeStruct((blocks, GROUPS, capacity, part), jnp.bfloat16),
            jax.ShapeDtypeStruct((GROUPS, TABLE, part), jnp.bfloat16),
        ),
        in_specs=[VMEM] * (1 + GROUPS),
        out_specs=(VMEM, VMEM),
        compiler_params=pltpu.CompilerParams(vmem_limit_bytes=LIMIT // 2),
    )(sel, *pieces)


def widen(value, width):
    return jnp.concatenate([value] * (width // 128), axis=1)


def lanes(value):
    total = value[:, 0:128]
    for start in range(128, value.shape[1], 128):
        total = total + value[:, start : start + 128]
    return total


def even(value):
    return jnp.broadcast_to(jnp.sum(value, axis=1, keepdims=True), (value.shape[0], 128))


def gains_of(table, group):
    rows = table[group, 24:32, :].astype(jnp.float32)
    return rows[0:1] + (rows[1:2] + rows[2:3])


def fetch_rows(order, source, target, sems, part):
    copies = []
    for group in range(GROUPS):
        start = pl.multiple_of(order[group] * part, part)
        copies.append(
            pltpu.make_async_copy(
                source.at[pl.ds(start, part), :],
                target.at[pl.ds(group * part, part), :],
                sems.at[group],
            )
        )
    return copies


def fetch_columns(order, source, target, sems, part):
    copies = []
    for group in range(GROUPS):
        start = group * part
        if order is not None:
            start = pl.multiple_of(order[group] * part, part)
        copies.append(
            pltpu.make_async_copy(
                source.at[:, pl.ds(start, part)],
                target.at[:, pl.ds(group * part, part)],
                sems.at[group],
            )
        )
    return copies


def prepare(own, other_start, take, other, table, normed, scales, diffs, logits, width):
    blocks = other.shape[0]
    part = width // GROUPS
    for group in range(GROUPS):
        rows = jnp.concatenate([take(group, block) for block in range(blocks)], axis=0)
        found = product(rows, table[group], CONTRACT)
        if group == 0:
            logits[...] = found
        else:
            logits[...] += found

    @pl.loop(0, blocks)
    def _(block):
        at = pl.ds(pl.multiple_of(block * STEP, STEP), STEP)
        total = jnp.zeros((STEP, 128), jnp.float32)
        for group in range(GROUPS):
            values = take(group, block).astype(jnp.float32)
            total = total + lanes(values * values)
        scale = lax.rsqrt(even(total) / width + EPSILON)
        scales[at, :] = scale
        place = lax.broadcasted_iota(jnp.int32, (STEP, TABLE), 1)
        ours = jnp.where((place < 24) & (lax.rem(place, 8) == own), 1.0, 0.0)
        theirs = other[block, other_start : other_start + STEP, 0:TABLE].astype(jnp.float32)
        diffs[at, :] = even(logits[at, :] * (ours - theirs)) * scale
        for group in range(GROUPS):
            values = take(group, block).astype(jnp.float32)
            normed[at, group * part : (group + 1) * part] = (
                values * widen(scale, part) * gains_of(table, group)
            ).astype(jnp.bfloat16)


def forward_kernel(
    order, own, moved, other, table, gate_w, up_w, down_w, out,
    gate_b, up_b, down_b, normed, gate, up, hidden, scales, diffs, logits, sem_g, sem_u, sem_d
):
    blocks, _, capacity, part = moved.shape
    copies = fetch_rows(order, gate_w, gate_b, sem_g, part)
    copies_up = fetch_rows(order, up_w, up_b, sem_u, part)
    copies_down = fetch_columns(None, down_w, down_b, sem_d, part)
    for copy in copies + copies_up + copies_down:
        copy.start()

    def take(group, block):
        return moved[block, group]

    prepare(own[0], capacity, take, other, table, normed, scales, diffs, logits, GROUPS * part)
    for copy in copies:
        copy.wait()
    gate[...] = product(normed[...], gate_b[...], INNER)
    for copy in copies_up:
        copy.wait()
    up[...] = product(normed[...], up_b[...], INNER)

    @pl.loop(0, blocks)
    def _(block):
        at = pl.ds(pl.multiple_of(block * STEP, STEP), STEP)
        value = gate[at, :]
        hidden[at, :] = (value * jax.nn.sigmoid(value) * up[at, :]).astype(jnp.bfloat16)

    share = widen(jax.nn.sigmoid(diffs[...]), part)
    for group in range(GROUPS):
        copies_down[group].wait()
        rows = product(hidden[...], down_b[:, group * part : (group + 1) * part], INNER)
        out[:, group] = (rows * share).astype(jnp.bfloat16).reshape(blocks, capacity, part)


def weight_scratch(width, units):
    return [
        pltpu.VMEM((width, units), jnp.bfloat16),
        pltpu.VMEM((width, units), jnp.bfloat16),
        pltpu.VMEM((units, width), jnp.bfloat16),
    ]


def forward(order, own, moved, other, table, gate_w, up_w, down_w):
    blocks, _, capacity, part = moved.shape
    width, units = gate_w.shape
    total = blocks * capacity
    return pl.pallas_call(
        forward_kernel,
        out_shape=jax.ShapeDtypeStruct(moved.shape, jnp.bfloat16),
        in_specs=[SMEM, SMEM, VMEM, VMEM, VMEM, PLACE, PLACE, PLACE],
        out_specs=VMEM,
        scratch_shapes=weight_scratch(width, units)
        + [
            pltpu.VMEM((total, width), jnp.bfloat16),
            pltpu.VMEM((total, units), jnp.float32),
            pltpu.VMEM((total, units), jnp.float32),
            pltpu.VMEM((total, units), jnp.bfloat16),
            pltpu.VMEM((total, 128), jnp.float32),
            pltpu.VMEM((total, 128), jnp.float32),
            pltpu.VMEM((total, TABLE), jnp.float32),
        ]
        + [pltpu.SemaphoreType.DMA((GROUPS,))] * 3,
        compiler_params=pltpu.CompilerParams(vmem_limit_bytes=LIMIT),
        cost_estimate=pl.CostEstimate(
            flops=6 * total * width * units,
            bytes_accessed=6 * width * units + 4 * total * width,
            transcendentals=total * units,
        ),
    )(order, own, moved, other, table, gate_w, up_w, down_w)


def backward_kernel(*refs):
    order, own, other, table, gate_w, up_w, down_w = refs[:7]
    pieces = refs[7 : 7 + GROUPS]
    (
        out, gate_b, up_b, down_b, normed, cots, gate, up, grad, grad_gate, grad_up,
        scales, diffs, ones, twos, logits, sem_g, sem_u, sem_d,
    ) = refs[7 + GROUPS :]
    blocks, _, capacity, part = out.shape
    width = GROUPS * part
    copies = fetch_rows(order, gate_w, gate_b, sem_g, part)
    copies_up = fetch_rows(order, up_w, up_b, sem_u, part)
    copies_down = fetch_columns(order, down_w, down_b, sem_d, part)
    for copy in copies + copies_up + copies_down:
        copy.start()

    def take(group, block):
        return pieces[group][block, 0:STEP, :]

    prepare(own[0], 0, take, other, table, normed, scales, diffs, logits, width)

    @pl.loop(0, blocks)
    def _(block):
        at = pl.ds(pl.multiple_of(block * STEP, STEP), STEP)
        for group in range(GROUPS):
            cots[at, group * part : (group + 1) * part] = pieces[group][block, STEP : 2 * STEP, :]

    for copy in copies:
        copy.wait()
    gate[...] = product(normed[...], gate_b[...], INNER)
    for copy in copies_up:
        copy.wait()
    up[...] = product(normed[...], up_b[...], INNER)
    for copy in copies_down:
        copy.wait()
    grad[...] = product(cots[...], down_b[...], CONTRACT)

    @pl.loop(0, blocks)
    def _(block):
        at = pl.ds(pl.multiple_of(block * STEP, STEP), STEP)
        slope, value, lift = grad[at, :], gate[at, :], up[at, :]
        sig = jax.nn.sigmoid(value)
        silu = value * sig
        hidden = (silu * lift).astype(jnp.bfloat16).astype(jnp.float32)
        to_gate = (slope * lift * (sig * (1.0 + value * (1.0 - sig)))).astype(jnp.bfloat16)
        to_up = (slope * silu).astype(jnp.bfloat16)
        grad_gate[at, :] = to_gate
        grad_up[at, :] = to_up
        row_dot = even(lanes(slope * hidden))
        norm_dot = even(
            lanes(to_gate.astype(jnp.float32) * value + to_up.astype(jnp.float32) * lift)
        )
        scale, diff = scales[at, :], diffs[at, :]
        ours, theirs = jax.nn.sigmoid(diff), jax.nn.sigmoid(-diff)
        through = ours * theirs * row_dot
        ones[at, :] = scale * through
        twos[at, :] = scale * scale * ((ours * norm_dot + through * diff) / width)
        diffs[at, :] = scale * ours

    place = lax.broadcasted_iota(jnp.int32, (blocks * STEP, TABLE), 1)
    away = jnp.where((place < 24) & (lax.rem(place, 8) == own[0]), 1.0, 0.0)
    away = away - jnp.concatenate(
        [other[block, 0:STEP, 0:TABLE].astype(jnp.float32) for block in range(blocks)], axis=0
    )
    away = away.astype(jnp.bfloat16)
    for group in range(GROUPS):
        at = slice(group * part, (group + 1) * part)
        rows = product(grad_gate[...], gate_b[at, :], CONTRACT)
        rows = rows + product(grad_up[...], up_b[at, :], CONTRACT)
        turn = product(away, table[group], INNER)
        values = jnp.concatenate([take(group, block) for block in range(blocks)], axis=0)
        rows = (
            rows * (widen(diffs[...], part) * gains_of(table, group))
            + turn * widen(ones[...], part)
            - values.astype(jnp.float32) * widen(twos[...], part)
        )
        out[:, pl.ds(order[group], 1)] = rows.astype(jnp.bfloat16).reshape(blocks, 1, capacity, part)


def backward(order, own, other, table, gate_w, up_w, down_w, pieces):
    blocks, double, part = pieces[0].shape
    capacity = double // 2
    width, units = gate_w.shape
    total = blocks * capacity
    small = pltpu.VMEM((total, 128), jnp.float32)
    return pl.pallas_call(
        backward_kernel,
        out_shape=jax.ShapeDtypeStruct((blocks, GROUPS, capacity, part), jnp.bfloat16),
        in_specs=[SMEM, SMEM, VMEM, VMEM, PLACE, PLACE, PLACE] + [VMEM] * GROUPS,
        out_specs=VMEM,
        scratch_shapes=weight_scratch(width, units)
        + [
            pltpu.VMEM((total, width), jnp.bfloat16),
            pltpu.VMEM((total, width), jnp.bfloat16),
            pltpu.VMEM((total, units), jnp.float32),
            pltpu.VMEM((total, units), jnp.float32),
            pltpu.VMEM((total, units), jnp.float32),
            pltpu.VMEM((total, units), jnp.bfloat16),
            pltpu.VMEM((total, units), jnp.bfloat16),
            small,
            small,
            small,
            small,
            pltpu.VMEM((total, TABLE), jnp.float32),
        ]
        + [pltpu.SemaphoreType.DMA((GROUPS,))] * 3,
        compiler_params=pltpu.CompilerParams(vmem_limit_bytes=LIMIT),
        cost_estimate=pl.CostEstimate(
            flops=10 * total * width * units,
            bytes_accessed=6 * width * units + 6 * total * width,
            transcendentals=total * units,
        ),
    )(order, own, other, table, gate_w, up_w, down_w, *pieces)


def finish_kernel(sel, home, base, out):
    blocks, groups, capacity, part = home.shape
    total = base[...].astype(jnp.float32)
    for group in range(groups):
        total = total + product(sel[...], home[:, group].reshape(blocks * capacity, part), INNER)
    out[...] = total.astype(jnp.bfloat16)


def finish(sel, home, base):
    return pl.pallas_call(
        finish_kernel,
        out_shape=jax.ShapeDtypeStruct(base.shape, jnp.bfloat16),
        in_specs=[VMEM] * 3,
        out_specs=VMEM,
        compiler_params=pltpu.CompilerParams(vmem_limit_bytes=LIMIT // 2),
    )(sel, home, base)


def send_home(pieces):
    experts, hids, capacity, part = pieces.shape
    home = swap(pieces.reshape(experts * hids, capacity, part), BOTH)
    return home.reshape(experts, hids, capacity, part)


def per_device(
    saved_input,
    cotangent,
    next_input,
    routes_saved,
    routes_next,
    norm_gain,
    router,
    expert_gate,
    expert_up,
    expert_down,
):
    gate_w, up_w, down_w = expert_gate[0, 0], expert_up[0, 0], expert_down[0, 0]
    tokens, part = saved_input.shape[1:]
    experts = lax.axis_size("expert")
    capacity = 3 * tokens // experts
    own = lax.axis_index("expert").astype(jnp.int32).reshape(1)
    order = arrival_order()

    packed, tokens_next, sel_saved, sel_next = pack(
        routes_saved[0],
        routes_next[0],
        saved_input[0],
        cotangent[0],
        next_input[0],
        norm_gain,
        router[0].T,
        capacity,
    )
    packed = swap(packed, "expert")
    moved_next, table = spread(sel_next, gather_groups(tokens_next), experts)
    moved_next = swap(moved_next, "expert")
    other = packed[:, :, part:]
    pieces = gather_groups(packed[:, :, :part])

    out_next = forward(order, own, moved_next, other, table, gate_w, up_w, down_w)
    out_home = send_home(out_next)
    pieces, out_next = lax.optimization_barrier((pieces, out_next))
    back_part = backward(order, own, other, table, gate_w, up_w, down_w, pieces)
    back_home = send_home(back_part)

    forward_out = finish(sel_next, out_home, next_input[0])
    grad_input = finish(sel_saved, back_home, cotangent[0])

    first_section = lax.axis_index("section") == 0
    outgoing = jnp.where(first_section, forward_out, grad_input)
    leaving = jnp.where(first_section, grad_input, forward_out)
    arriving = partner(outgoing, "section", 0)
    return (leaving[None], arriving[None])


def solution(mesh):
    placed = (
        P("section", "expert", "hid"),
        P("section", "expert", "hid"),
        P("section", "expert", "hid"),
        P("section", "expert", None),
        P("section", "expert", None),
        P("section", "hid"),
        P("section", "hid", None),
        P("section", "expert", None, "hid"),
        P("section", "expert", None, "hid"),
        P("section", "expert", "hid", None),
    )
    return jax.shard_map(
        per_device,
        mesh=mesh,
        in_specs=placed,
        out_specs=(P("section", "expert", "hid"), P("section", "expert", "hid")),
        check_vma=False,
    )
```

```python
import functools

import jax
import jax.numpy as jnp
from jax import lax
from jax.experimental import pallas as pl
from jax.experimental.pallas import tpu as pltpu
from jax.sharding import PartitionSpec as P

EPSILON = 1e-05
INNER = (((1,), (0,)), ((), ()))
CONTRACT = (((1,), (1,)), ((), ()))
LEADING = (((0,), (0,)), ((), ()))
BOTH = ("expert", "hid")
STEP = 48
GROUPS = 8
TABLE = 32
LIMIT = 56 * 1024 * 1024
VMEM = pl.BlockSpec(memory_space=pltpu.VMEM)
SMEM = pl.BlockSpec(memory_space=pltpu.SMEM)
PLACE = pl.BlockSpec(memory_space=pl.ANY)


def product(left, right, dims):
    return lax.dot_general(left, right, dims, preferred_element_type=jnp.float32)


def partner(block, axis, bit):
    count = lax.axis_size(axis)
    route = []
    for low in range(count):
        high = low | 1 << bit
        if high != low and high < count:
            route += [(low, high), (high, low)]
    return lax.ppermute(block, axis, route)


def swap(block, axes):
    return lax.all_to_all(block, axes, split_axis=0, concat_axis=0, tiled=True)


def shift(block, along, across):
    count = lax.axis_size("hid")
    route = []
    for source in range(count):
        x, y = source // 2, source % 2
        route.append((source, (x + along) % (count // 2) * 2 + (y ^ across)))
    return lax.ppermute(block, "hid", route)


def gather_groups(block):
    other = shift(block, 0, 1)
    right, left = shift(block, 1, 0), shift(block, -1, 0)
    other, right, left = lax.optimization_barrier((other, right, left))
    right_other, left_other = shift(other, 1, 0), shift(other, -1, 0)
    far, far_other = shift(right, 1, 0), shift(left_other, -1, 0)
    return [block, other, right, right_other, left, left_other, far, far_other]


def arrival_order():
    own = lax.axis_index("hid")
    half = lax.axis_size("hid") // 2
    x, y = own // 2, own % 2
    places = []
    for along in (0, -1, 1, 2):
        row = (x + along + half) % half * 2
        places += [row + y, row + 1 - y]
    return jnp.stack(places).astype(jnp.int32)


def three_parts(value):
    high = value.astype(jnp.bfloat16)
    rest = value - high.astype(jnp.float32)
    middle = rest.astype(jnp.bfloat16)
    low = (rest - middle.astype(jnp.float32)).astype(jnp.bfloat16)
    return high, middle, low


def pack_kernel(
    capacity, routes_s, routes_n, saved, cot, upcoming, gain, router, packed, tokens_out, sel_s, sel_n
):
    tokens, part = saved.shape
    experts = router.shape[0]
    tokens_out[0:tokens, :] = upcoming[...]
    gains = gain[...]
    scaled = router[...] * gains
    rows = [p.astype(jnp.float32) for p in three_parts(scaled)]
    rows += [p.astype(jnp.float32) for p in three_parts(gains)]
    rows.append(jnp.zeros((TABLE - 3 * experts - 3, part), jnp.float32))
    tokens_out[tokens : tokens + TABLE, :] = jnp.concatenate(rows, axis=0).astype(jnp.bfloat16)

    row = lax.broadcasted_iota(jnp.int32, (tokens, tokens), 0)
    lane = lax.broadcasted_iota(jnp.int32, (tokens, tokens), 1)
    earlier = jnp.where(lane < row, 1.0, 0.0).astype(jnp.bfloat16)
    wide = lax.broadcasted_iota(jnp.int32, (tokens, 128), 1)
    slots = lax.broadcasted_iota(jnp.int32, (tokens, experts * capacity), 1)

    def select(routes):
        ids = routes[...]
        one, two = ids[:, 0:1], ids[:, 1:2]
        hit_one = jnp.where(wide == one, 1.0, 0.0)
        hit_two = jnp.where(wide == two, 1.0, 0.0)
        counts = product(earlier, (hit_one + hit_two).astype(jnp.bfloat16), INNER)
        rank_one = jnp.sum(counts * hit_one, axis=1, keepdims=True).astype(jnp.int32)
        rank_two = jnp.sum(counts * hit_two, axis=1, keepdims=True).astype(jnp.int32)
        first = jnp.where(slots == one * capacity + rank_one, 1.0, 0.0)
        second = jnp.where(slots == two * capacity + rank_two, 1.0, 0.0)
        inside = wide < 3 * experts
        wide_one = jnp.where(inside & (lax.rem(wide, experts) == one), 1.0, 0.0).astype(jnp.bfloat16)
        wide_two = jnp.where(inside & (lax.rem(wide, experts) == two), 1.0, 0.0).astype(jnp.bfloat16)
        other = product(first.astype(jnp.bfloat16), wide_two, LEADING)
        other = other + product(second.astype(jnp.bfloat16), wide_one, LEADING)
        return (first + second).astype(jnp.bfloat16), other.astype(jnp.bfloat16)

    def put(start, lanes, width, value):
        packed[:, start : start + capacity, lanes : lanes + width] = value.reshape(
            experts, capacity, width
        )

    both, other = select(routes_s)
    sel_s[...] = both
    put(0, 0, part, product(both, saved[...], LEADING).astype(jnp.bfloat16))
    put(capacity, 0, part, product(both, cot[...], LEADING).astype(jnp.bfloat16))
    put(0, part, 128, other)
    both, other = select(routes_n)
    sel_n[...] = both
    put(capacity, part, 128, other)


def pack(routes_s, routes_n, saved, cot, upcoming, gain, router, capacity):
    tokens, part = saved.shape
    experts = router.shape[0]
    total = experts * capacity
    shapes = [
        (experts, 2 * capacity, part + 128),
        (tokens + TABLE, part),
        (tokens, total),
        (tokens, total),
    ]
    return pl.pallas_call(
        functools.partial(pack_kernel, capacity),
        out_shape=[jax.ShapeDtypeStruct(s, jnp.bfloat16) for s in shapes],
        in_specs=[VMEM] * 7,
        out_specs=[VMEM] * 4,
        compiler_params=pltpu.CompilerParams(vmem_limit_bytes=LIMIT // 2),
    )(routes_s, routes_n, saved, cot, upcoming, gain, router)


def spread_kernel(sel, *refs):
    pieces, (moved, table) = refs[:GROUPS], refs[GROUPS:]
    tokens = sel.shape[0]
    blocks, _, capacity, part = moved.shape
    for group, piece in enumerate(pieces):
        rows = product(sel[...], piece[0:tokens, :], LEADING).astype(jnp.bfloat16)
        moved[:, group] = rows.reshape(blocks, capacity, part)
        table[group] = piece[tokens : tokens + TABLE, :]


def spread(sel, pieces, blocks):
    part = pieces[0].shape[1]
    capacity = sel.shape[1] // blocks
    return pl.pallas_call(
        spread_kernel,
        out_shape=(
            jax.ShapeDtypeStruct((blocks, GROUPS, capacity, part), jnp.bfloat16),
            jax.ShapeDtypeStruct((GROUPS, TABLE, part), jnp.bfloat16),
        ),
        in_specs=[VMEM] * (1 + GROUPS),
        out_specs=(VMEM, VMEM),
        compiler_params=pltpu.CompilerParams(vmem_limit_bytes=LIMIT // 2),
    )(sel, *pieces)


def widen(value, width):
    return jnp.concatenate([value] * (width // 128), axis=1)


def lanes(value):
    total = value[:, 0:128]
    for start in range(128, value.shape[1], 128):
        total = total + value[:, start : start + 128]
    return total


def even(value):
    return jnp.broadcast_to(jnp.sum(value, axis=1, keepdims=True), (value.shape[0], 128))


def gains_of(table, group):
    rows = table[group, 24:32, :].astype(jnp.float32)
    return rows[0:1] + (rows[1:2] + rows[2:3])


def fetch_rows(order, source, target, sems, part):
    copies = []
    for group in range(GROUPS):
        start = pl.multiple_of(order[group] * part, part)
        copies.append(
            pltpu.make_async_copy(
                source.at[pl.ds(start, part), :],
                target.at[pl.ds(group * part, part), :],
                sems.at[group],
            )
        )
    return copies


def fetch_columns(order, source, target, sems, part):
    copies = []
    for group in range(GROUPS):
        start = group * part
        if order is not None:
            start = pl.multiple_of(order[group] * part, part)
        copies.append(
            pltpu.make_async_copy(
                source.at[:, pl.ds(start, part)],
                target.at[:, pl.ds(group * part, part)],
                sems.at[group],
            )
        )
    return copies


def prepare(own, other_start, take, other, table, normed, scales, diffs, logits, width):
    blocks = other.shape[0]
    part = width // GROUPS
    for group in range(GROUPS):
        rows = jnp.concatenate([take(group, block) for block in range(blocks)], axis=0)
        found = product(rows, table[group], CONTRACT)
        if group == 0:
            logits[...] = found
        else:
            logits[...] += found

    @pl.loop(0, blocks)
    def _(block):
        at = pl.ds(pl.multiple_of(block * STEP, STEP), STEP)
        total = jnp.zeros((STEP, 128), jnp.float32)
        for group in range(GROUPS):
            values = take(group, block).astype(jnp.float32)
            total = total + lanes(values * values)
        scale = lax.rsqrt(even(total) / width + EPSILON)
        scales[at, :] = scale
        place = lax.broadcasted_iota(jnp.int32, (STEP, TABLE), 1)
        ours = jnp.where((place < 24) & (lax.rem(place, 8) == own), 1.0, 0.0)
        theirs = other[block, other_start : other_start + STEP, 0:TABLE].astype(jnp.float32)
        diffs[at, :] = even(logits[at, :] * (ours - theirs)) * scale
        for group in range(GROUPS):
            values = take(group, block).astype(jnp.float32)
            normed[at, group * part : (group + 1) * part] = (
                values * widen(scale, part) * gains_of(table, group)
            ).astype(jnp.bfloat16)


def forward_kernel(
    order, own, moved, other, table, gate_w, up_w, down_w, out,
    gate_b, up_b, down_b, normed, gate, up, hidden, scales, diffs, logits, sem_g, sem_u, sem_d
):
    blocks, _, capacity, part = moved.shape
    copies = fetch_rows(order, gate_w, gate_b, sem_g, part)
    copies_up = fetch_rows(order, up_w, up_b, sem_u, part)
    copies_down = fetch_columns(None, down_w, down_b, sem_d, part)
    for copy in copies + copies_up + copies_down:
        copy.start()

    def take(group, block):
        return moved[block, group]

    prepare(own[0], capacity, take, other, table, normed, scales, diffs, logits, GROUPS * part)
    for copy in copies:
        copy.wait()
    gate[...] = product(normed[...], gate_b[...], INNER)
    for copy in copies_up:
        copy.wait()
    up[...] = product(normed[...], up_b[...], INNER)

    @pl.loop(0, blocks)
    def _(block):
        at = pl.ds(pl.multiple_of(block * STEP, STEP), STEP)
        value = gate[at, :]
        hidden[at, :] = (value * jax.nn.sigmoid(value) * up[at, :]).astype(jnp.bfloat16)

    share = widen(jax.nn.sigmoid(diffs[...]), part)
    for group in range(GROUPS):
        copies_down[group].wait()
        rows = product(hidden[...], down_b[:, group * part : (group + 1) * part], INNER)
        out[:, group] = (rows * share).astype(jnp.bfloat16).reshape(blocks, capacity, part)


def weight_scratch(width, units):
    return [
        pltpu.VMEM((width, units), jnp.bfloat16),
        pltpu.VMEM((width, units), jnp.bfloat16),
        pltpu.VMEM((units, width), jnp.bfloat16),
    ]


def forward(order, own, moved, other, table, gate_w, up_w, down_w):
    blocks, _, capacity, part = moved.shape
    width, units = gate_w.shape
    total = blocks * capacity
    return pl.pallas_call(
        forward_kernel,
        out_shape=jax.ShapeDtypeStruct(moved.shape, jnp.bfloat16),
        in_specs=[SMEM, SMEM, VMEM, VMEM, VMEM, PLACE, PLACE, PLACE],
        out_specs=VMEM,
        scratch_shapes=weight_scratch(width, units)
        + [
            pltpu.VMEM((total, width), jnp.bfloat16),
            pltpu.VMEM((total, units), jnp.float32),
            pltpu.VMEM((total, units), jnp.float32),
            pltpu.VMEM((total, units), jnp.bfloat16),
            pltpu.VMEM((total, 128), jnp.float32),
            pltpu.VMEM((total, 128), jnp.float32),
            pltpu.VMEM((total, TABLE), jnp.float32),
        ]
        + [pltpu.SemaphoreType.DMA((GROUPS,))] * 3,
        compiler_params=pltpu.CompilerParams(vmem_limit_bytes=LIMIT),
        cost_estimate=pl.CostEstimate(
            flops=6 * total * width * units,
            bytes_accessed=6 * width * units + 4 * total * width,
            transcendentals=total * units,
        ),
    )(order, own, moved, other, table, gate_w, up_w, down_w)


def backward_kernel(*refs):
    order, own, other, table, gate_w, up_w, down_w = refs[:7]
    pieces = refs[7 : 7 + GROUPS]
    (
        out, gate_b, up_b, down_b, normed, cots, gate, up, grad, grad_gate, grad_up,
        scales, diffs, ones, twos, logits, sem_g, sem_u, sem_d,
    ) = refs[7 + GROUPS :]
    blocks, _, capacity, part = out.shape
    width = GROUPS * part
    copies = fetch_rows(order, gate_w, gate_b, sem_g, part)
    copies_up = fetch_rows(order, up_w, up_b, sem_u, part)
    copies_down = fetch_columns(order, down_w, down_b, sem_d, part)
    for copy in copies + copies_up + copies_down:
        copy.start()

    def take(group, block):
        return pieces[group][block, 0:STEP, :]

    prepare(own[0], 0, take, other, table, normed, scales, diffs, logits, width)

    @pl.loop(0, blocks)
    def _(block):
        at = pl.ds(pl.multiple_of(block * STEP, STEP), STEP)
        for group in range(GROUPS):
            cots[at, group * part : (group + 1) * part] = pieces[group][block, STEP : 2 * STEP, :]

    for copy in copies:
        copy.wait()
    gate[...] = product(normed[...], gate_b[...], INNER)
    for copy in copies_up:
        copy.wait()
    up[...] = product(normed[...], up_b[...], INNER)
    for copy in copies_down:
        copy.wait()
    grad[...] = product(cots[...], down_b[...], CONTRACT)

    @pl.loop(0, blocks)
    def _(block):
        at = pl.ds(pl.multiple_of(block * STEP, STEP), STEP)
        slope, value, lift = grad[at, :], gate[at, :], up[at, :]
        sig = jax.nn.sigmoid(value)
        silu = value * sig
        hidden = (silu * lift).astype(jnp.bfloat16).astype(jnp.float32)
        to_gate = (slope * lift * (sig * (1.0 + value * (1.0 - sig)))).astype(jnp.bfloat16)
        to_up = (slope * silu).astype(jnp.bfloat16)
        grad_gate[at, :] = to_gate
        grad_up[at, :] = to_up
        row_dot = even(lanes(slope * hidden))
        norm_dot = even(
            lanes(to_gate.astype(jnp.float32) * value + to_up.astype(jnp.float32) * lift)
        )
        scale, diff = scales[at, :], diffs[at, :]
        ours, theirs = jax.nn.sigmoid(diff), jax.nn.sigmoid(-diff)
        through = ours * theirs * row_dot
        ones[at, :] = scale * through
        twos[at, :] = scale * scale * ((ours * norm_dot + through * diff) / width)
        diffs[at, :] = scale * ours

    place = lax.broadcasted_iota(jnp.int32, (blocks * STEP, TABLE), 1)
    away = jnp.where((place < 24) & (lax.rem(place, 8) == own[0]), 1.0, 0.0)
    away = away - jnp.concatenate(
        [other[block, 0:STEP, 0:TABLE].astype(jnp.float32) for block in range(blocks)], axis=0
    )
    away = away.astype(jnp.bfloat16)
    for group in range(GROUPS):
        at = slice(group * part, (group + 1) * part)
        rows = product(grad_gate[...], gate_b[at, :], CONTRACT)
        rows = rows + product(grad_up[...], up_b[at, :], CONTRACT)
        turn = product(away, table[group], INNER)
        values = jnp.concatenate([take(group, block) for block in range(blocks)], axis=0)
        rows = (
            rows * (widen(diffs[...], part) * gains_of(table, group))
            + turn * widen(ones[...], part)
            - values.astype(jnp.float32) * widen(twos[...], part)
        )
        out[:, pl.ds(order[group], 1)] = rows.astype(jnp.bfloat16).reshape(blocks, 1, capacity, part)


def backward(order, own, other, table, gate_w, up_w, down_w, pieces):
    blocks, double, part = pieces[0].shape
    capacity = double // 2
    width, units = gate_w.shape
    total = blocks * capacity
    small = pltpu.VMEM((total, 128), jnp.float32)
    return pl.pallas_call(
        backward_kernel,
        out_shape=jax.ShapeDtypeStruct((blocks, GROUPS, capacity, part), jnp.bfloat16),
        in_specs=[SMEM, SMEM, VMEM, VMEM, PLACE, PLACE, PLACE] + [VMEM] * GROUPS,
        out_specs=VMEM,
        scratch_shapes=weight_scratch(width, units)
        + [
            pltpu.VMEM((total, width), jnp.bfloat16),
            pltpu.VMEM((total, width), jnp.bfloat16),
            pltpu.VMEM((total, units), jnp.float32),
            pltpu.VMEM((total, units), jnp.float32),
            pltpu.VMEM((total, units), jnp.float32),
            pltpu.VMEM((total, units), jnp.bfloat16),
            pltpu.VMEM((total, units), jnp.bfloat16),
            small,
            small,
            small,
            small,
            pltpu.VMEM((total, TABLE), jnp.float32),
        ]
        + [pltpu.SemaphoreType.DMA((GROUPS,))] * 3,
        compiler_params=pltpu.CompilerParams(vmem_limit_bytes=LIMIT),
        cost_estimate=pl.CostEstimate(
            flops=10 * total * width * units,
            bytes_accessed=6 * width * units + 6 * total * width,
            transcendentals=total * units,
        ),
    )(order, own, other, table, gate_w, up_w, down_w, *pieces)


def finish_kernel(sel, home, base, out):
    blocks, groups, capacity, part = home.shape
    total = base[...].astype(jnp.float32)
    for group in range(groups):
        total = total + product(sel[...], home[:, group].reshape(blocks * capacity, part), INNER)
    out[...] = total.astype(jnp.bfloat16)


def finish(sel, home, base):
    return pl.pallas_call(
        finish_kernel,
        out_shape=jax.ShapeDtypeStruct(base.shape, jnp.bfloat16),
        in_specs=[VMEM] * 3,
        out_specs=VMEM,
        compiler_params=pltpu.CompilerParams(vmem_limit_bytes=LIMIT // 2),
    )(sel, home, base)


def send_home(pieces):
    experts, hids, capacity, part = pieces.shape
    home = swap(pieces.reshape(experts * hids, capacity, part), BOTH)
    return home.reshape(experts, hids, capacity, part)


def per_device(
    saved_input,
    cotangent,
    next_input,
    routes_saved,
    routes_next,
    norm_gain,
    router,
    expert_gate,
    expert_up,
    expert_down,
):
    gate_w, up_w, down_w = expert_gate[0, 0], expert_up[0, 0], expert_down[0, 0]
    tokens, part = saved_input.shape[1:]
    experts = lax.axis_size("expert")
    capacity = 3 * tokens // experts
    own = lax.axis_index("expert").astype(jnp.int32).reshape(1)
    order = arrival_order()

    packed, tokens_next, sel_saved, sel_next = pack(
        routes_saved[0],
        routes_next[0],
        saved_input[0],
        cotangent[0],
        next_input[0],
        norm_gain,
        router[0].T,
        capacity,
    )
    packed = swap(packed, "expert")
    moved_next, table = spread(sel_next, gather_groups(tokens_next), experts)
    moved_next = swap(moved_next, "expert")
    other = packed[:, :, part:]
    pieces = gather_groups(packed[:, :, :part])

    pieces, moved_next = lax.optimization_barrier((pieces, moved_next))
    out_next = forward(order, own, moved_next, other, table, gate_w, up_w, down_w)
    out_home = send_home(out_next)
    pieces, out_next = lax.optimization_barrier((pieces, out_next))
    back_part = backward(order, own, other, table, gate_w, up_w, down_w, pieces)
    back_home = send_home(back_part)

    forward_out = finish(sel_next, out_home, next_input[0])
    grad_input = finish(sel_saved, back_home, cotangent[0])

    first_section = lax.axis_index("section") == 0
    outgoing = jnp.where(first_section, forward_out, grad_input)
    leaving = jnp.where(first_section, grad_input, forward_out)
    arriving = partner(outgoing, "section", 0)
    return (leaving[None], arriving[None])


def solution(mesh):
    placed = (
        P("section", "expert", "hid"),
        P("section", "expert", "hid"),
        P("section", "expert", "hid"),
        P("section", "expert", None),
        P("section", "expert", None),
        P("section", "hid"),
        P("section", "hid", None),
        P("section", "expert", None, "hid"),
        P("section", "expert", None, "hid"),
        P("section", "expert", "hid", None),
    )
    return jax.shard_map(
        per_device,
        mesh=mesh,
        in_specs=placed,
        out_specs=(P("section", "expert", "hid"), P("section", "expert", "hid")),
        check_vma=False,
    )
```

```python
import functools

import jax
import jax.numpy as jnp
from jax import lax
from jax.experimental import pallas as pl
from jax.experimental.pallas import tpu as pltpu
from jax.sharding import PartitionSpec as P

EPSILON = 1e-05
INNER = (((1,), (0,)), ((), ()))
CONTRACT = (((1,), (1,)), ((), ()))
LEADING = (((0,), (0,)), ((), ()))
BOTH = ("expert", "hid")
STEP = 48
GROUPS = 8
TABLE = 32
LIMIT = 56 * 1024 * 1024
VMEM = pl.BlockSpec(memory_space=pltpu.VMEM)
SMEM = pl.BlockSpec(memory_space=pltpu.SMEM)
PLACE = pl.BlockSpec(memory_space=pl.ANY)


def product(left, right, dims):
    return lax.dot_general(left, right, dims, preferred_element_type=jnp.float32)


def partner(block, axis, bit):
    count = lax.axis_size(axis)
    route = []
    for low in range(count):
        high = low | 1 << bit
        if high != low and high < count:
            route += [(low, high), (high, low)]
    return lax.ppermute(block, axis, route)


def swap(block, axes):
    return lax.all_to_all(block, axes, split_axis=0, concat_axis=0, tiled=True)


def shift(block, along, across):
    count = lax.axis_size("hid")
    route = []
    for source in range(count):
        x, y = source // 2, source % 2
        route.append((source, (x + along) % (count // 2) * 2 + (y ^ across)))
    return lax.ppermute(block, "hid", route)


def gather_near(block):
    other = shift(block, 0, 1)
    right, left = shift(block, 1, 0), shift(block, -1, 0)
    other, right, left = lax.optimization_barrier((other, right, left))
    right_other, left_other = shift(other, 1, 0), shift(other, -1, 0)
    return [block, other, right, right_other, left, left_other]


def gather_far(near):
    return [shift(near[2], 1, 0), shift(near[5], -1, 0)]


def gather_groups(block):
    near = gather_near(block)
    return near + gather_far(near)


def arrival_order():
    own = lax.axis_index("hid")
    half = lax.axis_size("hid") // 2
    x, y = own // 2, own % 2
    places = []
    for along in (0, -1, 1, 2):
        row = (x + along + half) % half * 2
        places += [row + y, row + 1 - y]
    return jnp.stack(places).astype(jnp.int32)


def three_parts(value):
    high = value.astype(jnp.bfloat16)
    rest = value - high.astype(jnp.float32)
    middle = rest.astype(jnp.bfloat16)
    low = (rest - middle.astype(jnp.float32)).astype(jnp.bfloat16)
    return high, middle, low


def whole(shape):
    return pl.BlockSpec(shape, lambda i: (0,) * len(shape))


def pack_kernel(
    capacity, routes_s, routes_n, saved, cot, upcoming, gain, router, packed, tokens_out, sel_s, sel_n
):
    tokens, part = saved.shape
    experts = router.shape[0]
    tokens_out[0:tokens, :] = upcoming[...]
    gains = gain[...]
    scaled = router[...] * gains
    rows = [p.astype(jnp.float32) for p in three_parts(scaled)]
    rows += [p.astype(jnp.float32) for p in three_parts(gains)]
    rows.append(jnp.zeros((TABLE - 3 * experts - 3, part), jnp.float32))
    tokens_out[tokens : tokens + TABLE, :] = jnp.concatenate(rows, axis=0).astype(jnp.bfloat16)

    row = lax.broadcasted_iota(jnp.int32, (tokens, tokens), 0)
    lane = lax.broadcasted_iota(jnp.int32, (tokens, tokens), 1)
    earlier = jnp.where(lane < row, 1.0, 0.0).astype(jnp.bfloat16)
    wide = lax.broadcasted_iota(jnp.int32, (tokens, 128), 1)
    slots = lax.broadcasted_iota(jnp.int32, (tokens, experts * capacity), 1)

    def select(routes):
        ids = routes[...]
        one, two = ids[:, 0:1], ids[:, 1:2]
        hit_one = jnp.where(wide == one, 1.0, 0.0)
        hit_two = jnp.where(wide == two, 1.0, 0.0)
        counts = product(earlier, (hit_one + hit_two).astype(jnp.bfloat16), INNER)
        rank_one = jnp.sum(counts * hit_one, axis=1, keepdims=True).astype(jnp.int32)
        rank_two = jnp.sum(counts * hit_two, axis=1, keepdims=True).astype(jnp.int32)
        first = jnp.where(slots == one * capacity + rank_one, 1.0, 0.0)
        second = jnp.where(slots == two * capacity + rank_two, 1.0, 0.0)
        inside = wide < 3 * experts
        wide_one = jnp.where(inside & (lax.rem(wide, experts) == one), 1.0, 0.0).astype(jnp.bfloat16)
        wide_two = jnp.where(inside & (lax.rem(wide, experts) == two), 1.0, 0.0).astype(jnp.bfloat16)
        other = product(first.astype(jnp.bfloat16), wide_two, LEADING)
        other = other + product(second.astype(jnp.bfloat16), wide_one, LEADING)
        return (first + second).astype(jnp.bfloat16), other.astype(jnp.bfloat16)

    def put(start, lanes, width, value):
        packed[:, start : start + capacity, lanes : lanes + width] = value.reshape(
            experts, capacity, width
        )

    both, other = select(routes_s)
    sel_s[...] = both
    put(0, 0, part, product(both, saved[...], LEADING).astype(jnp.bfloat16))
    put(capacity, 0, part, product(both, cot[...], LEADING).astype(jnp.bfloat16))
    put(0, part, 128, other)
    both, other = select(routes_n)
    sel_n[...] = both
    put(capacity, part, 128, other)


def pack(routes_s, routes_n, saved, cot, upcoming, gain, router, capacity):
    tokens, part = saved.shape
    experts = router.shape[0]
    total = experts * capacity
    shapes = [
        (experts, 2 * capacity, part + 128),
        (tokens + TABLE, part),
        (tokens, total),
        (tokens, total),
    ]
    return pl.pallas_call(
        functools.partial(pack_kernel, capacity),
        out_shape=[jax.ShapeDtypeStruct(s, jnp.bfloat16) for s in shapes],
        grid=(1,),
        in_specs=[whole(a.shape) for a in (routes_s, routes_n, saved, cot, upcoming, gain, router)],
        out_specs=[whole(s) for s in shapes],
        compiler_params=pltpu.CompilerParams(vmem_limit_bytes=LIMIT // 2),
    )(routes_s, routes_n, saved, cot, upcoming, gain, router)


def spread_kernel(sel, *refs):
    pieces, (moved, table) = refs[:GROUPS], refs[GROUPS:]
    tokens = sel.shape[0]
    blocks, _, capacity, part = moved.shape
    for group, piece in enumerate(pieces):
        rows = product(sel[...], piece[0:tokens, :], LEADING).astype(jnp.bfloat16)
        moved[:, group] = rows.reshape(blocks, capacity, part)
        table[group] = piece[tokens : tokens + TABLE, :]


def spread(sel, pieces, blocks):
    part = pieces[0].shape[1]
    capacity = sel.shape[1] // blocks
    return pl.pallas_call(
        spread_kernel,
        out_shape=(
            jax.ShapeDtypeStruct((blocks, GROUPS, capacity, part), jnp.bfloat16),
            jax.ShapeDtypeStruct((GROUPS, TABLE, part), jnp.bfloat16),
        ),
        in_specs=[VMEM] * (1 + GROUPS),
        out_specs=(VMEM, VMEM),
        compiler_params=pltpu.CompilerParams(vmem_limit_bytes=LIMIT // 2),
    )(sel, *pieces)


def widen(value, width):
    return jnp.concatenate([value] * (width // 128), axis=1)


def lanes(value):
    total = value[:, 0:128]
    for start in range(128, value.shape[1], 128):
        total = total + value[:, start : start + 128]
    return total


def even(value):
    return jnp.broadcast_to(jnp.sum(value, axis=1, keepdims=True), (value.shape[0], 128))


def gains_of(table, group):
    rows = table[group, 24:32, :].astype(jnp.float32)
    return rows[0:1] + (rows[1:2] + rows[2:3])


def fetch_rows(order, source, target, sems, part):
    copies = []
    for group in range(GROUPS):
        start = pl.multiple_of(order[group] * part, part)
        copies.append(
            pltpu.make_async_copy(
                source.at[pl.ds(start, part), :],
                target.at[pl.ds(group * part, part), :],
                sems.at[group],
            )
        )
    return copies


def fetch_columns(order, source, target, sems, part):
    copies = []
    for group in range(GROUPS):
        start = group * part
        if order is not None:
            start = pl.multiple_of(order[group] * part, part)
        copies.append(
            pltpu.make_async_copy(
                source.at[:, pl.ds(start, part)],
                target.at[:, pl.ds(group * part, part)],
                sems.at[group],
            )
        )
    return copies


def start(copies):
    for copy in copies:
        copy.start()


def wait(copies):
    for copy in copies:
        copy.wait()


def prepare(own, other_start, take, other, table, normed, scales, diffs, logits, width, between):
    blocks = other.shape[0]
    part = width // GROUPS
    for group in range(GROUPS):
        rows = jnp.concatenate([take(group, block) for block in range(blocks)], axis=0)
        found = product(rows, table[group], CONTRACT)
        if group == 0:
            logits[...] = found
        else:
            logits[...] += found
    start(between)

    @pl.loop(0, blocks)
    def _(block):
        at = pl.ds(pl.multiple_of(block * STEP, STEP), STEP)
        total = jnp.zeros((STEP, 128), jnp.float32)
        for group in range(GROUPS):
            values = take(group, block).astype(jnp.float32)
            total = total + lanes(values * values)
        scale = lax.rsqrt(even(total) / width + EPSILON)
        scales[at, :] = scale
        place = lax.broadcasted_iota(jnp.int32, (STEP, TABLE), 1)
        ours = jnp.where((place < 24) & (lax.rem(place, 8) == own), 1.0, 0.0)
        theirs = other[block, other_start : other_start + STEP, 0:TABLE].astype(jnp.float32)
        diffs[at, :] = even(logits[at, :] * (ours - theirs)) * scale
        for group in range(GROUPS):
            values = take(group, block).astype(jnp.float32)
            normed[at, group * part : (group + 1) * part] = (
                values * widen(scale, part) * gains_of(table, group)
            ).astype(jnp.bfloat16)


def fetch_blocks(source, target, sems):
    return [
        pltpu.make_async_copy(source.at[block], target.at[block], sems.at[block])
        for block in range(source.shape[0])
    ]


def hand_out(group, place, source, target, sems):
    return pltpu.make_async_copy(
        source.at[:, group : group + 1], target.at[:, pl.ds(place, 1)], sems.at[group]
    )


def forward_kernel(
    order, own, moved_in, other, table, gate_w, up_w, down_w, out_to,
    moved, out, gate_b, up_b, down_b, normed, gate, up, hidden, scales, diffs, logits,
    sem_m, sem_o, sem_g, sem_u, sem_d
):
    blocks, _, capacity, part = moved.shape
    arrive = fetch_blocks(moved_in, moved, sem_m)
    start(arrive)
    copies = fetch_rows(order, gate_w, gate_b, sem_g, part)
    copies_up = fetch_rows(order, up_w, up_b, sem_u, part)
    copies_down = fetch_columns(None, down_w, down_b, sem_d, part)
    start(copies)
    wait(arrive)

    def take(group, block):
        return moved[block, group]

    prepare(
        own[0], capacity, take, other, table, normed, scales, diffs, logits, GROUPS * part, copies_up
    )
    wait(copies)
    start(copies_down)
    gate[...] = product(normed[...], gate_b[...], INNER)
    wait(copies_up)
    up[...] = product(normed[...], up_b[...], INNER)

    @pl.loop(0, blocks)
    def _(block):
        at = pl.ds(pl.multiple_of(block * STEP, STEP), STEP)
        value = gate[at, :]
        hidden[at, :] = (value * jax.nn.sigmoid(value) * up[at, :]).astype(jnp.bfloat16)

    share = widen(jax.nn.sigmoid(diffs[...]), part)
    for group in range(GROUPS):
        copies_down[group].wait()
        rows = product(hidden[...], down_b[:, group * part : (group + 1) * part], INNER)
        out[:, group] = (rows * share).astype(jnp.bfloat16).reshape(blocks, capacity, part)
        hand_out(group, group, out, out_to, sem_o).start()
    for group in range(GROUPS):
        hand_out(group, group, out, out_to, sem_o).wait()


def weight_scratch(width, units):
    return [
        pltpu.VMEM((width, units), jnp.bfloat16),
        pltpu.VMEM((width, units), jnp.bfloat16),
        pltpu.VMEM((units, width), jnp.bfloat16),
    ]


def forward(order, own, moved, other, table, gate_w, up_w, down_w):
    blocks, _, capacity, part = moved.shape
    width, units = gate_w.shape
    total = blocks * capacity
    return pl.pallas_call(
        forward_kernel,
        out_shape=jax.ShapeDtypeStruct(moved.shape, jnp.bfloat16),
        in_specs=[SMEM, SMEM, PLACE, VMEM, VMEM, PLACE, PLACE, PLACE],
        out_specs=PLACE,
        scratch_shapes=[pltpu.VMEM(moved.shape, jnp.bfloat16)] * 2
        + weight_scratch(width, units)
        + [
            pltpu.VMEM((total, width), jnp.bfloat16),
            pltpu.VMEM((total, units), jnp.float32),
            pltpu.VMEM((total, units), jnp.float32),
            pltpu.VMEM((total, units), jnp.bfloat16),
            pltpu.VMEM((total, 128), jnp.float32),
            pltpu.VMEM((total, 128), jnp.float32),
            pltpu.VMEM((total, TABLE), jnp.float32),
        ]
        + [pltpu.SemaphoreType.DMA((blocks,))]
        + [pltpu.SemaphoreType.DMA((GROUPS,))] * 4,
        compiler_params=pltpu.CompilerParams(vmem_limit_bytes=LIMIT),
        cost_estimate=pl.CostEstimate(
            flops=6 * total * width * units,
            bytes_accessed=6 * width * units + 4 * total * width,
            transcendentals=total * units,
        ),
    )(order, own, moved, other, table, gate_w, up_w, down_w)


def backward_kernel(*refs):
    order, own, other, table, gate_w, up_w, down_w = refs[:7]
    pieces_in = refs[7 : 7 + GROUPS]
    out_to, pieces = refs[7 + GROUPS], refs[8 + GROUPS : 8 + 2 * GROUPS]
    (
        out, gate_b, up_b, down_b, normed, cots, gate, up, grad, grad_gate, grad_up,
        scales, diffs, ones, twos, logits, sem_m, sem_o, sem_g, sem_u, sem_d,
    ) = refs[8 + 2 * GROUPS :]
    blocks, _, capacity, part = out.shape
    width = GROUPS * part
    arrive = [
        pltpu.make_async_copy(pieces_in[group], pieces[group], sem_m.at[group])
        for group in range(GROUPS)
    ]
    start(arrive)
    copies = fetch_rows(order, gate_w, gate_b, sem_g, part)
    copies_up = fetch_rows(order, up_w, up_b, sem_u, part)
    copies_down = fetch_columns(order, down_w, down_b, sem_d, part)
    start(copies)
    wait(arrive)

    def take(group, block):
        return pieces[group][block, 0:STEP, :]

    prepare(own[0], 0, take, other, table, normed, scales, diffs, logits, width, copies_up)

    @pl.loop(0, blocks)
    def _(block):
        at = pl.ds(pl.multiple_of(block * STEP, STEP), STEP)
        for group in range(GROUPS):
            cots[at, group * part : (group + 1) * part] = pieces[group][block, STEP : 2 * STEP, :]

    wait(copies)
    start(copies_down)
    gate[...] = product(normed[...], gate_b[...], INNER)
    wait(copies_up)
    up[...] = product(normed[...], up_b[...], INNER)
    wait(copies_down)
    grad[...] = product(cots[...], down_b[...], CONTRACT)

    @pl.loop(0, blocks)
    def _(block):
        at = pl.ds(pl.multiple_of(block * STEP, STEP), STEP)
        slope, value, lift = grad[at, :], gate[at, :], up[at, :]
        sig = jax.nn.sigmoid(value)
        silu = value * sig
        hidden = (silu * lift).astype(jnp.bfloat16).astype(jnp.float32)
        to_gate = (slope * lift * (sig * (1.0 + value * (1.0 - sig)))).astype(jnp.bfloat16)
        to_up = (slope * silu).astype(jnp.bfloat16)
        grad_gate[at, :] = to_gate
        grad_up[at, :] = to_up
        row_dot = even(lanes(slope * hidden))
        norm_dot = even(
            lanes(to_gate.astype(jnp.float32) * value + to_up.astype(jnp.float32) * lift)
        )
        scale, diff = scales[at, :], diffs[at, :]
        ours, theirs = jax.nn.sigmoid(diff), jax.nn.sigmoid(-diff)
        through = ours * theirs * row_dot
        ones[at, :] = scale * through
        twos[at, :] = scale * scale * ((ours * norm_dot + through * diff) / width)
        diffs[at, :] = scale * ours

    place = lax.broadcasted_iota(jnp.int32, (blocks * STEP, TABLE), 1)
    away = jnp.where((place < 24) & (lax.rem(place, 8) == own[0]), 1.0, 0.0)
    away = away - jnp.concatenate(
        [other[block, 0:STEP, 0:TABLE].astype(jnp.float32) for block in range(blocks)], axis=0
    )
    away = away.astype(jnp.bfloat16)
    for group in range(GROUPS):
        at = slice(group * part, (group + 1) * part)
        rows = product(grad_gate[...], gate_b[at, :], CONTRACT)
        rows = rows + product(grad_up[...], up_b[at, :], CONTRACT)
        turn = product(away, table[group], INNER)
        values = jnp.concatenate([take(group, block) for block in range(blocks)], axis=0)
        rows = (
            rows * (widen(diffs[...], part) * gains_of(table, group))
            + turn * widen(ones[...], part)
            - values.astype(jnp.float32) * widen(twos[...], part)
        )
        out[:, group] = rows.astype(jnp.bfloat16).reshape(blocks, capacity, part)
        hand_out(group, order[group], out, out_to, sem_o).start()
    for group in range(GROUPS):
        hand_out(group, order[group], out, out_to, sem_o).wait()


def backward(order, own, other, table, gate_w, up_w, down_w, pieces):
    blocks, double, part = pieces[0].shape
    capacity = double // 2
    width, units = gate_w.shape
    total = blocks * capacity
    small = pltpu.VMEM((total, 128), jnp.float32)
    return pl.pallas_call(
        backward_kernel,
        out_shape=jax.ShapeDtypeStruct((blocks, GROUPS, capacity, part), jnp.bfloat16),
        in_specs=[SMEM, SMEM, VMEM, VMEM, PLACE, PLACE, PLACE] + [PLACE] * GROUPS,
        out_specs=PLACE,
        scratch_shapes=[pltpu.VMEM((blocks, double, part), jnp.bfloat16)] * GROUPS
        + [pltpu.VMEM((blocks, GROUPS, capacity, part), jnp.bfloat16)]
        + weight_scratch(width, units)
        + [
            pltpu.VMEM((total, width), jnp.bfloat16),
            pltpu.VMEM((total, width), jnp.bfloat16),
            pltpu.VMEM((total, units), jnp.float32),
            pltpu.VMEM((total, units), jnp.float32),
            pltpu.VMEM((total, units), jnp.float32),
            pltpu.VMEM((total, units), jnp.bfloat16),
            pltpu.VMEM((total, units), jnp.bfloat16),
            small,
            small,
            small,
            small,
            pltpu.VMEM((total, TABLE), jnp.float32),
        ]
        + [pltpu.SemaphoreType.DMA((GROUPS,))] * 5,
        compiler_params=pltpu.CompilerParams(vmem_limit_bytes=LIMIT),
        cost_estimate=pl.CostEstimate(
            flops=10 * total * width * units,
            bytes_accessed=6 * width * units + 6 * total * width,
            transcendentals=total * units,
        ),
    )(order, own, other, table, gate_w, up_w, down_w, *pieces)


def finish_kernel(sel, home, base, out):
    blocks, groups, capacity, part = home.shape
    total = base[...].astype(jnp.float32)
    for group in range(groups):
        total = total + product(sel[...], home[:, group].reshape(blocks * capacity, part), INNER)
    out[...] = total.astype(jnp.bfloat16)


def finish(sel, home, base):
    return pl.pallas_call(
        finish_kernel,
        out_shape=jax.ShapeDtypeStruct(base.shape, jnp.bfloat16),
        in_specs=[VMEM] * 3,
        out_specs=VMEM,
        compiler_params=pltpu.CompilerParams(vmem_limit_bytes=LIMIT // 2),
    )(sel, home, base)


def send_home(pieces):
    experts, hids, capacity, part = pieces.shape
    home = swap(pieces.reshape(experts * hids, capacity, part), BOTH)
    return home.reshape(experts, hids, capacity, part)


def per_device(
    saved_input,
    cotangent,
    next_input,
    routes_saved,
    routes_next,
    norm_gain,
    router,
    expert_gate,
    expert_up,
    expert_down,
):
    gate_w, up_w, down_w = expert_gate[0, 0], expert_up[0, 0], expert_down[0, 0]
    tokens, part = saved_input.shape[1:]
    experts = lax.axis_size("expert")
    capacity = 3 * tokens // experts
    own = lax.axis_index("expert").astype(jnp.int32).reshape(1)
    order = arrival_order()

    packed, tokens_next, sel_saved, sel_next = pack(
        routes_saved[0],
        routes_next[0],
        saved_input[0],
        cotangent[0],
        next_input[0],
        norm_gain,
        router[0].T,
        capacity,
    )
    packed = swap(packed, "expert")
    moved_next, table = spread(sel_next, gather_groups(tokens_next), experts)
    moved_next = swap(moved_next, "expert")
    other = packed[:, :, part:]
    near = gather_near(packed[:, :, :part])

    near, moved_next = lax.optimization_barrier((near, moved_next))
    far = gather_far(near)
    out_next = forward(order, own, moved_next, other, table, gate_w, up_w, down_w)
    far, out_next = lax.optimization_barrier((far, out_next))
    pieces = near + far
    out_home = send_home(out_next)
    back_part = backward(order, own, other, table, gate_w, up_w, down_w, pieces)
    back_home = send_home(back_part)

    forward_out = finish(sel_next, out_home, next_input[0])
    grad_input = finish(sel_saved, back_home, cotangent[0])

    first_section = lax.axis_index("section") == 0
    outgoing = jnp.where(first_section, forward_out, grad_input)
    leaving = jnp.where(first_section, grad_input, forward_out)
    arriving = partner(outgoing, "section", 0)
    return (leaving[None], arriving[None])


def solution(mesh):
    placed = (
        P("section", "expert", "hid"),
        P("section", "expert", "hid"),
        P("section", "expert", "hid"),
        P("section", "expert", None),
        P("section", "expert", None),
        P("section", "hid"),
        P("section", "hid", None),
        P("section", "expert", None, "hid"),
        P("section", "expert", None, "hid"),
        P("section", "expert", "hid", None),
    )
    return jax.shard_map(
        per_device,
        mesh=mesh,
        in_specs=placed,
        out_specs=(P("section", "expert", "hid"), P("section", "expert", "hid")),
        check_vma=False,
    )
```

```python
import functools

import jax
import jax.numpy as jnp
from jax import lax
from jax.experimental import pallas as pl
from jax.experimental.pallas import tpu as pltpu
from jax.sharding import PartitionSpec as P

EPSILON = 1e-05
INNER = (((1,), (0,)), ((), ()))
CONTRACT = (((1,), (1,)), ((), ()))
LEADING = (((0,), (0,)), ((), ()))
BOTH = ("expert", "hid")
STEP = 48
GROUPS = 8
TABLE = 32
LIMIT = 56 * 1024 * 1024
MOST = 60 * 1024 * 1024
VMEM = pl.BlockSpec(memory_space=pltpu.VMEM)
SMEM = pl.BlockSpec(memory_space=pltpu.SMEM)
PLACE = pl.BlockSpec(memory_space=pl.ANY)


def product(left, right, dims):
    return lax.dot_general(left, right, dims, preferred_element_type=jnp.float32)


def partner(block, axis, bit):
    count = lax.axis_size(axis)
    route = []
    for low in range(count):
        high = low | 1 << bit
        if high != low and high < count:
            route += [(low, high), (high, low)]
    return lax.ppermute(block, axis, route)


def swap(block, axes):
    return lax.all_to_all(block, axes, split_axis=0, concat_axis=0, tiled=True)


def shift(block, along, across):
    count = lax.axis_size("hid")
    route = []
    for source in range(count):
        x, y = source // 2, source % 2
        route.append((source, (x + along) % (count // 2) * 2 + (y ^ across)))
    return lax.ppermute(block, "hid", route)


def gather_near(block, after=()):
    other = shift(block, 0, 1)
    right, left = shift(block, 1, 0), shift(block, -1, 0)
    other, right, left, after = lax.optimization_barrier((other, right, left, after))
    right_other, left_other = shift(other, 1, 0), shift(other, -1, 0)
    return [block, other, right, right_other, left, left_other], after


def gather_far(near):
    return [shift(near[2], 1, 0), shift(near[5], -1, 0)]


def arrival_order():
    own = lax.axis_index("hid")
    half = lax.axis_size("hid") // 2
    x, y = own // 2, own % 2
    places = []
    for along in (0, -1, 1, 2):
        row = (x + along + half) % half * 2
        places += [row + y, row + 1 - y]
    return jnp.stack(places).astype(jnp.int32)


def three_parts(value):
    high = value.astype(jnp.bfloat16)
    rest = value - high.astype(jnp.float32)
    middle = rest.astype(jnp.bfloat16)
    low = (rest - middle.astype(jnp.float32)).astype(jnp.bfloat16)
    return high, middle, low


def whole(shape):
    return pl.BlockSpec(shape, lambda i: (0,) * len(shape))


def table_kernel(upcoming, gain, router, tokens_out):
    tokens, part = upcoming.shape
    experts = router.shape[0]
    tokens_out[0:tokens, :] = upcoming[...]
    gains = gain[...]
    scaled = router[...] * gains
    rows = [p.astype(jnp.float32) for p in three_parts(scaled)]
    rows += [p.astype(jnp.float32) for p in three_parts(gains)]
    rows.append(jnp.zeros((TABLE - 3 * experts - 3, part), jnp.float32))
    tokens_out[tokens : tokens + TABLE, :] = jnp.concatenate(rows, axis=0).astype(jnp.bfloat16)


def with_table(upcoming, gain, router):
    tokens, part = upcoming.shape
    shape = (tokens + TABLE, part)
    return pl.pallas_call(
        table_kernel,
        out_shape=jax.ShapeDtypeStruct(shape, jnp.bfloat16),
        grid=(1,),
        in_specs=[whole(a.shape) for a in (upcoming, gain, router)],
        out_specs=whole(shape),
        compiler_params=pltpu.CompilerParams(vmem_limit_bytes=MOST),
    )(upcoming, gain, router)


def pack_kernel(experts, capacity, routes_s, routes_n, saved, cot, packed, sel_s, sel_n):
    tokens, part = saved.shape
    row = lax.broadcasted_iota(jnp.int32, (tokens, tokens), 0)
    lane = lax.broadcasted_iota(jnp.int32, (tokens, tokens), 1)
    earlier = jnp.where(lane < row, 1.0, 0.0).astype(jnp.bfloat16)
    wide = lax.broadcasted_iota(jnp.int32, (tokens, 128), 1)
    slots = lax.broadcasted_iota(jnp.int32, (tokens, experts * capacity), 1)

    def select(routes):
        ids = routes[...]
        one, two = ids[:, 0:1], ids[:, 1:2]
        hit_one = jnp.where(wide == one, 1.0, 0.0)
        hit_two = jnp.where(wide == two, 1.0, 0.0)
        counts = product(earlier, (hit_one + hit_two).astype(jnp.bfloat16), INNER)
        rank_one = jnp.sum(counts * hit_one, axis=1, keepdims=True).astype(jnp.int32)
        rank_two = jnp.sum(counts * hit_two, axis=1, keepdims=True).astype(jnp.int32)
        first = jnp.where(slots == one * capacity + rank_one, 1.0, 0.0)
        second = jnp.where(slots == two * capacity + rank_two, 1.0, 0.0)
        inside = wide < 3 * experts
        wide_one = jnp.where(inside & (lax.rem(wide, experts) == one), 1.0, 0.0).astype(jnp.bfloat16)
        wide_two = jnp.where(inside & (lax.rem(wide, experts) == two), 1.0, 0.0).astype(jnp.bfloat16)
        other = product(first.astype(jnp.bfloat16), wide_two, LEADING)
        other = other + product(second.astype(jnp.bfloat16), wide_one, LEADING)
        return (first + second).astype(jnp.bfloat16), other.astype(jnp.bfloat16)

    def put(start, lanes, width, value):
        packed[:, start : start + capacity, lanes : lanes + width] = value.reshape(
            experts, capacity, width
        )

    both, other = select(routes_s)
    sel_s[...] = both
    put(0, 0, part, product(both, saved[...], LEADING).astype(jnp.bfloat16))
    put(capacity, 0, part, product(both, cot[...], LEADING).astype(jnp.bfloat16))
    put(0, part, 128, other)
    both, other = select(routes_n)
    sel_n[...] = both
    put(capacity, part, 128, other)


def pack(routes_s, routes_n, saved, cot, experts, capacity):
    tokens, part = saved.shape
    total = experts * capacity
    shapes = [(experts, 2 * capacity, part + 128), (tokens, total), (tokens, total)]
    return pl.pallas_call(
        functools.partial(pack_kernel, experts, capacity),
        out_shape=[jax.ShapeDtypeStruct(s, jnp.bfloat16) for s in shapes],
        grid=(1,),
        in_specs=[whole(a.shape) for a in (routes_s, routes_n, saved, cot)],
        out_specs=[whole(s) for s in shapes],
        compiler_params=pltpu.CompilerParams(vmem_limit_bytes=MOST),
    )(routes_s, routes_n, saved, cot)


def spread_kernel(sel, *refs):
    pieces, (moved, table) = refs[:GROUPS], refs[GROUPS:]
    tokens = sel.shape[0]
    blocks, _, capacity, part = moved.shape
    for group, piece in enumerate(pieces):
        rows = product(sel[...], piece[0:tokens, :], LEADING).astype(jnp.bfloat16)
        moved[:, group] = rows.reshape(blocks, capacity, part)
        table[group] = piece[tokens : tokens + TABLE, :]


def spread(sel, pieces, blocks):
    part = pieces[0].shape[1]
    capacity = sel.shape[1] // blocks
    return pl.pallas_call(
        spread_kernel,
        out_shape=(
            jax.ShapeDtypeStruct((blocks, GROUPS, capacity, part), jnp.bfloat16),
            jax.ShapeDtypeStruct((GROUPS, TABLE, part), jnp.bfloat16),
        ),
        in_specs=[VMEM] * (1 + GROUPS),
        out_specs=(VMEM, VMEM),
        compiler_params=pltpu.CompilerParams(vmem_limit_bytes=LIMIT // 2),
    )(sel, *pieces)


def widen(value, width):
    return jnp.concatenate([value] * (width // 128), axis=1)


def lanes(value):
    total = value[:, 0:128]
    for start in range(128, value.shape[1], 128):
        total = total + value[:, start : start + 128]
    return total


def even(value):
    return jnp.broadcast_to(jnp.sum(value, axis=1, keepdims=True), (value.shape[0], 128))


def gains_of(table, group):
    rows = table[group, 24:32, :].astype(jnp.float32)
    return rows[0:1] + (rows[1:2] + rows[2:3])


def fetch_rows(order, source, target, sems, part):
    copies = []
    for group in range(GROUPS):
        start = pl.multiple_of(order[group] * part, part)
        copies.append(
            pltpu.make_async_copy(
                source.at[pl.ds(start, part), :],
                target.at[pl.ds(group * part, part), :],
                sems.at[group],
            )
        )
    return copies


def fetch_columns(order, source, target, sems, part):
    copies = []
    for group in range(GROUPS):
        start = group * part
        if order is not None:
            start = pl.multiple_of(order[group] * part, part)
        copies.append(
            pltpu.make_async_copy(
                source.at[:, pl.ds(start, part)],
                target.at[:, pl.ds(group * part, part)],
                sems.at[group],
            )
        )
    return copies


def start(copies):
    for copy in copies:
        copy.start()


def wait(copies):
    for copy in copies:
        copy.wait()


def prepare(own, other_start, take, other, table, normed, scales, diffs, logits, width, between):
    blocks = other.shape[0]
    part = width // GROUPS
    for group in range(GROUPS):
        rows = jnp.concatenate([take(group, block) for block in range(blocks)], axis=0)
        found = product(rows, table[group], CONTRACT)
        if group == 0:
            logits[...] = found
        else:
            logits[...] += found
    start(between)

    @pl.loop(0, blocks)
    def _(block):
        at = pl.ds(pl.multiple_of(block * STEP, STEP), STEP)
        total = jnp.zeros((STEP, 128), jnp.float32)
        for group in range(GROUPS):
            values = take(group, block).astype(jnp.float32)
            total = total + lanes(values * values)
        scale = lax.rsqrt(even(total) / width + EPSILON)
        scales[at, :] = scale
        place = lax.broadcasted_iota(jnp.int32, (STEP, TABLE), 1)
        ours = jnp.where((place < 24) & (lax.rem(place, 8) == own), 1.0, 0.0)
        theirs = other[block, other_start : other_start + STEP, 0:TABLE].astype(jnp.float32)
        diffs[at, :] = even(logits[at, :] * (ours - theirs)) * scale
        for group in range(GROUPS):
            values = take(group, block).astype(jnp.float32)
            normed[at, group * part : (group + 1) * part] = (
                values * widen(scale, part) * gains_of(table, group)
            ).astype(jnp.bfloat16)


def fetch_blocks(source, target, sems):
    return [
        pltpu.make_async_copy(source.at[block], target.at[block], sems.at[block])
        for block in range(source.shape[0])
    ]


def hand_out(group, place, source, target, sems):
    return pltpu.make_async_copy(
        source.at[:, group : group + 1], target.at[:, pl.ds(place, 1)], sems.at[group]
    )


def forward_kernel(
    order, own, moved_in, other, table, gate_w, up_w, down_w, out_to,
    moved, out, gate_b, up_b, down_b, normed, gate, up, hidden, scales, diffs, logits,
    sem_m, sem_o, sem_g, sem_u, sem_d
):
    blocks, _, capacity, part = moved.shape
    arrive = fetch_blocks(moved_in, moved, sem_m)
    start(arrive)
    copies = fetch_rows(order, gate_w, gate_b, sem_g, part)
    copies_up = fetch_rows(order, up_w, up_b, sem_u, part)
    copies_down = fetch_columns(None, down_w, down_b, sem_d, part)
    start(copies)
    wait(arrive)

    def take(group, block):
        return moved[block, group]

    prepare(
        own[0], capacity, take, other, table, normed, scales, diffs, logits, GROUPS * part, copies_up
    )
    wait(copies)
    start(copies_down)
    gate[...] = product(normed[...], gate_b[...], INNER)
    wait(copies_up)
    up[...] = product(normed[...], up_b[...], INNER)

    @pl.loop(0, blocks)
    def _(block):
        at = pl.ds(pl.multiple_of(block * STEP, STEP), STEP)
        value = gate[at, :]
        hidden[at, :] = (value * jax.nn.sigmoid(value) * up[at, :]).astype(jnp.bfloat16)

    share = widen(jax.nn.sigmoid(diffs[...]), part)
    for group in range(GROUPS):
        copies_down[group].wait()
        rows = product(hidden[...], down_b[:, group * part : (group + 1) * part], INNER)
        out[:, group] = (rows * share).astype(jnp.bfloat16).reshape(blocks, capacity, part)
        hand_out(group, group, out, out_to, sem_o).start()
    for group in range(GROUPS):
        hand_out(group, group, out, out_to, sem_o).wait()


def weight_scratch(width, units):
    return [
        pltpu.VMEM((width, units), jnp.bfloat16),
        pltpu.VMEM((width, units), jnp.bfloat16),
        pltpu.VMEM((units, width), jnp.bfloat16),
    ]


def forward(order, own, moved, other, table, gate_w, up_w, down_w):
    blocks, _, capacity, part = moved.shape
    width, units = gate_w.shape
    total = blocks * capacity
    return pl.pallas_call(
        forward_kernel,
        out_shape=jax.ShapeDtypeStruct(moved.shape, jnp.bfloat16),
        in_specs=[SMEM, SMEM, PLACE, VMEM, VMEM, PLACE, PLACE, PLACE],
        out_specs=PLACE,
        scratch_shapes=[pltpu.VMEM(moved.shape, jnp.bfloat16)] * 2
        + weight_scratch(width, units)
        + [
            pltpu.VMEM((total, width), jnp.bfloat16),
            pltpu.VMEM((total, units), jnp.float32),
            pltpu.VMEM((total, units), jnp.float32),
            pltpu.VMEM((total, units), jnp.bfloat16),
            pltpu.VMEM((total, 128), jnp.float32),
            pltpu.VMEM((total, 128), jnp.float32),
            pltpu.VMEM((total, TABLE), jnp.float32),
        ]
        + [pltpu.SemaphoreType.DMA((blocks,))]
        + [pltpu.SemaphoreType.DMA((GROUPS,))] * 4,
        compiler_params=pltpu.CompilerParams(vmem_limit_bytes=LIMIT),
        cost_estimate=pl.CostEstimate(
            flops=6 * total * width * units,
            bytes_accessed=6 * width * units + 4 * total * width,
            transcendentals=total * units,
        ),
    )(order, own, moved, other, table, gate_w, up_w, down_w)


def backward_kernel(*refs):
    order, own, other, table, gate_w, up_w, down_w = refs[:7]
    pieces_in = refs[7 : 7 + GROUPS]
    out_to, pieces = refs[7 + GROUPS], refs[8 + GROUPS : 8 + 2 * GROUPS]
    (
        out, gate_b, up_b, down_b, normed, cots, gate, up, grad, grad_gate, grad_up,
        scales, diffs, ones, twos, logits, sem_m, sem_o, sem_g, sem_u, sem_d,
    ) = refs[8 + 2 * GROUPS :]
    blocks, _, capacity, part = out.shape
    width = GROUPS * part
    arrive = [
        pltpu.make_async_copy(pieces_in[group], pieces[group], sem_m.at[group])
        for group in range(GROUPS)
    ]
    start(arrive)
    copies = fetch_rows(order, gate_w, gate_b, sem_g, part)
    copies_up = fetch_rows(order, up_w, up_b, sem_u, part)
    copies_down = fetch_columns(order, down_w, down_b, sem_d, part)
    start(copies)
    wait(arrive)

    def take(group, block):
        return pieces[group][block, 0:STEP, :]

    prepare(own[0], 0, take, other, table, normed, scales, diffs, logits, width, copies_up)

    @pl.loop(0, blocks)
    def _(block):
        at = pl.ds(pl.multiple_of(block * STEP, STEP), STEP)
        for group in range(GROUPS):
            cots[at, group * part : (group + 1) * part] = pieces[group][block, STEP : 2 * STEP, :]

    wait(copies)
    start(copies_down)
    gate[...] = product(normed[...], gate_b[...], INNER)
    wait(copies_up)
    up[...] = product(normed[...], up_b[...], INNER)
    wait(copies_down)
    grad[...] = product(cots[...], down_b[...], CONTRACT)

    @pl.loop(0, blocks)
    def _(block):
        at = pl.ds(pl.multiple_of(block * STEP, STEP), STEP)
        slope, value, lift = grad[at, :], gate[at, :], up[at, :]
        sig = jax.nn.sigmoid(value)
        silu = value * sig
        hidden = (silu * lift).astype(jnp.bfloat16).astype(jnp.float32)
        to_gate = (slope * lift * (sig * (1.0 + value * (1.0 - sig)))).astype(jnp.bfloat16)
        to_up = (slope * silu).astype(jnp.bfloat16)
        grad_gate[at, :] = to_gate
        grad_up[at, :] = to_up
        row_dot = even(lanes(slope * hidden))
        norm_dot = even(
            lanes(to_gate.astype(jnp.float32) * value + to_up.astype(jnp.float32) * lift)
        )
        scale, diff = scales[at, :], diffs[at, :]
        ours, theirs = jax.nn.sigmoid(diff), jax.nn.sigmoid(-diff)
        through = ours * theirs * row_dot
        ones[at, :] = scale * through
        twos[at, :] = scale * scale * ((ours * norm_dot + through * diff) / width)
        diffs[at, :] = scale * ours

    place = lax.broadcasted_iota(jnp.int32, (blocks * STEP, TABLE), 1)
    away = jnp.where((place < 24) & (lax.rem(place, 8) == own[0]), 1.0, 0.0)
    away = away - jnp.concatenate(
        [other[block, 0:STEP, 0:TABLE].astype(jnp.float32) for block in range(blocks)], axis=0
    )
    away = away.astype(jnp.bfloat16)
    for group in range(GROUPS):
        at = slice(group * part, (group + 1) * part)
        rows = product(grad_gate[...], gate_b[at, :], CONTRACT)
        rows = rows + product(grad_up[...], up_b[at, :], CONTRACT)
        turn = product(away, table[group], INNER)
        values = jnp.concatenate([take(group, block) for block in range(blocks)], axis=0)
        rows = (
            rows * (widen(diffs[...], part) * gains_of(table, group))
            + turn * widen(ones[...], part)
            - values.astype(jnp.float32) * widen(twos[...], part)
        )
        out[:, group] = rows.astype(jnp.bfloat16).reshape(blocks, capacity, part)
        hand_out(group, order[group], out, out_to, sem_o).start()
    for group in range(GROUPS):
        hand_out(group, order[group], out, out_to, sem_o).wait()


def backward(order, own, other, table, gate_w, up_w, down_w, pieces):
    blocks, double, part = pieces[0].shape
    capacity = double // 2
    width, units = gate_w.shape
    total = blocks * capacity
    small = pltpu.VMEM((total, 128), jnp.float32)
    return pl.pallas_call(
        backward_kernel,
        out_shape=jax.ShapeDtypeStruct((blocks, GROUPS, capacity, part), jnp.bfloat16),
        in_specs=[SMEM, SMEM, VMEM, VMEM, PLACE, PLACE, PLACE] + [PLACE] * GROUPS,
        out_specs=PLACE,
        scratch_shapes=[pltpu.VMEM((blocks, double, part), jnp.bfloat16)] * GROUPS
        + [pltpu.VMEM((blocks, GROUPS, capacity, part), jnp.bfloat16)]
        + weight_scratch(width, units)
        + [
            pltpu.VMEM((total, width), jnp.bfloat16),
            pltpu.VMEM((total, width), jnp.bfloat16),
            pltpu.VMEM((total, units), jnp.float32),
            pltpu.VMEM((total, units), jnp.float32),
            pltpu.VMEM((total, units), jnp.float32),
            pltpu.VMEM((total, units), jnp.bfloat16),
            pltpu.VMEM((total, units), jnp.bfloat16),
            small,
            small,
            small,
            small,
            pltpu.VMEM((total, TABLE), jnp.float32),
        ]
        + [pltpu.SemaphoreType.DMA((GROUPS,))] * 5,
        compiler_params=pltpu.CompilerParams(vmem_limit_bytes=LIMIT),
        cost_estimate=pl.CostEstimate(
            flops=10 * total * width * units,
            bytes_accessed=6 * width * units + 6 * total * width,
            transcendentals=total * units,
        ),
    )(order, own, other, table, gate_w, up_w, down_w, *pieces)


def finish_kernel(sel, home, base, out):
    blocks, groups, capacity, part = home.shape
    total = base[...].astype(jnp.float32)
    for group in range(groups):
        total = total + product(sel[...], home[:, group].reshape(blocks * capacity, part), INNER)
    out[...] = total.astype(jnp.bfloat16)


def finish(sel, home, base):
    return pl.pallas_call(
        finish_kernel,
        out_shape=jax.ShapeDtypeStruct(base.shape, jnp.bfloat16),
        in_specs=[VMEM] * 3,
        out_specs=VMEM,
        compiler_params=pltpu.CompilerParams(vmem_limit_bytes=LIMIT // 2),
    )(sel, home, base)


def send_home(pieces):
    experts, hids, capacity, part = pieces.shape
    home = swap(pieces.reshape(experts * hids, capacity, part), BOTH)
    return home.reshape(experts, hids, capacity, part)


def per_device(
    saved_input,
    cotangent,
    next_input,
    routes_saved,
    routes_next,
    norm_gain,
    router,
    expert_gate,
    expert_up,
    expert_down,
):
    gate_w, up_w, down_w = expert_gate[0, 0], expert_up[0, 0], expert_down[0, 0]
    tokens, part = saved_input.shape[1:]
    experts = lax.axis_size("expert")
    capacity = 3 * tokens // experts
    own = lax.axis_index("expert").astype(jnp.int32).reshape(1)
    order = arrival_order()

    tokens_next = with_table(next_input[0], norm_gain, router[0].T)
    tokens_next, routes = lax.optimization_barrier((tokens_next, (routes_saved[0], routes_next[0])))
    packed, sel_saved, sel_next = pack(*routes, saved_input[0], cotangent[0], experts, capacity)
    near, packed = gather_near(tokens_next, packed)
    packed = swap(packed, "expert")
    moved_next, table = spread(sel_next, near + gather_far(near), experts)
    moved_next = swap(moved_next, "expert")
    other = packed[:, :, part:]
    near, _ = gather_near(packed[:, :, :part])
    near, moved_next = lax.optimization_barrier((near, moved_next))
    far = gather_far(near)
    out_next = forward(order, own, moved_next, other, table, gate_w, up_w, down_w)
    far, out_next = lax.optimization_barrier((far, out_next))
    pieces = near + far
    out_home = send_home(out_next)
    back_part = backward(order, own, other, table, gate_w, up_w, down_w, pieces)
    back_home = send_home(back_part)

    forward_out = finish(sel_next, out_home, next_input[0])
    grad_input = finish(sel_saved, back_home, cotangent[0])

    first_section = lax.axis_index("section") == 0
    outgoing = jnp.where(first_section, forward_out, grad_input)
    leaving = jnp.where(first_section, grad_input, forward_out)
    arriving = partner(outgoing, "section", 0)
    return (leaving[None], arriving[None])


def solution(mesh):
    placed = (
        P("section", "expert", "hid"),
        P("section", "expert", "hid"),
        P("section", "expert", "hid"),
        P("section", "expert", None),
        P("section", "expert", None),
        P("section", "hid"),
        P("section", "hid", None),
        P("section", "expert", None, "hid"),
        P("section", "expert", None, "hid"),
        P("section", "expert", "hid", None),
    )
    return jax.shard_map(
        per_device,
        mesh=mesh,
        in_specs=placed,
        out_specs=(P("section", "expert", "hid"), P("section", "expert", "hid")),
        check_vma=False,
    )
```

```python
import functools

import jax
import jax.numpy as jnp
from jax import lax
from jax.experimental import pallas as pl
from jax.experimental.pallas import tpu as pltpu
from jax.sharding import PartitionSpec as P

EPSILON = 1e-05
INNER = (((1,), (0,)), ((), ()))
CONTRACT = (((1,), (1,)), ((), ()))
LEADING = (((0,), (0,)), ((), ()))
BOTH = ("expert", "hid")
STEP = 48
GROUPS = 8
TABLE = 32
LIMIT = 56 * 1024 * 1024
MOST = 60 * 1024 * 1024
VMEM = pl.BlockSpec(memory_space=pltpu.VMEM)
SMEM = pl.BlockSpec(memory_space=pltpu.SMEM)
PLACE = pl.BlockSpec(memory_space=pl.ANY)


def product(left, right, dims):
    return lax.dot_general(left, right, dims, preferred_element_type=jnp.float32)


def partner(block, axis, bit):
    count = lax.axis_size(axis)
    route = []
    for low in range(count):
        high = low | 1 << bit
        if high != low and high < count:
            route += [(low, high), (high, low)]
    return lax.ppermute(block, axis, route)


def swap(block, axes):
    return lax.all_to_all(block, axes, split_axis=0, concat_axis=0, tiled=True)


def shift(block, along, across):
    count = lax.axis_size("hid")
    route = []
    for source in range(count):
        x, y = source // 2, source % 2
        route.append((source, (x + along) % (count // 2) * 2 + (y ^ across)))
    return lax.ppermute(block, "hid", route)


def gather_near(block, after=()):
    other = shift(block, 0, 1)
    right, left = shift(block, 1, 0), shift(block, -1, 0)
    other, right, left, after = lax.optimization_barrier((other, right, left, after))
    right_other, left_other = shift(other, 1, 0), shift(other, -1, 0)
    return [block, other, right, right_other, left, left_other], after


def gather_far(near):
    return [shift(near[2], 1, 0), shift(near[5], -1, 0)]


def arrival_order():
    own = lax.axis_index("hid")
    half = lax.axis_size("hid") // 2
    x, y = own // 2, own % 2
    places = []
    for along in (0, -1, 1, 2):
        row = (x + along + half) % half * 2
        places += [row + y, row + 1 - y]
    return jnp.stack(places).astype(jnp.int32)


def three_parts(value):
    high = value.astype(jnp.bfloat16)
    rest = value - high.astype(jnp.float32)
    middle = rest.astype(jnp.bfloat16)
    low = (rest - middle.astype(jnp.float32)).astype(jnp.bfloat16)
    return high, middle, low


def whole(shape):
    return pl.BlockSpec(shape, lambda i: (0,) * len(shape))


def table_kernel(upcoming, gain, router, tokens_out):
    tokens, part = upcoming.shape
    experts = router.shape[0]
    gains = gain[...]
    scaled = router[...] * gains
    rows = [p.astype(jnp.float32) for p in three_parts(scaled)]
    rows += [p.astype(jnp.float32) for p in three_parts(gains)]
    rows.append(jnp.zeros((TABLE - 3 * experts - 3, part), jnp.float32))
    table = jnp.concatenate(rows, axis=0).astype(jnp.bfloat16)
    for copy in range(tokens_out.shape[0]):
        tokens_out[copy, 0:tokens, :] = upcoming[...]
        tokens_out[copy, tokens : tokens + TABLE, :] = table


def with_table(upcoming, gain, router):
    tokens, part = upcoming.shape
    shape = (GROUPS, tokens + TABLE, part)
    return pl.pallas_call(
        table_kernel,
        out_shape=jax.ShapeDtypeStruct(shape, jnp.bfloat16),
        grid=(1,),
        in_specs=[whole(a.shape) for a in (upcoming, gain, router)],
        out_specs=whole(shape),
        compiler_params=pltpu.CompilerParams(vmem_limit_bytes=MOST),
    )(upcoming, gain, router)


def pack_kernel(experts, capacity, routes_s, routes_n, saved, cot, packed, sel_s, sel_n):
    tokens, part = saved.shape
    row = lax.broadcasted_iota(jnp.int32, (tokens, tokens), 0)
    lane = lax.broadcasted_iota(jnp.int32, (tokens, tokens), 1)
    earlier = jnp.where(lane < row, 1.0, 0.0).astype(jnp.bfloat16)
    wide = lax.broadcasted_iota(jnp.int32, (tokens, 128), 1)
    slots = lax.broadcasted_iota(jnp.int32, (tokens, experts * capacity), 1)

    def select(routes):
        ids = routes[...]
        one, two = ids[:, 0:1], ids[:, 1:2]
        hit_one = jnp.where(wide == one, 1.0, 0.0)
        hit_two = jnp.where(wide == two, 1.0, 0.0)
        counts = product(earlier, (hit_one + hit_two).astype(jnp.bfloat16), INNER)
        rank_one = jnp.sum(counts * hit_one, axis=1, keepdims=True).astype(jnp.int32)
        rank_two = jnp.sum(counts * hit_two, axis=1, keepdims=True).astype(jnp.int32)
        first = jnp.where(slots == one * capacity + rank_one, 1.0, 0.0)
        second = jnp.where(slots == two * capacity + rank_two, 1.0, 0.0)
        inside = wide < 3 * experts
        wide_one = jnp.where(inside & (lax.rem(wide, experts) == one), 1.0, 0.0).astype(jnp.bfloat16)
        wide_two = jnp.where(inside & (lax.rem(wide, experts) == two), 1.0, 0.0).astype(jnp.bfloat16)
        other = product(first.astype(jnp.bfloat16), wide_two, LEADING)
        other = other + product(second.astype(jnp.bfloat16), wide_one, LEADING)
        return (first + second).astype(jnp.bfloat16), other.astype(jnp.bfloat16)

    def put(start, lanes, width, value):
        packed[:, start : start + capacity, lanes : lanes + width] = value.reshape(
            experts, capacity, width
        )

    both, other = select(routes_s)
    sel_s[...] = both
    put(0, 0, part, product(both, saved[...], LEADING).astype(jnp.bfloat16))
    put(capacity, 0, part, product(both, cot[...], LEADING).astype(jnp.bfloat16))
    put(0, part, 128, other)
    both, other = select(routes_n)
    sel_n[...] = both
    put(capacity, part, 128, other)


def pack(routes_s, routes_n, saved, cot, experts, capacity):
    tokens, part = saved.shape
    total = experts * capacity
    shapes = [(experts, 2 * capacity, part + 128), (tokens, total), (tokens, total)]
    return pl.pallas_call(
        functools.partial(pack_kernel, experts, capacity),
        out_shape=[jax.ShapeDtypeStruct(s, jnp.bfloat16) for s in shapes],
        grid=(1,),
        in_specs=[whole(a.shape) for a in (routes_s, routes_n, saved, cot)],
        out_specs=[whole(s) for s in shapes],
        compiler_params=pltpu.CompilerParams(vmem_limit_bytes=MOST),
    )(routes_s, routes_n, saved, cot)


def spread_kernel(order, sel, pieces, moved, table):
    tokens = sel.shape[0]
    blocks, _, capacity, part = moved.shape
    for group in range(GROUPS):
        piece = pieces[order[group]]
        rows = product(sel[...], piece[0:tokens, :], LEADING).astype(jnp.bfloat16)
        moved[:, group] = rows.reshape(blocks, capacity, part)
        table[group] = piece[tokens : tokens + TABLE, :]


def spread(order, sel, pieces, blocks):
    part = pieces.shape[2]
    capacity = sel.shape[1] // blocks
    return pl.pallas_call(
        spread_kernel,
        out_shape=(
            jax.ShapeDtypeStruct((blocks, GROUPS, capacity, part), jnp.bfloat16),
            jax.ShapeDtypeStruct((GROUPS, TABLE, part), jnp.bfloat16),
        ),
        grid=(1,),
        in_specs=[SMEM, whole(sel.shape), whole(pieces.shape)],
        out_specs=(whole((blocks, GROUPS, capacity, part)), whole((GROUPS, TABLE, part))),
        compiler_params=pltpu.CompilerParams(vmem_limit_bytes=MOST),
    )(order, sel, pieces)


def widen(value, width):
    return jnp.concatenate([value] * (width // 128), axis=1)


def lanes(value):
    total = value[:, 0:128]
    for start in range(128, value.shape[1], 128):
        total = total + value[:, start : start + 128]
    return total


def even(value):
    return jnp.broadcast_to(jnp.sum(value, axis=1, keepdims=True), (value.shape[0], 128))


def gains_of(table, group):
    rows = table[group, 24:32, :].astype(jnp.float32)
    return rows[0:1] + (rows[1:2] + rows[2:3])


def fetch_rows(order, source, target, sems, part):
    copies = []
    for group in range(GROUPS):
        start = pl.multiple_of(order[group] * part, part)
        copies.append(
            pltpu.make_async_copy(
                source.at[pl.ds(start, part), :],
                target.at[pl.ds(group * part, part), :],
                sems.at[group],
            )
        )
    return copies


def fetch_columns(order, source, target, sems, part):
    copies = []
    for group in range(GROUPS):
        start = group * part
        if order is not None:
            start = pl.multiple_of(order[group] * part, part)
        copies.append(
            pltpu.make_async_copy(
                source.at[:, pl.ds(start, part)],
                target.at[:, pl.ds(group * part, part)],
                sems.at[group],
            )
        )
    return copies


def start(copies):
    for copy in copies:
        copy.start()


def wait(copies):
    for copy in copies:
        copy.wait()


def prepare(own, other_start, take, other, table, normed, scales, diffs, logits, width, between):
    blocks = other.shape[0]
    part = width // GROUPS
    for group in range(GROUPS):
        rows = jnp.concatenate([take(group, block) for block in range(blocks)], axis=0)
        found = product(rows, table[group], CONTRACT)
        if group == 0:
            logits[...] = found
        else:
            logits[...] += found
    start(between)

    @pl.loop(0, blocks)
    def _(block):
        at = pl.ds(pl.multiple_of(block * STEP, STEP), STEP)
        total = jnp.zeros((STEP, 128), jnp.float32)
        for group in range(GROUPS):
            values = take(group, block).astype(jnp.float32)
            total = total + lanes(values * values)
        scale = lax.rsqrt(even(total) / width + EPSILON)
        scales[at, :] = scale
        place = lax.broadcasted_iota(jnp.int32, (STEP, TABLE), 1)
        ours = jnp.where((place < 24) & (lax.rem(place, 8) == own), 1.0, 0.0)
        theirs = other[block, other_start : other_start + STEP, 0:TABLE].astype(jnp.float32)
        diffs[at, :] = even(logits[at, :] * (ours - theirs)) * scale
        for group in range(GROUPS):
            values = take(group, block).astype(jnp.float32)
            normed[at, group * part : (group + 1) * part] = (
                values * widen(scale, part) * gains_of(table, group)
            ).astype(jnp.bfloat16)


def fetch_blocks(source, target, sems):
    return [
        pltpu.make_async_copy(source.at[block], target.at[block], sems.at[block])
        for block in range(source.shape[0])
    ]


def hand_out(group, place, source, target, sems):
    return pltpu.make_async_copy(
        source.at[:, group : group + 1], target.at[:, pl.ds(place, 1)], sems.at[group]
    )


def forward_kernel(
    order, own, moved_in, other, table, gate_w, up_w, down_w, out_to,
    moved, out, gate_b, up_b, down_b, normed, gate, up, hidden, scales, diffs, logits,
    sem_m, sem_o, sem_g, sem_u, sem_d
):
    blocks, _, capacity, part = moved.shape
    arrive = fetch_blocks(moved_in, moved, sem_m)
    start(arrive)
    copies = fetch_rows(order, gate_w, gate_b, sem_g, part)
    copies_up = fetch_rows(order, up_w, up_b, sem_u, part)
    copies_down = fetch_columns(None, down_w, down_b, sem_d, part)
    start(copies)
    wait(arrive)

    def take(group, block):
        return moved[block, group]

    prepare(
        own[0], capacity, take, other, table, normed, scales, diffs, logits, GROUPS * part, copies_up
    )
    wait(copies)
    start(copies_down)
    gate[...] = product(normed[...], gate_b[...], INNER)
    wait(copies_up)
    up[...] = product(normed[...], up_b[...], INNER)

    @pl.loop(0, blocks)
    def _(block):
        at = pl.ds(pl.multiple_of(block * STEP, STEP), STEP)
        value = gate[at, :]
        hidden[at, :] = (value * jax.nn.sigmoid(value) * up[at, :]).astype(jnp.bfloat16)

    share = widen(jax.nn.sigmoid(diffs[...]), part)
    for group in range(GROUPS):
        copies_down[group].wait()
        rows = product(hidden[...], down_b[:, group * part : (group + 1) * part], INNER)
        out[:, group] = (rows * share).astype(jnp.bfloat16).reshape(blocks, capacity, part)
        hand_out(group, group, out, out_to, sem_o).start()
    for group in range(GROUPS):
        hand_out(group, group, out, out_to, sem_o).wait()


def weight_scratch(width, units):
    return [
        pltpu.VMEM((width, units), jnp.bfloat16),
        pltpu.VMEM((width, units), jnp.bfloat16),
        pltpu.VMEM((units, width), jnp.bfloat16),
    ]


def forward(order, own, moved, other, table, gate_w, up_w, down_w):
    blocks, _, capacity, part = moved.shape
    width, units = gate_w.shape
    total = blocks * capacity
    return pl.pallas_call(
        forward_kernel,
        out_shape=jax.ShapeDtypeStruct(moved.shape, jnp.bfloat16),
        in_specs=[SMEM, SMEM, PLACE, VMEM, VMEM, PLACE, PLACE, PLACE],
        out_specs=PLACE,
        scratch_shapes=[pltpu.VMEM(moved.shape, jnp.bfloat16)] * 2
        + weight_scratch(width, units)
        + [
            pltpu.VMEM((total, width), jnp.bfloat16),
            pltpu.VMEM((total, units), jnp.float32),
            pltpu.VMEM((total, units), jnp.float32),
            pltpu.VMEM((total, units), jnp.bfloat16),
            pltpu.VMEM((total, 128), jnp.float32),
            pltpu.VMEM((total, 128), jnp.float32),
            pltpu.VMEM((total, TABLE), jnp.float32),
        ]
        + [pltpu.SemaphoreType.DMA((blocks,))]
        + [pltpu.SemaphoreType.DMA((GROUPS,))] * 4,
        compiler_params=pltpu.CompilerParams(vmem_limit_bytes=LIMIT),
        cost_estimate=pl.CostEstimate(
            flops=6 * total * width * units,
            bytes_accessed=6 * width * units + 4 * total * width,
            transcendentals=total * units,
        ),
    )(order, own, moved, other, table, gate_w, up_w, down_w)


def backward_kernel(*refs):
    order, own, other, table, gate_w, up_w, down_w = refs[:7]
    pieces_in = refs[7 : 7 + GROUPS]
    out_to, pieces = refs[7 + GROUPS], refs[8 + GROUPS : 8 + 2 * GROUPS]
    (
        out, gate_b, up_b, down_b, normed, cots, gate, up, grad, grad_gate, grad_up,
        scales, diffs, ones, twos, logits, sem_m, sem_o, sem_g, sem_u, sem_d,
    ) = refs[8 + 2 * GROUPS :]
    blocks, _, capacity, part = out.shape
    width = GROUPS * part
    arrive = [
        pltpu.make_async_copy(pieces_in[group], pieces[group], sem_m.at[group])
        for group in range(GROUPS)
    ]
    start(arrive)
    copies = fetch_rows(order, gate_w, gate_b, sem_g, part)
    copies_up = fetch_rows(order, up_w, up_b, sem_u, part)
    copies_down = fetch_columns(order, down_w, down_b, sem_d, part)
    start(copies)
    wait(arrive)

    def take(group, block):
        return pieces[group][block, 0:STEP, :]

    prepare(own[0], 0, take, other, table, normed, scales, diffs, logits, width, copies_up)

    @pl.loop(0, blocks)
    def _(block):
        at = pl.ds(pl.multiple_of(block * STEP, STEP), STEP)
        for group in range(GROUPS):
            cots[at, group * part : (group + 1) * part] = pieces[group][block, STEP : 2 * STEP, :]

    wait(copies)
    start(copies_down)
    gate[...] = product(normed[...], gate_b[...], INNER)
    wait(copies_up)
    up[...] = product(normed[...], up_b[...], INNER)
    wait(copies_down)
    grad[...] = product(cots[...], down_b[...], CONTRACT)

    @pl.loop(0, blocks)
    def _(block):
        at = pl.ds(pl.multiple_of(block * STEP, STEP), STEP)
        slope, value, lift = grad[at, :], gate[at, :], up[at, :]
        sig = jax.nn.sigmoid(value)
        silu = value * sig
        hidden = (silu * lift).astype(jnp.bfloat16).astype(jnp.float32)
        to_gate = (slope * lift * (sig * (1.0 + value * (1.0 - sig)))).astype(jnp.bfloat16)
        to_up = (slope * silu).astype(jnp.bfloat16)
        grad_gate[at, :] = to_gate
        grad_up[at, :] = to_up
        row_dot = even(lanes(slope * hidden))
        norm_dot = even(
            lanes(to_gate.astype(jnp.float32) * value + to_up.astype(jnp.float32) * lift)
        )
        scale, diff = scales[at, :], diffs[at, :]
        ours, theirs = jax.nn.sigmoid(diff), jax.nn.sigmoid(-diff)
        through = ours * theirs * row_dot
        ones[at, :] = scale * through
        twos[at, :] = scale * scale * ((ours * norm_dot + through * diff) / width)
        diffs[at, :] = scale * ours

    place = lax.broadcasted_iota(jnp.int32, (blocks * STEP, TABLE), 1)
    away = jnp.where((place < 24) & (lax.rem(place, 8) == own[0]), 1.0, 0.0)
    away = away - jnp.concatenate(
        [other[block, 0:STEP, 0:TABLE].astype(jnp.float32) for block in range(blocks)], axis=0
    )
    away = away.astype(jnp.bfloat16)
    for group in range(GROUPS):
        at = slice(group * part, (group + 1) * part)
        rows = product(grad_gate[...], gate_b[at, :], CONTRACT)
        rows = rows + product(grad_up[...], up_b[at, :], CONTRACT)
        turn = product(away, table[group], INNER)
        values = jnp.concatenate([take(group, block) for block in range(blocks)], axis=0)
        rows = (
            rows * (widen(diffs[...], part) * gains_of(table, group))
            + turn * widen(ones[...], part)
            - values.astype(jnp.float32) * widen(twos[...], part)
        )
        out[:, group] = rows.astype(jnp.bfloat16).reshape(blocks, capacity, part)
        hand_out(group, order[group], out, out_to, sem_o).start()
    for group in range(GROUPS):
        hand_out(group, order[group], out, out_to, sem_o).wait()


def backward(order, own, other, table, gate_w, up_w, down_w, pieces):
    blocks, double, part = pieces[0].shape
    capacity = double // 2
    width, units = gate_w.shape
    total = blocks * capacity
    small = pltpu.VMEM((total, 128), jnp.float32)
    return pl.pallas_call(
        backward_kernel,
        out_shape=jax.ShapeDtypeStruct((blocks, GROUPS, capacity, part), jnp.bfloat16),
        in_specs=[SMEM, SMEM, VMEM, VMEM, PLACE, PLACE, PLACE] + [PLACE] * GROUPS,
        out_specs=PLACE,
        scratch_shapes=[pltpu.VMEM((blocks, double, part), jnp.bfloat16)] * GROUPS
        + [pltpu.VMEM((blocks, GROUPS, capacity, part), jnp.bfloat16)]
        + weight_scratch(width, units)
        + [
            pltpu.VMEM((total, width), jnp.bfloat16),
            pltpu.VMEM((total, width), jnp.bfloat16),
            pltpu.VMEM((total, units), jnp.float32),
            pltpu.VMEM((total, units), jnp.float32),
            pltpu.VMEM((total, units), jnp.float32),
            pltpu.VMEM((total, units), jnp.bfloat16),
            pltpu.VMEM((total, units), jnp.bfloat16),
            small,
            small,
            small,
            small,
            pltpu.VMEM((total, TABLE), jnp.float32),
        ]
        + [pltpu.SemaphoreType.DMA((GROUPS,))] * 5,
        compiler_params=pltpu.CompilerParams(vmem_limit_bytes=LIMIT),
        cost_estimate=pl.CostEstimate(
            flops=10 * total * width * units,
            bytes_accessed=6 * width * units + 6 * total * width,
            transcendentals=total * units,
        ),
    )(order, own, other, table, gate_w, up_w, down_w, *pieces)


def finish_kernel(sel, home, base, out):
    blocks, groups, capacity, part = home.shape
    total = base[...].astype(jnp.float32)
    for group in range(groups):
        total = total + product(sel[...], home[:, group].reshape(blocks * capacity, part), INNER)
    out[...] = total.astype(jnp.bfloat16)


def finish(sel, home, base):
    return pl.pallas_call(
        finish_kernel,
        out_shape=jax.ShapeDtypeStruct(base.shape, jnp.bfloat16),
        in_specs=[VMEM] * 3,
        out_specs=VMEM,
        compiler_params=pltpu.CompilerParams(vmem_limit_bytes=LIMIT // 2),
    )(sel, home, base)


def send_home(pieces):
    experts, hids, capacity, part = pieces.shape
    home = swap(pieces.reshape(experts * hids, capacity, part), BOTH)
    return home.reshape(experts, hids, capacity, part)


def per_device(
    saved_input,
    cotangent,
    next_input,
    routes_saved,
    routes_next,
    norm_gain,
    router,
    expert_gate,
    expert_up,
    expert_down,
):
    gate_w, up_w, down_w = expert_gate[0, 0], expert_up[0, 0], expert_down[0, 0]
    tokens, part = saved_input.shape[1:]
    experts = lax.axis_size("expert")
    capacity = 3 * tokens // experts
    own = lax.axis_index("expert").astype(jnp.int32).reshape(1)
    order = arrival_order()

    tokens_next = with_table(next_input[0], norm_gain, router[0].T)
    tokens_next, routes = lax.optimization_barrier((tokens_next, (routes_saved[0], routes_next[0])))
    packed, sel_saved, sel_next = pack(*routes, saved_input[0], cotangent[0], experts, capacity)
    tokens_next = swap(tokens_next, "hid")
    packed = swap(packed, "expert")
    moved_next, table = spread(order, sel_next, tokens_next, experts)
    moved_next = swap(moved_next, "expert")
    other = packed[:, :, part:]
    near, _ = gather_near(packed[:, :, :part])
    near, moved_next = lax.optimization_barrier((near, moved_next))
    far = gather_far(near)
    out_next = forward(order, own, moved_next, other, table, gate_w, up_w, down_w)
    far, out_next = lax.optimization_barrier((far, out_next))
    pieces = near + far
    out_home = send_home(out_next)
    back_part = backward(order, own, other, table, gate_w, up_w, down_w, pieces)
    back_home = send_home(back_part)

    forward_out = finish(sel_next, out_home, next_input[0])
    grad_input = finish(sel_saved, back_home, cotangent[0])

    first_section = lax.axis_index("section") == 0
    outgoing = jnp.where(first_section, forward_out, grad_input)
    leaving = jnp.where(first_section, grad_input, forward_out)
    arriving = partner(outgoing, "section", 0)
    return (leaving[None], arriving[None])


def solution(mesh):
    placed = (
        P("section", "expert", "hid"),
        P("section", "expert", "hid"),
        P("section", "expert", "hid"),
        P("section", "expert", None),
        P("section", "expert", None),
        P("section", "hid"),
        P("section", "hid", None),
        P("section", "expert", None, "hid"),
        P("section", "expert", None, "hid"),
        P("section", "expert", "hid", None),
    )
    return jax.shard_map(
        per_device,
        mesh=mesh,
        in_specs=placed,
        out_specs=(P("section", "expert", "hid"), P("section", "expert", "hid")),
        check_vma=False,
    )
```

```python
import functools

import jax
import jax.numpy as jnp
from jax import lax
from jax.experimental import pallas as pl
from jax.experimental.pallas import tpu as pltpu
from jax.sharding import PartitionSpec as P

EPSILON = 1e-05
INNER = (((1,), (0,)), ((), ()))
CONTRACT = (((1,), (1,)), ((), ()))
LEADING = (((0,), (0,)), ((), ()))
BOTH = ("expert", "hid")
STEP = 48
GROUPS = 8
TABLE = 32
LIMIT = 56 * 1024 * 1024
MOST = 60 * 1024 * 1024
VMEM = pl.BlockSpec(memory_space=pltpu.VMEM)
SMEM = pl.BlockSpec(memory_space=pltpu.SMEM)
PLACE = pl.BlockSpec(memory_space=pl.ANY)


def product(left, right, dims):
    return lax.dot_general(left, right, dims, preferred_element_type=jnp.float32)


def partner(block, axis, bit):
    count = lax.axis_size(axis)
    route = []
    for low in range(count):
        high = low | 1 << bit
        if high != low and high < count:
            route += [(low, high), (high, low)]
    return lax.ppermute(block, axis, route)


def swap(block, axes):
    return lax.all_to_all(block, axes, split_axis=0, concat_axis=0, tiled=True)


def shift(block, along, across):
    count = lax.axis_size("hid")
    route = []
    for source in range(count):
        x, y = source // 2, source % 2
        route.append((source, (x + along) % (count // 2) * 2 + (y ^ across)))
    return lax.ppermute(block, "hid", route)


def gather_near(block, after=()):
    other = shift(block, 0, 1)
    right, left = shift(block, 1, 0), shift(block, -1, 0)
    other, right, left, after = lax.optimization_barrier((other, right, left, after))
    right_other, left_other = shift(other, 1, 0), shift(other, -1, 0)
    return [block, other, right, right_other, left, left_other], after


def gather_far(near):
    return [shift(near[2], 1, 0), shift(near[5], -1, 0)]


def arrival_order():
    own = lax.axis_index("hid")
    half = lax.axis_size("hid") // 2
    x, y = own // 2, own % 2
    places = []
    for along in (0, -1, 1, 2):
        row = (x + along + half) % half * 2
        places += [row + y, row + 1 - y]
    return jnp.stack(places).astype(jnp.int32)


def three_parts(value):
    high = value.astype(jnp.bfloat16)
    rest = value - high.astype(jnp.float32)
    middle = rest.astype(jnp.bfloat16)
    low = (rest - middle.astype(jnp.float32)).astype(jnp.bfloat16)
    return high, middle, low


def whole(shape):
    return pl.BlockSpec(shape, lambda i: (0,) * len(shape))


def table_kernel(upcoming, gain, router, tokens_out):
    tokens, part = upcoming.shape
    experts = router.shape[0]
    tokens_out[0:tokens, :] = upcoming[...]
    gains = gain[...]
    scaled = router[...] * gains
    rows = [p.astype(jnp.float32) for p in three_parts(scaled)]
    rows += [p.astype(jnp.float32) for p in three_parts(gains)]
    rows.append(jnp.zeros((TABLE - 3 * experts - 3, part), jnp.float32))
    tokens_out[tokens : tokens + TABLE, :] = jnp.concatenate(rows, axis=0).astype(jnp.bfloat16)


def with_table(upcoming, gain, router):
    tokens, part = upcoming.shape
    shape = (tokens + TABLE, part)
    return pl.pallas_call(
        table_kernel,
        out_shape=jax.ShapeDtypeStruct(shape, jnp.bfloat16),
        grid=(1,),
        in_specs=[whole(a.shape) for a in (upcoming, gain, router)],
        out_specs=whole(shape),
        compiler_params=pltpu.CompilerParams(vmem_limit_bytes=MOST),
    )(upcoming, gain, router)


def pack_kernel(experts, capacity, routes_s, routes_n, saved, cot, packed, sel_s, one_n, two_n):
    tokens, part = saved.shape
    row = lax.broadcasted_iota(jnp.int32, (tokens, tokens), 0)
    lane = lax.broadcasted_iota(jnp.int32, (tokens, tokens), 1)
    earlier = jnp.where(lane < row, 1.0, 0.0).astype(jnp.bfloat16)
    wide = lax.broadcasted_iota(jnp.int32, (tokens, 128), 1)
    slots = lax.broadcasted_iota(jnp.int32, (tokens, experts * capacity), 1)

    def select(routes):
        ids = routes[...]
        one, two = ids[:, 0:1], ids[:, 1:2]
        hit_one = jnp.where(wide == one, 1.0, 0.0)
        hit_two = jnp.where(wide == two, 1.0, 0.0)
        counts = product(earlier, (hit_one + hit_two).astype(jnp.bfloat16), INNER)
        rank_one = jnp.sum(counts * hit_one, axis=1, keepdims=True).astype(jnp.int32)
        rank_two = jnp.sum(counts * hit_two, axis=1, keepdims=True).astype(jnp.int32)
        first = jnp.where(slots == one * capacity + rank_one, 1.0, 0.0)
        second = jnp.where(slots == two * capacity + rank_two, 1.0, 0.0)
        return one, two, first.astype(jnp.bfloat16), second.astype(jnp.bfloat16)

    def put(start, lanes, width, value):
        packed[:, start : start + capacity, lanes : lanes + width] = value.reshape(
            experts, capacity, width
        )

    one, two, first, second = select(routes_s)
    inside = wide < 3 * experts
    wide_one = jnp.where(inside & (lax.rem(wide, experts) == one), 1.0, 0.0).astype(jnp.bfloat16)
    wide_two = jnp.where(inside & (lax.rem(wide, experts) == two), 1.0, 0.0).astype(jnp.bfloat16)
    both = first + second
    sel_s[...] = both
    put(0, 0, part, product(both, saved[...], LEADING).astype(jnp.bfloat16))
    put(capacity, 0, part, product(both, cot[...], LEADING).astype(jnp.bfloat16))
    other = product(first, wide_two, LEADING) + product(second, wide_one, LEADING)
    put(0, part, 128, other.astype(jnp.bfloat16))
    put(capacity, part, 128, jnp.zeros(other.shape, jnp.bfloat16))
    _, _, first, second = select(routes_n)
    one_n[...] = first
    two_n[...] = second


def pack(routes_s, routes_n, saved, cot, experts, capacity):
    tokens, part = saved.shape
    total = experts * capacity
    shapes = [(experts, 2 * capacity, part + 128)] + [(tokens, total)] * 3
    return pl.pallas_call(
        functools.partial(pack_kernel, experts, capacity),
        out_shape=[jax.ShapeDtypeStruct(s, jnp.bfloat16) for s in shapes],
        grid=(1,),
        in_specs=[whole(a.shape) for a in (routes_s, routes_n, saved, cot)],
        out_specs=[whole(s) for s in shapes],
        compiler_params=pltpu.CompilerParams(vmem_limit_bytes=MOST),
    )(routes_s, routes_n, saved, cot)


def spread_kernel(routes, one_n, two_n, *refs):
    pieces, (moved, table, ones, twos) = refs[:GROUPS], refs[GROUPS:]
    tokens = one_n.shape[0]
    blocks, _, capacity, part = moved.shape
    total = jnp.zeros((tokens, 128), jnp.float32)
    logits = jnp.zeros((tokens, TABLE), jnp.float32)
    for group, piece in enumerate(pieces):
        table[group] = piece[tokens : tokens + TABLE, :]
        values = piece[0:tokens, :].astype(jnp.float32)
        total = total + lanes(values * values)
        logits = logits + product(piece[0:tokens, :], piece[tokens : tokens + TABLE, :], CONTRACT)
    scale = lax.rsqrt(even(total) / (GROUPS * part) + EPSILON)
    ids = routes[...]
    place = lax.broadcasted_iota(jnp.int32, (tokens, TABLE), 1)
    first = jnp.where((place < 24) & (lax.rem(place, 8) == ids[:, 0:1]), 1.0, 0.0)
    second = jnp.where((place < 24) & (lax.rem(place, 8) == ids[:, 1:2]), 1.0, 0.0)
    diff = even(logits * (first - second)) * scale
    ones[...] = jax.nn.sigmoid(diff)
    twos[...] = jax.nn.sigmoid(-diff)
    both = one_n[...] + two_n[...]
    for group, piece in enumerate(pieces):
        values = piece[0:tokens, :].astype(jnp.float32)
        normed = (values * widen(scale, part) * gains_of(table, group)).astype(jnp.bfloat16)
        rows = product(both, normed, LEADING).astype(jnp.bfloat16)
        moved[:, group] = rows.reshape(blocks, capacity, part)


def spread(routes, one_n, two_n, pieces, blocks):
    part = pieces[0].shape[1]
    tokens, total = one_n.shape
    return pl.pallas_call(
        spread_kernel,
        out_shape=(
            jax.ShapeDtypeStruct((blocks, GROUPS, total // blocks, part), jnp.bfloat16),
            jax.ShapeDtypeStruct((GROUPS, TABLE, part), jnp.bfloat16),
            jax.ShapeDtypeStruct((tokens, 128), jnp.float32),
            jax.ShapeDtypeStruct((tokens, 128), jnp.float32),
        ),
        in_specs=[VMEM] * (3 + GROUPS),
        out_specs=(VMEM,) * 4,
        compiler_params=pltpu.CompilerParams(vmem_limit_bytes=LIMIT // 2),
    )(routes, one_n, two_n, *pieces)


def widen(value, width):
    return jnp.concatenate([value] * (width // 128), axis=1)


def lanes(value):
    total = value[:, 0:128]
    for start in range(128, value.shape[1], 128):
        total = total + value[:, start : start + 128]
    return total


def even(value):
    return jnp.broadcast_to(jnp.sum(value, axis=1, keepdims=True), (value.shape[0], 128))


def gains_of(table, group):
    rows = table[group, 24:32, :].astype(jnp.float32)
    return rows[0:1] + (rows[1:2] + rows[2:3])


def fetch_rows(order, source, target, sems, part):
    copies = []
    for group in range(GROUPS):
        start = pl.multiple_of(order[group] * part, part)
        copies.append(
            pltpu.make_async_copy(
                source.at[pl.ds(start, part), :],
                target.at[pl.ds(group * part, part), :],
                sems.at[group],
            )
        )
    return copies


def fetch_columns(order, source, target, sems, part):
    copies = []
    for group in range(GROUPS):
        start = group * part
        if order is not None:
            start = pl.multiple_of(order[group] * part, part)
        copies.append(
            pltpu.make_async_copy(
                source.at[:, pl.ds(start, part)],
                target.at[:, pl.ds(group * part, part)],
                sems.at[group],
            )
        )
    return copies


def start(copies):
    for copy in copies:
        copy.start()


def wait(copies):
    for copy in copies:
        copy.wait()


def prepare(own, other_start, take, other, table, normed, scales, diffs, logits, width, between):
    blocks = other.shape[0]
    part = width // GROUPS
    for group in range(GROUPS):
        rows = jnp.concatenate([take(group, block) for block in range(blocks)], axis=0)
        found = product(rows, table[group], CONTRACT)
        if group == 0:
            logits[...] = found
        else:
            logits[...] += found
    start(between)

    @pl.loop(0, blocks)
    def _(block):
        at = pl.ds(pl.multiple_of(block * STEP, STEP), STEP)
        total = jnp.zeros((STEP, 128), jnp.float32)
        for group in range(GROUPS):
            values = take(group, block).astype(jnp.float32)
            total = total + lanes(values * values)
        scale = lax.rsqrt(even(total) / width + EPSILON)
        scales[at, :] = scale
        place = lax.broadcasted_iota(jnp.int32, (STEP, TABLE), 1)
        ours = jnp.where((place < 24) & (lax.rem(place, 8) == own), 1.0, 0.0)
        theirs = other[block, other_start : other_start + STEP, 0:TABLE].astype(jnp.float32)
        diffs[at, :] = even(logits[at, :] * (ours - theirs)) * scale
        for group in range(GROUPS):
            values = take(group, block).astype(jnp.float32)
            normed[at, group * part : (group + 1) * part] = (
                values * widen(scale, part) * gains_of(table, group)
            ).astype(jnp.bfloat16)


def hand_out(group, place, source, target, sems):
    return pltpu.make_async_copy(
        source.at[:, group : group + 1], target.at[:, pl.ds(place, 1)], sems.at[group]
    )


def forward_kernel(
    order, moved, gate_w, up_w, down_w, out_to,
    rows, out, gate_b, up_b, down_b, gate, up, hidden, sem_m, sem_o, sem_g, sem_u, sem_d
):
    blocks, _, capacity, part = moved.shape
    total, width = blocks * capacity, GROUPS * part
    arrive = [
        pltpu.make_async_copy(
            moved.at[:, group], rows.at[:, :, pl.ds(group * part, part)], sem_m.at[group]
        )
        for group in range(GROUPS)
    ]
    copies = fetch_rows(order, gate_w, gate_b, sem_g, part)
    copies_up = fetch_rows(order, up_w, up_b, sem_u, part)
    copies_down = fetch_columns(None, down_w, down_b, sem_d, part)
    start(arrive)
    start(copies)
    wait(arrive)
    start(copies_up)
    wait(copies)
    start(copies_down)
    gate[...] = product(rows[...].reshape(total, width), gate_b[...], INNER)
    wait(copies_up)
    up[...] = product(rows[...].reshape(total, width), up_b[...], INNER)

    @pl.loop(0, blocks)
    def _(block):
        at = pl.ds(pl.multiple_of(block * STEP, STEP), STEP)
        value = gate[at, :]
        hidden[at, :] = (value * jax.nn.sigmoid(value) * up[at, :]).astype(jnp.bfloat16)

    for group in range(GROUPS):
        copies_down[group].wait()
        part_out = product(hidden[...], down_b[:, group * part : (group + 1) * part], INNER)
        out[:, group] = part_out.astype(jnp.bfloat16).reshape(blocks, capacity, part)
        hand_out(group, group, out, out_to, sem_o).start()
    for group in range(GROUPS):
        hand_out(group, group, out, out_to, sem_o).wait()


def weight_scratch(width, units):
    return [
        pltpu.VMEM((width, units), jnp.bfloat16),
        pltpu.VMEM((width, units), jnp.bfloat16),
        pltpu.VMEM((units, width), jnp.bfloat16),
    ]


def forward(order, moved, gate_w, up_w, down_w):
    blocks, _, capacity, part = moved.shape
    width, units = gate_w.shape
    total = blocks * capacity
    return pl.pallas_call(
        forward_kernel,
        out_shape=jax.ShapeDtypeStruct(moved.shape, jnp.bfloat16),
        in_specs=[SMEM] + [PLACE] * 4,
        out_specs=PLACE,
        scratch_shapes=[
            pltpu.VMEM((blocks, capacity, width), jnp.bfloat16),
            pltpu.VMEM(moved.shape, jnp.bfloat16),
        ]
        + weight_scratch(width, units)
        + [
            pltpu.VMEM((total, units), jnp.float32),
            pltpu.VMEM((total, units), jnp.float32),
            pltpu.VMEM((total, units), jnp.bfloat16),
        ]
        + [pltpu.SemaphoreType.DMA((GROUPS,))] * 5,
        compiler_params=pltpu.CompilerParams(vmem_limit_bytes=LIMIT),
        cost_estimate=pl.CostEstimate(
            flops=6 * total * width * units,
            bytes_accessed=6 * width * units + 4 * total * width,
            transcendentals=total * units,
        ),
    )(order, moved, gate_w, up_w, down_w)


def backward_kernel(*refs):
    order, own, other, table, gate_w, up_w, down_w = refs[:7]
    pieces_in = refs[7 : 7 + GROUPS]
    out_to, pieces = refs[7 + GROUPS], refs[8 + GROUPS : 8 + 2 * GROUPS]
    (
        out, gate_b, up_b, down_b, normed, cots, gate, up, grad, grad_gate, grad_up,
        scales, diffs, ones, twos, logits, sem_m, sem_o, sem_g, sem_u, sem_d,
    ) = refs[8 + 2 * GROUPS :]
    blocks, _, capacity, part = out.shape
    width = GROUPS * part
    arrive = [
        pltpu.make_async_copy(pieces_in[group], pieces[group], sem_m.at[group])
        for group in range(GROUPS)
    ]
    start(arrive)
    copies = fetch_rows(order, gate_w, gate_b, sem_g, part)
    copies_up = fetch_rows(order, up_w, up_b, sem_u, part)
    copies_down = fetch_columns(order, down_w, down_b, sem_d, part)
    start(copies)
    wait(arrive)

    def take(group, block):
        return pieces[group][block, 0:STEP, :]

    prepare(own[0], 0, take, other, table, normed, scales, diffs, logits, width, copies_up)

    @pl.loop(0, blocks)
    def _(block):
        at = pl.ds(pl.multiple_of(block * STEP, STEP), STEP)
        for group in range(GROUPS):
            cots[at, group * part : (group + 1) * part] = pieces[group][block, STEP : 2 * STEP, :]

    wait(copies)
    start(copies_down)
    gate[...] = product(normed[...], gate_b[...], INNER)
    wait(copies_up)
    up[...] = product(normed[...], up_b[...], INNER)
    wait(copies_down)
    grad[...] = product(cots[...], down_b[...], CONTRACT)

    @pl.loop(0, blocks)
    def _(block):
        at = pl.ds(pl.multiple_of(block * STEP, STEP), STEP)
        slope, value, lift = grad[at, :], gate[at, :], up[at, :]
        sig = jax.nn.sigmoid(value)
        silu = value * sig
        hidden = (silu * lift).astype(jnp.bfloat16).astype(jnp.float32)
        to_gate = (slope * lift * (sig * (1.0 + value * (1.0 - sig)))).astype(jnp.bfloat16)
        to_up = (slope * silu).astype(jnp.bfloat16)
        grad_gate[at, :] = to_gate
        grad_up[at, :] = to_up
        row_dot = even(lanes(slope * hidden))
        norm_dot = even(
            lanes(to_gate.astype(jnp.float32) * value + to_up.astype(jnp.float32) * lift)
        )
        scale, diff = scales[at, :], diffs[at, :]
        ours, theirs = jax.nn.sigmoid(diff), jax.nn.sigmoid(-diff)
        through = ours * theirs * row_dot
        ones[at, :] = scale * through
        twos[at, :] = scale * scale * ((ours * norm_dot + through * diff) / width)
        diffs[at, :] = scale * ours

    place = lax.broadcasted_iota(jnp.int32, (blocks * STEP, TABLE), 1)
    away = jnp.where((place < 24) & (lax.rem(place, 8) == own[0]), 1.0, 0.0)
    away = away - jnp.concatenate(
        [other[block, 0:STEP, 0:TABLE].astype(jnp.float32) for block in range(blocks)], axis=0
    )
    away = away.astype(jnp.bfloat16)
    for group in range(GROUPS):
        at = slice(group * part, (group + 1) * part)
        rows = product(grad_gate[...], gate_b[at, :], CONTRACT)
        rows = rows + product(grad_up[...], up_b[at, :], CONTRACT)
        turn = product(away, table[group], INNER)
        values = jnp.concatenate([take(group, block) for block in range(blocks)], axis=0)
        rows = (
            rows * (widen(diffs[...], part) * gains_of(table, group))
            + turn * widen(ones[...], part)
            - values.astype(jnp.float32) * widen(twos[...], part)
        )
        out[:, group] = rows.astype(jnp.bfloat16).reshape(blocks, capacity, part)
        hand_out(group, order[group], out, out_to, sem_o).start()
    for group in range(GROUPS):
        hand_out(group, order[group], out, out_to, sem_o).wait()


def backward(order, own, other, table, gate_w, up_w, down_w, pieces):
    blocks, double, part = pieces[0].shape
    capacity = double // 2
    width, units = gate_w.shape
    total = blocks * capacity
    small = pltpu.VMEM((total, 128), jnp.float32)
    return pl.pallas_call(
        backward_kernel,
        out_shape=jax.ShapeDtypeStruct((blocks, GROUPS, capacity, part), jnp.bfloat16),
        in_specs=[SMEM, SMEM, VMEM, VMEM, PLACE, PLACE, PLACE] + [PLACE] * GROUPS,
        out_specs=PLACE,
        scratch_shapes=[pltpu.VMEM((blocks, double, part), jnp.bfloat16)] * GROUPS
        + [pltpu.VMEM((blocks, GROUPS, capacity, part), jnp.bfloat16)]
        + weight_scratch(width, units)
        + [
            pltpu.VMEM((total, width), jnp.bfloat16),
            pltpu.VMEM((total, width), jnp.bfloat16),
            pltpu.VMEM((total, units), jnp.float32),
            pltpu.VMEM((total, units), jnp.float32),
            pltpu.VMEM((total, units), jnp.float32),
            pltpu.VMEM((total, units), jnp.bfloat16),
            pltpu.VMEM((total, units), jnp.bfloat16),
            small,
            small,
            small,
            small,
            pltpu.VMEM((total, TABLE), jnp.float32),
        ]
        + [pltpu.SemaphoreType.DMA((GROUPS,))] * 5,
        compiler_params=pltpu.CompilerParams(vmem_limit_bytes=LIMIT),
        cost_estimate=pl.CostEstimate(
            flops=10 * total * width * units,
            bytes_accessed=6 * width * units + 6 * total * width,
            transcendentals=total * units,
        ),
    )(order, own, other, table, gate_w, up_w, down_w, *pieces)


def finish_kernel(sel, home, base, out):
    blocks, groups, capacity, part = home.shape
    total = base[...].astype(jnp.float32)
    for group in range(groups):
        total = total + product(sel[...], home[:, group].reshape(blocks * capacity, part), INNER)
    out[...] = total.astype(jnp.bfloat16)


def finish(sel, home, base):
    return pl.pallas_call(
        finish_kernel,
        out_shape=jax.ShapeDtypeStruct(base.shape, jnp.bfloat16),
        in_specs=[VMEM] * 3,
        out_specs=VMEM,
        compiler_params=pltpu.CompilerParams(vmem_limit_bytes=LIMIT // 2),
    )(sel, home, base)


def finish_weighted_kernel(one_n, two_n, ones, twos, home, base, out):
    blocks, groups, capacity, part = home.shape
    first = jnp.zeros(base.shape, jnp.float32)
    second = jnp.zeros(base.shape, jnp.float32)
    for group in range(groups):
        rows = home[:, group].reshape(blocks * capacity, part)
        first = first + product(one_n[...], rows, INNER)
        second = second + product(two_n[...], rows, INNER)
    total = base[...].astype(jnp.float32) + first * widen(ones[...], part)
    out[...] = (total + second * widen(twos[...], part)).astype(jnp.bfloat16)


def finish_weighted(one_n, two_n, ones, twos, home, base):
    return pl.pallas_call(
        finish_weighted_kernel,
        out_shape=jax.ShapeDtypeStruct(base.shape, jnp.bfloat16),
        in_specs=[VMEM] * 6,
        out_specs=VMEM,
        compiler_params=pltpu.CompilerParams(vmem_limit_bytes=LIMIT // 2),
    )(one_n, two_n, ones, twos, home, base)


def send_home(pieces):
    experts, hids, capacity, part = pieces.shape
    home = swap(pieces.reshape(experts * hids, capacity, part), BOTH)
    return home.reshape(experts, hids, capacity, part)


def per_device(
    saved_input,
    cotangent,
    next_input,
    routes_saved,
    routes_next,
    norm_gain,
    router,
    expert_gate,
    expert_up,
    expert_down,
):
    gate_w, up_w, down_w = expert_gate[0, 0], expert_up[0, 0], expert_down[0, 0]
    tokens, part = saved_input.shape[1:]
    experts = lax.axis_size("expert")
    capacity = 3 * tokens // experts
    own = lax.axis_index("expert").astype(jnp.int32).reshape(1)
    order = arrival_order()

    tokens_next = with_table(next_input[0], norm_gain, router[0].T)
    tokens_next, routes = lax.optimization_barrier((tokens_next, (routes_saved[0], routes_next[0])))
    packed, sel_saved, one_next, two_next = pack(
        *routes, saved_input[0], cotangent[0], experts, capacity
    )
    near, packed = gather_near(tokens_next, packed)
    packed = swap(packed, "expert")
    moved_next, table, ones, twos = spread(
        routes[1], one_next, two_next, near + gather_far(near), experts
    )
    moved_next = swap(moved_next, "expert")
    other = packed[:, :, part:]
    near, _ = gather_near(packed[:, :, :part])
    near, moved_next = lax.optimization_barrier((near, moved_next))
    far = gather_far(near)
    out_next = forward(order, moved_next, gate_w, up_w, down_w)
    far, out_next = lax.optimization_barrier((far, out_next))
    pieces = near + far
    out_home = send_home(out_next)
    back_part = backward(order, own, other, table, gate_w, up_w, down_w, pieces)
    back_part, out_home = lax.optimization_barrier((back_part, out_home))
    back_home = send_home(back_part)

    forward_out = finish_weighted(one_next, two_next, ones, twos, out_home, next_input[0])
    grad_input = finish(sel_saved, back_home, cotangent[0])

    first_section = lax.axis_index("section") == 0
    outgoing = jnp.where(first_section, forward_out, grad_input)
    leaving = jnp.where(first_section, grad_input, forward_out)
    arriving = partner(outgoing, "section", 0)
    return (leaving[None], arriving[None])


def solution(mesh):
    placed = (
        P("section", "expert", "hid"),
        P("section", "expert", "hid"),
        P("section", "expert", "hid"),
        P("section", "expert", None),
        P("section", "expert", None),
        P("section", "hid"),
        P("section", "hid", None),
        P("section", "expert", None, "hid"),
        P("section", "expert", None, "hid"),
        P("section", "expert", "hid", None),
    )
    return jax.shard_map(
        per_device,
        mesh=mesh,
        in_specs=placed,
        out_specs=(P("section", "expert", "hid"), P("section", "expert", "hid")),
        check_vma=False,
    )
```

```python
import functools

import jax
import jax.numpy as jnp
from jax import lax
from jax.experimental import pallas as pl
from jax.experimental.pallas import tpu as pltpu
from jax.sharding import PartitionSpec as P

EPSILON = 1e-05
INNER = (((1,), (0,)), ((), ()))
CONTRACT = (((1,), (1,)), ((), ()))
LEADING = (((0,), (0,)), ((), ()))
BOTH = ("expert", "hid")
STEP = 48
GROUPS = 8
TABLE = 32
LIMIT = 56 * 1024 * 1024
MOST = 60 * 1024 * 1024
VMEM = pl.BlockSpec(memory_space=pltpu.VMEM)
SMEM = pl.BlockSpec(memory_space=pltpu.SMEM)
PLACE = pl.BlockSpec(memory_space=pl.ANY)


def product(left, right, dims):
    return lax.dot_general(left, right, dims, preferred_element_type=jnp.float32)


def partner(block, axis, bit):
    count = lax.axis_size(axis)
    route = []
    for low in range(count):
        high = low | 1 << bit
        if high != low and high < count:
            route += [(low, high), (high, low)]
    return lax.ppermute(block, axis, route)


def swap(block, axes):
    return lax.all_to_all(block, axes, split_axis=0, concat_axis=0, tiled=True)


def shift(block, along, across):
    count = lax.axis_size("hid")
    route = []
    for source in range(count):
        x, y = source // 2, source % 2
        route.append((source, (x + along) % (count // 2) * 2 + (y ^ across)))
    return lax.ppermute(block, "hid", route)


def gather_near(block, after=()):
    other = shift(block, 0, 1)
    right, left = shift(block, 1, 0), shift(block, -1, 0)
    other, right, left, after = lax.optimization_barrier((other, right, left, after))
    right_other, left_other = shift(other, 1, 0), shift(other, -1, 0)
    return [block, other, right, right_other, left, left_other], after


def gather_far(near):
    return [shift(near[2], 1, 0), shift(near[5], -1, 0)]


def arrival_order():
    own = lax.axis_index("hid")
    half = lax.axis_size("hid") // 2
    x, y = own // 2, own % 2
    places = []
    for along in (0, -1, 1, 2):
        row = (x + along + half) % half * 2
        places += [row + y, row + 1 - y]
    return jnp.stack(places).astype(jnp.int32)


def three_parts(value):
    high = value.astype(jnp.bfloat16)
    rest = value - high.astype(jnp.float32)
    middle = rest.astype(jnp.bfloat16)
    low = (rest - middle.astype(jnp.float32)).astype(jnp.bfloat16)
    return high, middle, low


def whole(shape):
    return pl.BlockSpec(shape, lambda i: (0,) * len(shape))


def table_kernel(upcoming, gain, router, tokens_out):
    tokens, part = upcoming.shape
    experts = router.shape[0]
    tokens_out[0:tokens, :] = upcoming[...]
    gains = gain[...]
    scaled = router[...] * gains
    rows = [p.astype(jnp.float32) for p in three_parts(scaled)]
    rows += [p.astype(jnp.float32) for p in three_parts(gains)]
    rows.append(jnp.zeros((TABLE - 3 * experts - 3, part), jnp.float32))
    tokens_out[tokens : tokens + TABLE, :] = jnp.concatenate(rows, axis=0).astype(jnp.bfloat16)


def with_table(upcoming, gain, router):
    tokens, part = upcoming.shape
    shape = (tokens + TABLE, part)
    return pl.pallas_call(
        table_kernel,
        out_shape=jax.ShapeDtypeStruct(shape, jnp.bfloat16),
        grid=(1,),
        in_specs=[whole(a.shape) for a in (upcoming, gain, router)],
        out_specs=whole(shape),
        compiler_params=pltpu.CompilerParams(vmem_limit_bytes=MOST),
    )(upcoming, gain, router)


def pack_kernel(experts, capacity, routes_s, routes_n, saved, cot, packed, sel_s, one_n, two_n):
    tokens, part = saved.shape
    row = lax.broadcasted_iota(jnp.int32, (tokens, tokens), 0)
    lane = lax.broadcasted_iota(jnp.int32, (tokens, tokens), 1)
    earlier = jnp.where(lane < row, 1.0, 0.0).astype(jnp.bfloat16)
    wide = lax.broadcasted_iota(jnp.int32, (tokens, 128), 1)
    slots = lax.broadcasted_iota(jnp.int32, (tokens, experts * capacity), 1)

    def select(routes):
        ids = routes[...]
        one, two = ids[:, 0:1], ids[:, 1:2]
        hit_one = jnp.where(wide == one, 1.0, 0.0)
        hit_two = jnp.where(wide == two, 1.0, 0.0)
        counts = product(earlier, (hit_one + hit_two).astype(jnp.bfloat16), INNER)
        rank_one = jnp.sum(counts * hit_one, axis=1, keepdims=True).astype(jnp.int32)
        rank_two = jnp.sum(counts * hit_two, axis=1, keepdims=True).astype(jnp.int32)
        first = jnp.where(slots == one * capacity + rank_one, 1.0, 0.0)
        second = jnp.where(slots == two * capacity + rank_two, 1.0, 0.0)
        return one, two, first.astype(jnp.bfloat16), second.astype(jnp.bfloat16)

    def put(start, lanes, width, value):
        packed[:, start : start + capacity, lanes : lanes + width] = value.reshape(
            experts, capacity, width
        )

    one, two, first, second = select(routes_s)
    inside = wide < 3 * experts
    wide_one = jnp.where(inside & (lax.rem(wide, experts) == one), 1.0, 0.0).astype(jnp.bfloat16)
    wide_two = jnp.where(inside & (lax.rem(wide, experts) == two), 1.0, 0.0).astype(jnp.bfloat16)
    both = first + second
    sel_s[...] = both
    put(0, 0, part, product(both, saved[...], LEADING).astype(jnp.bfloat16))
    put(capacity, 0, part, product(both, cot[...], LEADING).astype(jnp.bfloat16))
    other = product(first, wide_two, LEADING) + product(second, wide_one, LEADING)
    put(0, part, 128, other.astype(jnp.bfloat16))
    put(capacity, part, 128, jnp.zeros(other.shape, jnp.bfloat16))
    _, _, first, second = select(routes_n)
    one_n[...] = first
    two_n[...] = second


def pack(routes_s, routes_n, saved, cot, experts, capacity):
    tokens, part = saved.shape
    total = experts * capacity
    shapes = [(experts, 2 * capacity, part + 128)] + [(tokens, total)] * 3
    return pl.pallas_call(
        functools.partial(pack_kernel, experts, capacity),
        out_shape=[jax.ShapeDtypeStruct(s, jnp.bfloat16) for s in shapes],
        grid=(1,),
        in_specs=[whole(a.shape) for a in (routes_s, routes_n, saved, cot)],
        out_specs=[whole(s) for s in shapes],
        compiler_params=pltpu.CompilerParams(vmem_limit_bytes=MOST),
    )(routes_s, routes_n, saved, cot)


def spread_kernel(routes, one_n, two_n, *refs):
    pieces, (moved, table, ones, twos) = refs[:GROUPS], refs[GROUPS:]
    tokens = one_n.shape[0]
    blocks, _, capacity, part = moved.shape
    total = jnp.zeros((tokens, 128), jnp.float32)
    logits = jnp.zeros((tokens, TABLE), jnp.float32)
    for group, piece in enumerate(pieces):
        table[group] = piece[tokens : tokens + TABLE, :]
        values = piece[0:tokens, :].astype(jnp.float32)
        total = total + lanes(values * values)
        logits = logits + product(piece[0:tokens, :], piece[tokens : tokens + TABLE, :], CONTRACT)
    scale = lax.rsqrt(even(total) / (GROUPS * part) + EPSILON)
    ids = routes[...]
    place = lax.broadcasted_iota(jnp.int32, (tokens, TABLE), 1)
    first = jnp.where((place < 24) & (lax.rem(place, 8) == ids[:, 0:1]), 1.0, 0.0)
    second = jnp.where((place < 24) & (lax.rem(place, 8) == ids[:, 1:2]), 1.0, 0.0)
    diff = even(logits * (first - second)) * scale
    ones[...] = jax.nn.sigmoid(diff)
    twos[...] = jax.nn.sigmoid(-diff)
    both = one_n[...] + two_n[...]
    for group, piece in enumerate(pieces):
        values = piece[0:tokens, :].astype(jnp.float32)
        normed = (values * widen(scale, part) * gains_of(table, group)).astype(jnp.bfloat16)
        rows = product(both, normed, LEADING).astype(jnp.bfloat16)
        moved[:, group] = rows.reshape(blocks, capacity, part)


def spread(routes, one_n, two_n, pieces, blocks):
    part = pieces[0].shape[1]
    tokens, total = one_n.shape
    return pl.pallas_call(
        spread_kernel,
        out_shape=(
            jax.ShapeDtypeStruct((blocks, GROUPS, total // blocks, part), jnp.bfloat16),
            jax.ShapeDtypeStruct((GROUPS, TABLE, part), jnp.bfloat16),
            jax.ShapeDtypeStruct((tokens, 128), jnp.float32),
            jax.ShapeDtypeStruct((tokens, 128), jnp.float32),
        ),
        grid=(1,),
        in_specs=[whole(a.shape) for a in (routes, one_n, two_n)] + [VMEM] * GROUPS,
        out_specs=(
            whole((blocks, GROUPS, total // blocks, part)),
            whole((GROUPS, TABLE, part)),
            whole((tokens, 128)),
            whole((tokens, 128)),
        ),
        compiler_params=pltpu.CompilerParams(vmem_limit_bytes=MOST),
    )(routes, one_n, two_n, *pieces)


def widen(value, width):
    return jnp.concatenate([value] * (width // 128), axis=1)


def lanes(value):
    total = value[:, 0:128]
    for start in range(128, value.shape[1], 128):
        total = total + value[:, start : start + 128]
    return total


def even(value):
    return jnp.broadcast_to(jnp.sum(value, axis=1, keepdims=True), (value.shape[0], 128))


def gains_of(table, group):
    rows = table[group, 24:32, :].astype(jnp.float32)
    return rows[0:1] + (rows[1:2] + rows[2:3])


def fetch_rows(order, source, target, sems, part):
    copies = []
    for group in range(GROUPS):
        start = pl.multiple_of(order[group] * part, part)
        copies.append(
            pltpu.make_async_copy(
                source.at[pl.ds(start, part), :],
                target.at[pl.ds(group * part, part), :],
                sems.at[group],
            )
        )
    return copies


def fetch_columns(order, source, target, sems, part):
    copies = []
    for group in range(GROUPS):
        start = group * part
        if order is not None:
            start = pl.multiple_of(order[group] * part, part)
        copies.append(
            pltpu.make_async_copy(
                source.at[:, pl.ds(start, part)],
                target.at[:, pl.ds(group * part, part)],
                sems.at[group],
            )
        )
    return copies


def start(copies):
    for copy in copies:
        copy.start()


def wait(copies):
    for copy in copies:
        copy.wait()


def prepare(own, other_start, take, other, table, normed, scales, diffs, logits, width, between):
    blocks = other.shape[0]
    part = width // GROUPS
    for group in range(GROUPS):
        rows = jnp.concatenate([take(group, block) for block in range(blocks)], axis=0)
        found = product(rows, table[group], CONTRACT)
        if group == 0:
            logits[...] = found
        else:
            logits[...] += found
    start(between)

    @pl.loop(0, blocks)
    def _(block):
        at = pl.ds(pl.multiple_of(block * STEP, STEP), STEP)
        total = jnp.zeros((STEP, 128), jnp.float32)
        for group in range(GROUPS):
            values = take(group, block).astype(jnp.float32)
            total = total + lanes(values * values)
        scale = lax.rsqrt(even(total) / width + EPSILON)
        scales[at, :] = scale
        place = lax.broadcasted_iota(jnp.int32, (STEP, TABLE), 1)
        ours = jnp.where((place < 24) & (lax.rem(place, 8) == own), 1.0, 0.0)
        theirs = other[block, other_start : other_start + STEP, 0:TABLE].astype(jnp.float32)
        diffs[at, :] = even(logits[at, :] * (ours - theirs)) * scale
        for group in range(GROUPS):
            values = take(group, block).astype(jnp.float32)
            normed[at, group * part : (group + 1) * part] = (
                values * widen(scale, part) * gains_of(table, group)
            ).astype(jnp.bfloat16)


def hand_out(group, place, source, target, sems):
    return pltpu.make_async_copy(
        source.at[:, group : group + 1], target.at[:, pl.ds(place, 1)], sems.at[group]
    )


def forward_kernel(
    order, moved, gate_w, up_w, down_w, out_to,
    rows, out, gate_b, up_b, down_b, gate, up, hidden, sem_m, sem_o, sem_g, sem_u, sem_d
):
    blocks, _, capacity, part = moved.shape
    total, width = blocks * capacity, GROUPS * part
    arrive = [
        pltpu.make_async_copy(
            moved.at[:, group], rows.at[:, :, pl.ds(group * part, part)], sem_m.at[group]
        )
        for group in range(GROUPS)
    ]
    copies = fetch_rows(order, gate_w, gate_b, sem_g, part)
    copies_up = fetch_rows(order, up_w, up_b, sem_u, part)
    copies_down = fetch_columns(None, down_w, down_b, sem_d, part)
    start(arrive)
    start(copies)
    wait(arrive)
    start(copies_up)
    wait(copies)
    start(copies_down)
    gate[...] = product(rows[...].reshape(total, width), gate_b[...], INNER)
    wait(copies_up)
    up[...] = product(rows[...].reshape(total, width), up_b[...], INNER)

    @pl.loop(0, blocks)
    def _(block):
        at = pl.ds(pl.multiple_of(block * STEP, STEP), STEP)
        value = gate[at, :]
        hidden[at, :] = (value * jax.nn.sigmoid(value) * up[at, :]).astype(jnp.bfloat16)

    for group in range(GROUPS):
        copies_down[group].wait()
        part_out = product(hidden[...], down_b[:, group * part : (group + 1) * part], INNER)
        out[:, group] = part_out.astype(jnp.bfloat16).reshape(blocks, capacity, part)
        hand_out(group, group, out, out_to, sem_o).start()
    for group in range(GROUPS):
        hand_out(group, group, out, out_to, sem_o).wait()


def weight_scratch(width, units):
    return [
        pltpu.VMEM((width, units), jnp.bfloat16),
        pltpu.VMEM((width, units), jnp.bfloat16),
        pltpu.VMEM((units, width), jnp.bfloat16),
    ]


def forward(order, moved, gate_w, up_w, down_w):
    blocks, _, capacity, part = moved.shape
    width, units = gate_w.shape
    total = blocks * capacity
    return pl.pallas_call(
        forward_kernel,
        out_shape=jax.ShapeDtypeStruct(moved.shape, jnp.bfloat16),
        in_specs=[SMEM] + [PLACE] * 4,
        out_specs=PLACE,
        scratch_shapes=[
            pltpu.VMEM((blocks, capacity, width), jnp.bfloat16),
            pltpu.VMEM(moved.shape, jnp.bfloat16),
        ]
        + weight_scratch(width, units)
        + [
            pltpu.VMEM((total, units), jnp.float32),
            pltpu.VMEM((total, units), jnp.float32),
            pltpu.VMEM((total, units), jnp.bfloat16),
        ]
        + [pltpu.SemaphoreType.DMA((GROUPS,))] * 5,
        compiler_params=pltpu.CompilerParams(vmem_limit_bytes=LIMIT),
        cost_estimate=pl.CostEstimate(
            flops=6 * total * width * units,
            bytes_accessed=6 * width * units + 4 * total * width,
            transcendentals=total * units,
        ),
    )(order, moved, gate_w, up_w, down_w)


def backward_kernel(*refs):
    order, own, other, table, gate_w, up_w, down_w = refs[:7]
    pieces_in = refs[7 : 7 + GROUPS]
    out_to, pieces = refs[7 + GROUPS], refs[8 + GROUPS : 8 + 2 * GROUPS]
    (
        out, gate_b, up_b, down_b, normed, cots, gate, up, grad, grad_gate, grad_up,
        scales, diffs, ones, twos, logits, sem_m, sem_o, sem_g, sem_u, sem_d,
    ) = refs[8 + 2 * GROUPS :]
    blocks, _, capacity, part = out.shape
    width = GROUPS * part
    arrive = [
        pltpu.make_async_copy(pieces_in[group], pieces[group], sem_m.at[group])
        for group in range(GROUPS)
    ]
    start(arrive)
    copies = fetch_rows(order, gate_w, gate_b, sem_g, part)
    copies_up = fetch_rows(order, up_w, up_b, sem_u, part)
    copies_down = fetch_columns(order, down_w, down_b, sem_d, part)
    start(copies)
    wait(arrive)

    def take(group, block):
        return pieces[group][block, 0:STEP, :]

    prepare(own[0], 0, take, other, table, normed, scales, diffs, logits, width, copies_up)

    @pl.loop(0, blocks)
    def _(block):
        at = pl.ds(pl.multiple_of(block * STEP, STEP), STEP)
        for group in range(GROUPS):
            cots[at, group * part : (group + 1) * part] = pieces[group][block, STEP : 2 * STEP, :]

    wait(copies)
    start(copies_down)
    gate[...] = product(normed[...], gate_b[...], INNER)
    wait(copies_up)
    up[...] = product(normed[...], up_b[...], INNER)
    wait(copies_down)
    grad[...] = product(cots[...], down_b[...], CONTRACT)

    @pl.loop(0, blocks)
    def _(block):
        at = pl.ds(pl.multiple_of(block * STEP, STEP), STEP)
        slope, value, lift = grad[at, :], gate[at, :], up[at, :]
        sig = jax.nn.sigmoid(value)
        silu = value * sig
        hidden = (silu * lift).astype(jnp.bfloat16).astype(jnp.float32)
        to_gate = (slope * lift * (sig * (1.0 + value * (1.0 - sig)))).astype(jnp.bfloat16)
        to_up = (slope * silu).astype(jnp.bfloat16)
        grad_gate[at, :] = to_gate
        grad_up[at, :] = to_up
        row_dot = even(lanes(slope * hidden))
        norm_dot = even(
            lanes(to_gate.astype(jnp.float32) * value + to_up.astype(jnp.float32) * lift)
        )
        scale, diff = scales[at, :], diffs[at, :]
        ours, theirs = jax.nn.sigmoid(diff), jax.nn.sigmoid(-diff)
        through = ours * theirs * row_dot
        ones[at, :] = scale * through
        twos[at, :] = scale * scale * ((ours * norm_dot + through * diff) / width)
        diffs[at, :] = scale * ours

    place = lax.broadcasted_iota(jnp.int32, (blocks * STEP, TABLE), 1)
    away = jnp.where((place < 24) & (lax.rem(place, 8) == own[0]), 1.0, 0.0)
    away = away - jnp.concatenate(
        [other[block, 0:STEP, 0:TABLE].astype(jnp.float32) for block in range(blocks)], axis=0
    )
    away = away.astype(jnp.bfloat16)
    for group in range(GROUPS):
        at = slice(group * part, (group + 1) * part)
        rows = product(grad_gate[...], gate_b[at, :], CONTRACT)
        rows = rows + product(grad_up[...], up_b[at, :], CONTRACT)
        turn = product(away, table[group], INNER)
        values = jnp.concatenate([take(group, block) for block in range(blocks)], axis=0)
        rows = (
            rows * (widen(diffs[...], part) * gains_of(table, group))
            + turn * widen(ones[...], part)
            - values.astype(jnp.float32) * widen(twos[...], part)
        )
        out[:, group] = rows.astype(jnp.bfloat16).reshape(blocks, capacity, part)
        hand_out(group, order[group], out, out_to, sem_o).start()
    for group in range(GROUPS):
        hand_out(group, order[group], out, out_to, sem_o).wait()


def backward(order, own, other, table, gate_w, up_w, down_w, pieces):
    blocks, double, part = pieces[0].shape
    capacity = double // 2
    width, units = gate_w.shape
    total = blocks * capacity
    small = pltpu.VMEM((total, 128), jnp.float32)
    return pl.pallas_call(
        backward_kernel,
        out_shape=jax.ShapeDtypeStruct((blocks, GROUPS, capacity, part), jnp.bfloat16),
        in_specs=[SMEM, SMEM, VMEM, VMEM, PLACE, PLACE, PLACE] + [PLACE] * GROUPS,
        out_specs=PLACE,
        scratch_shapes=[pltpu.VMEM((blocks, double, part), jnp.bfloat16)] * GROUPS
        + [pltpu.VMEM((blocks, GROUPS, capacity, part), jnp.bfloat16)]
        + weight_scratch(width, units)
        + [
            pltpu.VMEM((total, width), jnp.bfloat16),
            pltpu.VMEM((total, width), jnp.bfloat16),
            pltpu.VMEM((total, units), jnp.float32),
            pltpu.VMEM((total, units), jnp.float32),
            pltpu.VMEM((total, units), jnp.float32),
            pltpu.VMEM((total, units), jnp.bfloat16),
            pltpu.VMEM((total, units), jnp.bfloat16),
            small,
            small,
            small,
            small,
            pltpu.VMEM((total, TABLE), jnp.float32),
        ]
        + [pltpu.SemaphoreType.DMA((GROUPS,))] * 5,
        compiler_params=pltpu.CompilerParams(vmem_limit_bytes=LIMIT),
        cost_estimate=pl.CostEstimate(
            flops=10 * total * width * units,
            bytes_accessed=6 * width * units + 6 * total * width,
            transcendentals=total * units,
        ),
    )(order, own, other, table, gate_w, up_w, down_w, *pieces)


def finish_kernel(sel, home, base, out):
    blocks, groups, capacity, part = home.shape
    total = base[...].astype(jnp.float32)
    for group in range(groups):
        total = total + product(sel[...], home[:, group].reshape(blocks * capacity, part), INNER)
    out[...] = total.astype(jnp.bfloat16)


def finish(sel, home, base):
    return pl.pallas_call(
        finish_kernel,
        out_shape=jax.ShapeDtypeStruct(base.shape, jnp.bfloat16),
        in_specs=[VMEM] * 3,
        out_specs=VMEM,
        compiler_params=pltpu.CompilerParams(vmem_limit_bytes=LIMIT // 2),
    )(sel, home, base)


def finish_weighted_kernel(one_n, two_n, ones, twos, home, base, out):
    blocks, groups, capacity, part = home.shape
    first = jnp.zeros(base.shape, jnp.float32)
    second = jnp.zeros(base.shape, jnp.float32)
    for group in range(groups):
        rows = home[:, group].reshape(blocks * capacity, part)
        first = first + product(one_n[...], rows, INNER)
        second = second + product(two_n[...], rows, INNER)
    total = base[...].astype(jnp.float32) + first * widen(ones[...], part)
    out[...] = (total + second * widen(twos[...], part)).astype(jnp.bfloat16)


def finish_weighted(one_n, two_n, ones, twos, home, base):
    return pl.pallas_call(
        finish_weighted_kernel,
        out_shape=jax.ShapeDtypeStruct(base.shape, jnp.bfloat16),
        in_specs=[VMEM] * 6,
        out_specs=VMEM,
        compiler_params=pltpu.CompilerParams(vmem_limit_bytes=LIMIT // 2),
    )(one_n, two_n, ones, twos, home, base)


def send_home(pieces):
    experts, hids, capacity, part = pieces.shape
    home = swap(pieces.reshape(experts * hids, capacity, part), BOTH)
    return home.reshape(experts, hids, capacity, part)


def per_device(
    saved_input,
    cotangent,
    next_input,
    routes_saved,
    routes_next,
    norm_gain,
    router,
    expert_gate,
    expert_up,
    expert_down,
):
    gate_w, up_w, down_w = expert_gate[0, 0], expert_up[0, 0], expert_down[0, 0]
    tokens, part = saved_input.shape[1:]
    experts = lax.axis_size("expert")
    capacity = 3 * tokens // experts
    own = lax.axis_index("expert").astype(jnp.int32).reshape(1)
    order = arrival_order()

    tokens_next = with_table(next_input[0], norm_gain, router[0].T)
    tokens_next, routes = lax.optimization_barrier((tokens_next, (routes_saved[0], routes_next[0])))
    packed, sel_saved, one_next, two_next = pack(
        *routes, saved_input[0], cotangent[0], experts, capacity
    )
    near, packed = gather_near(tokens_next, packed)
    packed = swap(packed, "expert")
    moved_next, table, ones, twos = spread(
        routes[1], one_next, two_next, near + gather_far(near), experts
    )
    moved_next = swap(moved_next, "expert")
    other = packed[:, :, part:]
    near, _ = gather_near(packed[:, :, :part])
    near, moved_next = lax.optimization_barrier((near, moved_next))
    far = gather_far(near)
    out_next = forward(order, moved_next, gate_w, up_w, down_w)
    far, out_next = lax.optimization_barrier((far, out_next))
    pieces = near + far
    out_home = send_home(out_next)
    back_part = backward(order, own, other, table, gate_w, up_w, down_w, pieces)
    back_part, out_home = lax.optimization_barrier((back_part, out_home))
    back_home = send_home(back_part)

    forward_out = finish_weighted(one_next, two_next, ones, twos, out_home, next_input[0])
    grad_input = finish(sel_saved, back_home, cotangent[0])

    first_section = lax.axis_index("section") == 0
    outgoing = jnp.where(first_section, forward_out, grad_input)
    leaving = jnp.where(first_section, grad_input, forward_out)
    arriving = partner(outgoing, "section", 0)
    return (leaving[None], arriving[None])


def solution(mesh):
    placed = (
        P("section", "expert", "hid"),
        P("section", "expert", "hid"),
        P("section", "expert", "hid"),
        P("section", "expert", None),
        P("section", "expert", None),
        P("section", "hid"),
        P("section", "hid", None),
        P("section", "expert", None, "hid"),
        P("section", "expert", None, "hid"),
        P("section", "expert", "hid", None),
    )
    return jax.shard_map(
        per_device,
        mesh=mesh,
        in_specs=placed,
        out_specs=(P("section", "expert", "hid"), P("section", "expert", "hid")),
        check_vma=False,
    )
```

```python
import functools

import jax
import jax.numpy as jnp
from jax import lax
from jax.experimental import pallas as pl
from jax.experimental.pallas import tpu as pltpu
from jax.sharding import PartitionSpec as P

EPSILON = 1e-05
INNER = (((1,), (0,)), ((), ()))
CONTRACT = (((1,), (1,)), ((), ()))
LEADING = (((0,), (0,)), ((), ()))
BOTH = ("expert", "hid")
STEP = 48
GROUPS = 8
TABLE = 32
LIMIT = 56 * 1024 * 1024
MOST = 60 * 1024 * 1024
VMEM = pl.BlockSpec(memory_space=pltpu.VMEM)
SMEM = pl.BlockSpec(memory_space=pltpu.SMEM)
PLACE = pl.BlockSpec(memory_space=pl.ANY)


def product(left, right, dims):
    return lax.dot_general(left, right, dims, preferred_element_type=jnp.float32)


def partner(block, axis, bit):
    count = lax.axis_size(axis)
    route = []
    for low in range(count):
        high = low | 1 << bit
        if high != low and high < count:
            route += [(low, high), (high, low)]
    return lax.ppermute(block, axis, route)


def swap(block, axes):
    return lax.all_to_all(block, axes, split_axis=0, concat_axis=0, tiled=True)


def shift(block, along, across):
    count = lax.axis_size("hid")
    route = []
    for source in range(count):
        x, y = source // 2, source % 2
        route.append((source, (x + along) % (count // 2) * 2 + (y ^ across)))
    return lax.ppermute(block, "hid", route)


def gather_near(block, after=()):
    other = shift(block, 0, 1)
    right, left = shift(block, 1, 0), shift(block, -1, 0)
    other, right, left, after = lax.optimization_barrier((other, right, left, after))
    right_other, left_other = shift(other, 1, 0), shift(other, -1, 0)
    return [block, other, right, right_other, left, left_other], after


def gather_far(near):
    return [shift(near[2], 1, 0), shift(near[5], -1, 0)]


def arrival_order():
    own = lax.axis_index("hid")
    half = lax.axis_size("hid") // 2
    x, y = own // 2, own % 2
    places = []
    for along in (0, -1, 1, 2):
        row = (x + along + half) % half * 2
        places += [row + y, row + 1 - y]
    return jnp.stack(places).astype(jnp.int32)


def three_parts(value):
    high = value.astype(jnp.bfloat16)
    rest = value - high.astype(jnp.float32)
    middle = rest.astype(jnp.bfloat16)
    low = (rest - middle.astype(jnp.float32)).astype(jnp.bfloat16)
    return high, middle, low


def whole(shape):
    return pl.BlockSpec(shape, lambda i: (0,) * len(shape))


def table_kernel(upcoming, gain, router, tokens_out):
    tokens, part = upcoming.shape
    experts = router.shape[0]
    tokens_out[0:tokens, :] = upcoming[...]
    gains = gain[...]
    scaled = router[...] * gains
    rows = [p.astype(jnp.float32) for p in three_parts(scaled)]
    rows += [p.astype(jnp.float32) for p in three_parts(gains)]
    rows.append(jnp.zeros((TABLE - 3 * experts - 3, part), jnp.float32))
    tokens_out[tokens : tokens + TABLE, :] = jnp.concatenate(rows, axis=0).astype(jnp.bfloat16)


def with_table(upcoming, gain, router):
    tokens, part = upcoming.shape
    shape = (tokens + TABLE, part)
    return pl.pallas_call(
        table_kernel,
        out_shape=jax.ShapeDtypeStruct(shape, jnp.bfloat16),
        grid=(1,),
        in_specs=[whole(a.shape) for a in (upcoming, gain, router)],
        out_specs=whole(shape),
        compiler_params=pltpu.CompilerParams(vmem_limit_bytes=MOST),
    )(upcoming, gain, router)


def column(row, number):
    width = row.shape[1]
    down = lax.broadcasted_iota(jnp.int32, (width, width), 0)
    across = lax.broadcasted_iota(jnp.int32, (width, width), 1)
    values = row[number : number + 1, :].astype(jnp.float32)
    return jnp.sum(jnp.where(down == across, values, 0.0), axis=1, keepdims=True).astype(jnp.int32)


def pack_kernel(experts, capacity, routes_s, routes_n, saved, cot, packed, sel_s, one_n, two_n):
    tokens, part = saved.shape
    row = lax.broadcasted_iota(jnp.int32, (tokens, tokens), 0)
    lane = lax.broadcasted_iota(jnp.int32, (tokens, tokens), 1)
    earlier = jnp.where(lane < row, 1.0, 0.0).astype(jnp.bfloat16)
    wide = lax.broadcasted_iota(jnp.int32, (tokens, 128), 1)
    slots = lax.broadcasted_iota(jnp.int32, (tokens, experts * capacity), 1)

    def select(routes):
        ids = routes[...]
        one, two = column(ids, 0), column(ids, 1)
        hit_one = jnp.where(wide == one, 1.0, 0.0)
        hit_two = jnp.where(wide == two, 1.0, 0.0)
        counts = product(earlier, (hit_one + hit_two).astype(jnp.bfloat16), INNER)
        rank_one = jnp.sum(counts * hit_one, axis=1, keepdims=True).astype(jnp.int32)
        rank_two = jnp.sum(counts * hit_two, axis=1, keepdims=True).astype(jnp.int32)
        first = jnp.where(slots == one * capacity + rank_one, 1.0, 0.0)
        second = jnp.where(slots == two * capacity + rank_two, 1.0, 0.0)
        return one, two, first.astype(jnp.bfloat16), second.astype(jnp.bfloat16)

    def put(start, lanes, width, value):
        packed[:, start : start + capacity, lanes : lanes + width] = value.reshape(
            experts, capacity, width
        )

    one, two, first, second = select(routes_s)
    inside = wide < 3 * experts
    wide_one = jnp.where(inside & (lax.rem(wide, experts) == one), 1.0, 0.0).astype(jnp.bfloat16)
    wide_two = jnp.where(inside & (lax.rem(wide, experts) == two), 1.0, 0.0).astype(jnp.bfloat16)
    both = first + second
    sel_s[...] = both
    put(0, 0, part, product(both, saved[...], LEADING).astype(jnp.bfloat16))
    put(capacity, 0, part, product(both, cot[...], LEADING).astype(jnp.bfloat16))
    other = product(first, wide_two, LEADING) + product(second, wide_one, LEADING)
    put(0, part, 128, other.astype(jnp.bfloat16))
    put(capacity, part, 128, jnp.zeros(other.shape, jnp.bfloat16))
    _, _, first, second = select(routes_n)
    one_n[...] = first
    two_n[...] = second


def pack(routes_s, routes_n, saved, cot, experts, capacity):
    tokens, part = saved.shape
    total = experts * capacity
    shapes = [(experts, 2 * capacity, part + 128)] + [(tokens, total)] * 3
    return pl.pallas_call(
        functools.partial(pack_kernel, experts, capacity),
        out_shape=[jax.ShapeDtypeStruct(s, jnp.bfloat16) for s in shapes],
        grid=(1,),
        in_specs=[whole(a.shape) for a in (routes_s, routes_n, saved, cot)],
        out_specs=[whole(s) for s in shapes],
        compiler_params=pltpu.CompilerParams(vmem_limit_bytes=MOST),
    )(routes_s, routes_n, saved, cot)


def spread_kernel(routes, one_n, two_n, *refs):
    pieces, (moved, table, ones, twos) = refs[:GROUPS], refs[GROUPS:]
    tokens = one_n.shape[0]
    blocks, _, capacity, part = moved.shape
    total = jnp.zeros((tokens, 128), jnp.float32)
    logits = jnp.zeros((tokens, TABLE), jnp.float32)
    for group, piece in enumerate(pieces):
        table[group] = piece[tokens : tokens + TABLE, :]
        values = piece[0:tokens, :].astype(jnp.float32)
        total = total + lanes(values * values)
        logits = logits + product(piece[0:tokens, :], piece[tokens : tokens + TABLE, :], CONTRACT)
    scale = lax.rsqrt(even(total) / (GROUPS * part) + EPSILON)
    ids = routes[...]
    place = lax.broadcasted_iota(jnp.int32, (tokens, TABLE), 1)
    first = jnp.where((place < 24) & (lax.rem(place, 8) == column(ids, 0)), 1.0, 0.0)
    second = jnp.where((place < 24) & (lax.rem(place, 8) == column(ids, 1)), 1.0, 0.0)
    diff = even(logits * (first - second)) * scale
    ones[...] = jax.nn.sigmoid(diff)
    twos[...] = jax.nn.sigmoid(-diff)
    both = one_n[...] + two_n[...]
    for group, piece in enumerate(pieces):
        values = piece[0:tokens, :].astype(jnp.float32)
        normed = (values * widen(scale, part) * gains_of(table, group)).astype(jnp.bfloat16)
        rows = product(both, normed, LEADING).astype(jnp.bfloat16)
        moved[:, group] = rows.reshape(blocks, capacity, part)


def spread(routes, one_n, two_n, pieces, blocks):
    part = pieces[0].shape[1]
    tokens, total = one_n.shape
    return pl.pallas_call(
        spread_kernel,
        out_shape=(
            jax.ShapeDtypeStruct((blocks, GROUPS, total // blocks, part), jnp.bfloat16),
            jax.ShapeDtypeStruct((GROUPS, TABLE, part), jnp.bfloat16),
            jax.ShapeDtypeStruct((tokens, 128), jnp.float32),
            jax.ShapeDtypeStruct((tokens, 128), jnp.float32),
        ),
        grid=(1,),
        in_specs=[whole(a.shape) for a in (routes, one_n, two_n)] + [VMEM] * GROUPS,
        out_specs=(
            whole((blocks, GROUPS, total // blocks, part)),
            whole((GROUPS, TABLE, part)),
            whole((tokens, 128)),
            whole((tokens, 128)),
        ),
        compiler_params=pltpu.CompilerParams(vmem_limit_bytes=MOST),
    )(routes, one_n, two_n, *pieces)


def widen(value, width):
    return jnp.concatenate([value] * (width // 128), axis=1)


def lanes(value):
    total = value[:, 0:128]
    for start in range(128, value.shape[1], 128):
        total = total + value[:, start : start + 128]
    return total


def even(value):
    return jnp.broadcast_to(jnp.sum(value, axis=1, keepdims=True), (value.shape[0], 128))


def gains_of(table, group):
    rows = table[group, 24:32, :].astype(jnp.float32)
    return rows[0:1] + (rows[1:2] + rows[2:3])


def fetch_rows(order, source, target, sems, part):
    copies = []
    for group in range(GROUPS):
        start = pl.multiple_of(order[group] * part, part)
        copies.append(
            pltpu.make_async_copy(
                source.at[pl.ds(start, part), :],
                target.at[pl.ds(group * part, part), :],
                sems.at[group],
            )
        )
    return copies


def fetch_columns(order, source, target, sems, part):
    copies = []
    for group in range(GROUPS):
        start = group * part
        if order is not None:
            start = pl.multiple_of(order[group] * part, part)
        copies.append(
            pltpu.make_async_copy(
                source.at[:, pl.ds(start, part)],
                target.at[:, pl.ds(group * part, part)],
                sems.at[group],
            )
        )
    return copies


def start(copies):
    for copy in copies:
        copy.start()


def wait(copies):
    for copy in copies:
        copy.wait()


def prepare(own, other_start, take, other, table, normed, scales, diffs, logits, width, between):
    blocks = other.shape[0]
    part = width // GROUPS
    for group in range(GROUPS):
        rows = jnp.concatenate([take(group, block) for block in range(blocks)], axis=0)
        found = product(rows, table[group], CONTRACT)
        if group == 0:
            logits[...] = found
        else:
            logits[...] += found
    start(between)

    @pl.loop(0, blocks)
    def _(block):
        at = pl.ds(pl.multiple_of(block * STEP, STEP), STEP)
        total = jnp.zeros((STEP, 128), jnp.float32)
        for group in range(GROUPS):
            values = take(group, block).astype(jnp.float32)
            total = total + lanes(values * values)
        scale = lax.rsqrt(even(total) / width + EPSILON)
        scales[at, :] = scale
        place = lax.broadcasted_iota(jnp.int32, (STEP, TABLE), 1)
        ours = jnp.where((place < 24) & (lax.rem(place, 8) == own), 1.0, 0.0)
        theirs = other[block, other_start : other_start + STEP, 0:TABLE].astype(jnp.float32)
        diffs[at, :] = even(logits[at, :] * (ours - theirs)) * scale
        for group in range(GROUPS):
            values = take(group, block).astype(jnp.float32)
            normed[at, group * part : (group + 1) * part] = (
                values * widen(scale, part) * gains_of(table, group)
            ).astype(jnp.bfloat16)


def hand_out(group, place, source, target, sems):
    return pltpu.make_async_copy(
        source.at[:, group : group + 1], target.at[:, pl.ds(place, 1)], sems.at[group]
    )


def forward_kernel(
    order, moved, gate_w, up_w, down_w, out_to,
    rows, out, gate_b, up_b, down_b, gate, up, hidden, sem_m, sem_o, sem_g, sem_u, sem_d
):
    blocks, _, capacity, part = moved.shape
    total, width = blocks * capacity, GROUPS * part
    arrive = [
        pltpu.make_async_copy(
            moved.at[:, group], rows.at[:, :, pl.ds(group * part, part)], sem_m.at[group]
        )
        for group in range(GROUPS)
    ]
    copies = fetch_rows(order, gate_w, gate_b, sem_g, part)
    copies_up = fetch_rows(order, up_w, up_b, sem_u, part)
    copies_down = fetch_columns(None, down_w, down_b, sem_d, part)
    start(arrive)
    start(copies)
    wait(arrive)
    start(copies_up)
    wait(copies)
    start(copies_down)
    gate[...] = product(rows[...].reshape(total, width), gate_b[...], INNER)
    wait(copies_up)
    up[...] = product(rows[...].reshape(total, width), up_b[...], INNER)

    @pl.loop(0, blocks)
    def _(block):
        at = pl.ds(pl.multiple_of(block * STEP, STEP), STEP)
        value = gate[at, :]
        hidden[at, :] = (value * jax.nn.sigmoid(value) * up[at, :]).astype(jnp.bfloat16)

    for group in range(GROUPS):
        copies_down[group].wait()
        part_out = product(hidden[...], down_b[:, group * part : (group + 1) * part], INNER)
        out[:, group] = part_out.astype(jnp.bfloat16).reshape(blocks, capacity, part)
        hand_out(group, group, out, out_to, sem_o).start()
    for group in range(GROUPS):
        hand_out(group, group, out, out_to, sem_o).wait()


def weight_scratch(width, units):
    return [
        pltpu.VMEM((width, units), jnp.bfloat16),
        pltpu.VMEM((width, units), jnp.bfloat16),
        pltpu.VMEM((units, width), jnp.bfloat16),
    ]


def forward(order, moved, gate_w, up_w, down_w):
    blocks, _, capacity, part = moved.shape
    width, units = gate_w.shape
    total = blocks * capacity
    return pl.pallas_call(
        forward_kernel,
        out_shape=jax.ShapeDtypeStruct(moved.shape, jnp.bfloat16),
        in_specs=[SMEM] + [PLACE] * 4,
        out_specs=PLACE,
        scratch_shapes=[
            pltpu.VMEM((blocks, capacity, width), jnp.bfloat16),
            pltpu.VMEM(moved.shape, jnp.bfloat16),
        ]
        + weight_scratch(width, units)
        + [
            pltpu.VMEM((total, units), jnp.float32),
            pltpu.VMEM((total, units), jnp.float32),
            pltpu.VMEM((total, units), jnp.bfloat16),
        ]
        + [pltpu.SemaphoreType.DMA((GROUPS,))] * 5,
        compiler_params=pltpu.CompilerParams(vmem_limit_bytes=LIMIT),
        cost_estimate=pl.CostEstimate(
            flops=6 * total * width * units,
            bytes_accessed=6 * width * units + 4 * total * width,
            transcendentals=total * units,
        ),
    )(order, moved, gate_w, up_w, down_w)


def backward_kernel(*refs):
    order, own, other, table, gate_w, up_w, down_w = refs[:7]
    pieces_in = refs[7 : 7 + GROUPS]
    out_to, pieces = refs[7 + GROUPS], refs[8 + GROUPS : 8 + 2 * GROUPS]
    (
        out, gate_b, up_b, down_b, normed, cots, gate, up, grad, grad_gate, grad_up,
        scales, diffs, ones, twos, logits, sem_m, sem_o, sem_g, sem_u, sem_d,
    ) = refs[8 + 2 * GROUPS :]
    blocks, _, capacity, part = out.shape
    width = GROUPS * part
    arrive = [
        pltpu.make_async_copy(pieces_in[group], pieces[group], sem_m.at[group])
        for group in range(GROUPS)
    ]
    start(arrive)
    copies = fetch_rows(order, gate_w, gate_b, sem_g, part)
    copies_up = fetch_rows(order, up_w, up_b, sem_u, part)
    copies_down = fetch_columns(order, down_w, down_b, sem_d, part)
    start(copies)
    wait(arrive)

    def take(group, block):
        return pieces[group][block, 0:STEP, :]

    prepare(own[0], 0, take, other, table, normed, scales, diffs, logits, width, copies_up)

    @pl.loop(0, blocks)
    def _(block):
        at = pl.ds(pl.multiple_of(block * STEP, STEP), STEP)
        for group in range(GROUPS):
            cots[at, group * part : (group + 1) * part] = pieces[group][block, STEP : 2 * STEP, :]

    wait(copies)
    start(copies_down)
    gate[...] = product(normed[...], gate_b[...], INNER)
    wait(copies_up)
    up[...] = product(normed[...], up_b[...], INNER)
    wait(copies_down)
    grad[...] = product(cots[...], down_b[...], CONTRACT)

    @pl.loop(0, blocks)
    def _(block):
        at = pl.ds(pl.multiple_of(block * STEP, STEP), STEP)
        slope, value, lift = grad[at, :], gate[at, :], up[at, :]
        sig = jax.nn.sigmoid(value)
        silu = value * sig
        hidden = (silu * lift).astype(jnp.bfloat16).astype(jnp.float32)
        to_gate = (slope * lift * (sig * (1.0 + value * (1.0 - sig)))).astype(jnp.bfloat16)
        to_up = (slope * silu).astype(jnp.bfloat16)
        grad_gate[at, :] = to_gate
        grad_up[at, :] = to_up
        row_dot = even(lanes(slope * hidden))
        norm_dot = even(
            lanes(to_gate.astype(jnp.float32) * value + to_up.astype(jnp.float32) * lift)
        )
        scale, diff = scales[at, :], diffs[at, :]
        ours, theirs = jax.nn.sigmoid(diff), jax.nn.sigmoid(-diff)
        through = ours * theirs * row_dot
        ones[at, :] = scale * through
        twos[at, :] = scale * scale * ((ours * norm_dot + through * diff) / width)
        diffs[at, :] = scale * ours

    place = lax.broadcasted_iota(jnp.int32, (blocks * STEP, TABLE), 1)
    away = jnp.where((place < 24) & (lax.rem(place, 8) == own[0]), 1.0, 0.0)
    away = away - jnp.concatenate(
        [other[block, 0:STEP, 0:TABLE].astype(jnp.float32) for block in range(blocks)], axis=0
    )
    away = away.astype(jnp.bfloat16)
    for group in range(GROUPS):
        at = slice(group * part, (group + 1) * part)
        rows = product(grad_gate[...], gate_b[at, :], CONTRACT)
        rows = rows + product(grad_up[...], up_b[at, :], CONTRACT)
        turn = product(away, table[group], INNER)
        values = jnp.concatenate([take(group, block) for block in range(blocks)], axis=0)
        rows = (
            rows * (widen(diffs[...], part) * gains_of(table, group))
            + turn * widen(ones[...], part)
            - values.astype(jnp.float32) * widen(twos[...], part)
        )
        out[:, group] = rows.astype(jnp.bfloat16).reshape(blocks, capacity, part)
        hand_out(group, order[group], out, out_to, sem_o).start()
    for group in range(GROUPS):
        hand_out(group, order[group], out, out_to, sem_o).wait()


def backward(order, own, other, table, gate_w, up_w, down_w, pieces):
    blocks, double, part = pieces[0].shape
    capacity = double // 2
    width, units = gate_w.shape
    total = blocks * capacity
    small = pltpu.VMEM((total, 128), jnp.float32)
    return pl.pallas_call(
        backward_kernel,
        out_shape=jax.ShapeDtypeStruct((blocks, GROUPS, capacity, part), jnp.bfloat16),
        in_specs=[SMEM, SMEM, VMEM, VMEM, PLACE, PLACE, PLACE] + [PLACE] * GROUPS,
        out_specs=PLACE,
        scratch_shapes=[pltpu.VMEM((blocks, double, part), jnp.bfloat16)] * GROUPS
        + [pltpu.VMEM((blocks, GROUPS, capacity, part), jnp.bfloat16)]
        + weight_scratch(width, units)
        + [
            pltpu.VMEM((total, width), jnp.bfloat16),
            pltpu.VMEM((total, width), jnp.bfloat16),
            pltpu.VMEM((total, units), jnp.float32),
            pltpu.VMEM((total, units), jnp.float32),
            pltpu.VMEM((total, units), jnp.float32),
            pltpu.VMEM((total, units), jnp.bfloat16),
            pltpu.VMEM((total, units), jnp.bfloat16),
            small,
            small,
            small,
            small,
            pltpu.VMEM((total, TABLE), jnp.float32),
        ]
        + [pltpu.SemaphoreType.DMA((GROUPS,))] * 5,
        compiler_params=pltpu.CompilerParams(vmem_limit_bytes=LIMIT),
        cost_estimate=pl.CostEstimate(
            flops=10 * total * width * units,
            bytes_accessed=6 * width * units + 6 * total * width,
            transcendentals=total * units,
        ),
    )(order, own, other, table, gate_w, up_w, down_w, *pieces)


def finish_kernel(sel, home, base, out):
    blocks, groups, capacity, part = home.shape
    total = base[...].astype(jnp.float32)
    for group in range(groups):
        total = total + product(sel[...], home[:, group].reshape(blocks * capacity, part), INNER)
    out[...] = total.astype(jnp.bfloat16)


def finish(sel, home, base):
    return pl.pallas_call(
        finish_kernel,
        out_shape=jax.ShapeDtypeStruct(base.shape, jnp.bfloat16),
        in_specs=[VMEM] * 3,
        out_specs=VMEM,
        compiler_params=pltpu.CompilerParams(vmem_limit_bytes=LIMIT // 2),
    )(sel, home, base)


def finish_weighted_kernel(one_n, two_n, ones, twos, home, base, out):
    blocks, groups, capacity, part = home.shape
    first = jnp.zeros(base.shape, jnp.float32)
    second = jnp.zeros(base.shape, jnp.float32)
    for group in range(groups):
        rows = home[:, group].reshape(blocks * capacity, part)
        first = first + product(one_n[...], rows, INNER)
        second = second + product(two_n[...], rows, INNER)
    total = base[...].astype(jnp.float32) + first * widen(ones[...], part)
    out[...] = (total + second * widen(twos[...], part)).astype(jnp.bfloat16)


def finish_weighted(one_n, two_n, ones, twos, home, base):
    return pl.pallas_call(
        finish_weighted_kernel,
        out_shape=jax.ShapeDtypeStruct(base.shape, jnp.bfloat16),
        in_specs=[VMEM] * 6,
        out_specs=VMEM,
        compiler_params=pltpu.CompilerParams(vmem_limit_bytes=LIMIT // 2),
    )(one_n, two_n, ones, twos, home, base)


def send_home(pieces):
    experts, hids, capacity, part = pieces.shape
    home = swap(pieces.reshape(experts * hids, capacity, part), BOTH)
    return home.reshape(experts, hids, capacity, part)


def per_device(
    saved_input,
    cotangent,
    next_input,
    routes_saved,
    routes_next,
    norm_gain,
    router,
    expert_gate,
    expert_up,
    expert_down,
):
    gate_w, up_w, down_w = expert_gate[0, 0], expert_up[0, 0], expert_down[0, 0]
    tokens, part = saved_input.shape[1:]
    experts = lax.axis_size("expert")
    capacity = 3 * tokens // experts
    own = lax.axis_index("expert").astype(jnp.int32).reshape(1)
    order = arrival_order()

    tokens_next = with_table(next_input[0], norm_gain, router[0].T)
    tokens_next, routes = lax.optimization_barrier((tokens_next, (routes_saved[0].T, routes_next[0].T)))
    packed, sel_saved, one_next, two_next = pack(
        *routes, saved_input[0], cotangent[0], experts, capacity
    )
    near, packed = gather_near(tokens_next, packed)
    packed = swap(packed, "expert")
    moved_next, table, ones, twos = spread(
        routes[1], one_next, two_next, near + gather_far(near), experts
    )
    moved_next = swap(moved_next, "expert")
    other = packed[:, :, part:]
    near, _ = gather_near(packed[:, :, :part])
    near, moved_next = lax.optimization_barrier((near, moved_next))
    far = gather_far(near)
    out_next = forward(order, moved_next, gate_w, up_w, down_w)
    far, out_next = lax.optimization_barrier((far, out_next))
    pieces = near + far
    out_home = send_home(out_next)
    back_part = backward(order, own, other, table, gate_w, up_w, down_w, pieces)
    back_part, out_home = lax.optimization_barrier((back_part, out_home))
    back_home = send_home(back_part)

    forward_out = finish_weighted(one_next, two_next, ones, twos, out_home, next_input[0])
    grad_input = finish(sel_saved, back_home, cotangent[0])

    first_section = lax.axis_index("section") == 0
    outgoing = jnp.where(first_section, forward_out, grad_input)
    leaving = jnp.where(first_section, grad_input, forward_out)
    arriving = partner(outgoing, "section", 0)
    return (leaving[None], arriving[None])


def solution(mesh):
    placed = (
        P("section", "expert", "hid"),
        P("section", "expert", "hid"),
        P("section", "expert", "hid"),
        P("section", "expert", None),
        P("section", "expert", None),
        P("section", "hid"),
        P("section", "hid", None),
        P("section", "expert", None, "hid"),
        P("section", "expert", None, "hid"),
        P("section", "expert", "hid", None),
    )
    return jax.shard_map(
        per_device,
        mesh=mesh,
        in_specs=placed,
        out_specs=(P("section", "expert", "hid"), P("section", "expert", "hid")),
        check_vma=False,
    )
```

```python
import functools

import jax
import jax.numpy as jnp
from jax import lax
from jax.experimental import pallas as pl
from jax.experimental.pallas import tpu as pltpu
from jax.sharding import PartitionSpec as P

EPSILON = 1e-05
INNER = (((1,), (0,)), ((), ()))
CONTRACT = (((1,), (1,)), ((), ()))
LEADING = (((0,), (0,)), ((), ()))
BOTH = ("expert", "hid")
STEP = 48
GROUPS = 8
TABLE = 32
LIMIT = 56 * 1024 * 1024
MOST = 60 * 1024 * 1024
VMEM = pl.BlockSpec(memory_space=pltpu.VMEM)
SMEM = pl.BlockSpec(memory_space=pltpu.SMEM)
PLACE = pl.BlockSpec(memory_space=pl.ANY)


def product(left, right, dims):
    return lax.dot_general(left, right, dims, preferred_element_type=jnp.float32)


def partner(block, axis, bit):
    count = lax.axis_size(axis)
    route = []
    for low in range(count):
        high = low | 1 << bit
        if high != low and high < count:
            route += [(low, high), (high, low)]
    return lax.ppermute(block, axis, route)


def swap(block, axes):
    return lax.all_to_all(block, axes, split_axis=0, concat_axis=0, tiled=True)


def shift(block, along, across):
    count = lax.axis_size("hid")
    route = []
    for source in range(count):
        x, y = source // 2, source % 2
        route.append((source, (x + along) % (count // 2) * 2 + (y ^ across)))
    return lax.ppermute(block, "hid", route)


def gather_near(block, after=()):
    other = shift(block, 0, 1)
    right, left = shift(block, 1, 0), shift(block, -1, 0)
    other, right, left, after = lax.optimization_barrier((other, right, left, after))
    right_other, left_other = shift(other, 1, 0), shift(other, -1, 0)
    return [block, other, right, right_other, left, left_other], after


def gather_far(near):
    return [shift(near[2], 1, 0), shift(near[5], -1, 0)]


def arrival_order():
    own = lax.axis_index("hid")
    half = lax.axis_size("hid") // 2
    x, y = own // 2, own % 2
    places = []
    for along in (0, -1, 1, 2):
        row = (x + along + half) % half * 2
        places += [row + y, row + 1 - y]
    return jnp.stack(places).astype(jnp.int32)


def three_parts(value):
    high = value.astype(jnp.bfloat16)
    rest = value - high.astype(jnp.float32)
    middle = rest.astype(jnp.bfloat16)
    low = (rest - middle.astype(jnp.float32)).astype(jnp.bfloat16)
    return high, middle, low


def whole(shape):
    return pl.BlockSpec(shape, lambda i: (0,) * len(shape))


def table_kernel(upcoming, gain, router, tokens_out):
    tokens, part = upcoming.shape
    experts = router.shape[0]
    tokens_out[0:tokens, :] = upcoming[...]
    gains = gain[...]
    scaled = router[...] * gains
    rows = [p.astype(jnp.float32) for p in three_parts(scaled)]
    rows += [p.astype(jnp.float32) for p in three_parts(gains)]
    rows.append(jnp.zeros((TABLE - 3 * experts - 3, part), jnp.float32))
    tokens_out[tokens : tokens + TABLE, :] = jnp.concatenate(rows, axis=0).astype(jnp.bfloat16)


def with_table(upcoming, gain, router):
    tokens, part = upcoming.shape
    shape = (tokens + TABLE, part)
    return pl.pallas_call(
        table_kernel,
        out_shape=jax.ShapeDtypeStruct(shape, jnp.bfloat16),
        grid=(1,),
        in_specs=[whole(a.shape) for a in (upcoming, gain, router)],
        out_specs=whole(shape),
        compiler_params=pltpu.CompilerParams(vmem_limit_bytes=MOST),
    )(upcoming, gain, router)


def column(row, number):
    width = row.shape[1]
    down = lax.broadcasted_iota(jnp.int32, (width, width), 0)
    across = lax.broadcasted_iota(jnp.int32, (width, width), 1)
    values = row[number : number + 1, :].astype(jnp.float32)
    return jnp.sum(jnp.where(down == across, values, 0.0), axis=1, keepdims=True).astype(jnp.int32)


def pack_kernel(experts, capacity, routes_s, routes_n, saved, cot, packed, sel_s, one_n, two_n):
    tokens, part = saved.shape
    row = lax.broadcasted_iota(jnp.int32, (tokens, tokens), 0)
    lane = lax.broadcasted_iota(jnp.int32, (tokens, tokens), 1)
    earlier = jnp.where(lane < row, 1.0, 0.0).astype(jnp.bfloat16)
    wide = lax.broadcasted_iota(jnp.int32, (tokens, 128), 1)
    slots = lax.broadcasted_iota(jnp.int32, (tokens, experts * capacity), 1)

    def select(routes):
        ids = routes[...]
        one, two = column(ids, 0), column(ids, 1)
        hit_one = jnp.where(wide == one, 1.0, 0.0)
        hit_two = jnp.where(wide == two, 1.0, 0.0)
        counts = product(earlier, (hit_one + hit_two).astype(jnp.bfloat16), INNER)
        rank_one = jnp.sum(counts * hit_one, axis=1, keepdims=True).astype(jnp.int32)
        rank_two = jnp.sum(counts * hit_two, axis=1, keepdims=True).astype(jnp.int32)
        first = jnp.where(slots == one * capacity + rank_one, 1.0, 0.0)
        second = jnp.where(slots == two * capacity + rank_two, 1.0, 0.0)
        return one, two, first.astype(jnp.bfloat16), second.astype(jnp.bfloat16)

    def put(start, lanes, width, value):
        packed[:, start : start + capacity, lanes : lanes + width] = value.reshape(
            experts, capacity, width
        )

    one, two, first, second = select(routes_s)
    inside = wide < 3 * experts
    wide_one = jnp.where(inside & (lax.rem(wide, experts) == one), 1.0, 0.0).astype(jnp.bfloat16)
    wide_two = jnp.where(inside & (lax.rem(wide, experts) == two), 1.0, 0.0).astype(jnp.bfloat16)
    both = first + second
    sel_s[...] = both
    put(0, 0, part, product(both, saved[...], LEADING).astype(jnp.bfloat16))
    put(capacity, 0, part, product(both, cot[...], LEADING).astype(jnp.bfloat16))
    other = product(first, wide_two, LEADING) + product(second, wide_one, LEADING)
    put(0, part, 128, other.astype(jnp.bfloat16))
    put(capacity, part, 128, jnp.zeros(other.shape, jnp.bfloat16))
    _, _, first, second = select(routes_n)
    one_n[...] = first
    two_n[...] = second


def pack(routes_s, routes_n, saved, cot, experts, capacity):
    tokens, part = saved.shape
    total = experts * capacity
    shapes = [(experts, 2 * capacity, part + 128)] + [(tokens, total)] * 3
    return pl.pallas_call(
        functools.partial(pack_kernel, experts, capacity),
        out_shape=[jax.ShapeDtypeStruct(s, jnp.bfloat16) for s in shapes],
        grid=(1,),
        in_specs=[whole(a.shape) for a in (routes_s, routes_n, saved, cot)],
        out_specs=[whole(s) for s in shapes],
        compiler_params=pltpu.CompilerParams(vmem_limit_bytes=MOST),
    )(routes_s, routes_n, saved, cot)


def spread_kernel(routes, one_n, two_n, *refs):
    pieces, (moved, table, ones, twos) = refs[:GROUPS], refs[GROUPS:]
    tokens = one_n.shape[0]
    blocks, _, capacity, part = moved.shape
    total = jnp.zeros((tokens, 128), jnp.float32)
    logits = jnp.zeros((tokens, TABLE), jnp.float32)
    for group, piece in enumerate(pieces):
        table[group] = piece[tokens : tokens + TABLE, :]
        values = piece[0:tokens, :].astype(jnp.float32)
        total = total + lanes(values * values)
        logits = logits + product(piece[0:tokens, :], piece[tokens : tokens + TABLE, :], CONTRACT)
    scale = lax.rsqrt(even(total) / (GROUPS * part) + EPSILON)
    ids = routes[...]
    place = lax.broadcasted_iota(jnp.int32, (tokens, TABLE), 1)
    first = jnp.where((place < 24) & (lax.rem(place, 8) == column(ids, 0)), 1.0, 0.0)
    second = jnp.where((place < 24) & (lax.rem(place, 8) == column(ids, 1)), 1.0, 0.0)
    diff = even(logits * (first - second)) * scale
    ones[...] = jax.nn.sigmoid(diff)
    twos[...] = jax.nn.sigmoid(-diff)
    both = one_n[...] + two_n[...]
    for group, piece in enumerate(pieces):
        values = piece[0:tokens, :].astype(jnp.float32)
        normed = (values * widen(scale, part) * gains_of(table, group)).astype(jnp.bfloat16)
        rows = product(both, normed, LEADING).astype(jnp.bfloat16)
        moved[:, group] = rows.reshape(blocks, capacity, part)


def spread(routes, one_n, two_n, pieces, blocks):
    part = pieces[0].shape[1]
    tokens, total = one_n.shape
    return pl.pallas_call(
        spread_kernel,
        out_shape=(
            jax.ShapeDtypeStruct((blocks, GROUPS, total // blocks, part), jnp.bfloat16),
            jax.ShapeDtypeStruct((GROUPS, TABLE, part), jnp.bfloat16),
            jax.ShapeDtypeStruct((tokens, 128), jnp.float32),
            jax.ShapeDtypeStruct((tokens, 128), jnp.float32),
        ),
        grid=(1,),
        in_specs=[whole(a.shape) for a in (routes, one_n, two_n)] + [VMEM] * GROUPS,
        out_specs=(
            whole((blocks, GROUPS, total // blocks, part)),
            whole((GROUPS, TABLE, part)),
            whole((tokens, 128)),
            whole((tokens, 128)),
        ),
        compiler_params=pltpu.CompilerParams(vmem_limit_bytes=MOST),
    )(routes, one_n, two_n, *pieces)


def widen(value, width):
    return jnp.concatenate([value] * (width // 128), axis=1)


def lanes(value):
    total = value[:, 0:128]
    for start in range(128, value.shape[1], 128):
        total = total + value[:, start : start + 128]
    return total


def even(value):
    return jnp.broadcast_to(jnp.sum(value, axis=1, keepdims=True), (value.shape[0], 128))


def gains_of(table, group):
    rows = table[group, 24:32, :].astype(jnp.float32)
    return rows[0:1] + (rows[1:2] + rows[2:3])


def fetch_rows(order, source, target, sems, part, columns=slice(None)):
    copies = []
    for group in range(GROUPS):
        start = pl.multiple_of(order[group] * part, part)
        copies.append(
            pltpu.make_async_copy(
                source.at[pl.ds(start, part), columns],
                target.at[pl.ds(group * part, part), columns],
                sems.at[group],
            )
        )
    return copies


def fetch_columns(order, source, target, sems, part):
    copies = []
    for group in range(GROUPS):
        start = group * part
        if order is not None:
            start = pl.multiple_of(order[group] * part, part)
        copies.append(
            pltpu.make_async_copy(
                source.at[:, pl.ds(start, part)],
                target.at[:, pl.ds(group * part, part)],
                sems.at[group],
            )
        )
    return copies


def start(copies):
    for copy in copies:
        copy.start()


def wait(copies):
    for copy in copies:
        copy.wait()


def prepare(own, other_start, take, other, table, normed, scales, diffs, logits, width, between):
    blocks = other.shape[0]
    part = width // GROUPS
    for group in range(GROUPS):
        rows = jnp.concatenate([take(group, block) for block in range(blocks)], axis=0)
        found = product(rows, table[group], CONTRACT)
        if group == 0:
            logits[...] = found
        else:
            logits[...] += found
    start(between)

    @pl.loop(0, blocks)
    def _(block):
        at = pl.ds(pl.multiple_of(block * STEP, STEP), STEP)
        total = jnp.zeros((STEP, 128), jnp.float32)
        for group in range(GROUPS):
            values = take(group, block).astype(jnp.float32)
            total = total + lanes(values * values)
        scale = lax.rsqrt(even(total) / width + EPSILON)
        scales[at, :] = scale
        place = lax.broadcasted_iota(jnp.int32, (STEP, TABLE), 1)
        ours = jnp.where((place < 24) & (lax.rem(place, 8) == own), 1.0, 0.0)
        theirs = other[block, other_start : other_start + STEP, 0:TABLE].astype(jnp.float32)
        diffs[at, :] = even(logits[at, :] * (ours - theirs)) * scale
        for group in range(GROUPS):
            values = take(group, block).astype(jnp.float32)
            normed[at, group * part : (group + 1) * part] = (
                values * widen(scale, part) * gains_of(table, group)
            ).astype(jnp.bfloat16)


def hand_out(group, place, source, target, sems):
    return pltpu.make_async_copy(
        source.at[:, group : group + 1], target.at[:, pl.ds(place, 1)], sems.at[group]
    )


def forward_kernel(
    order, moved, gate_w, up_w, down_w, out_to,
    rows, out, gate_b, up_b, down_b, gate, up, hidden, sem_m, sem_o, sem_g, sem_h, sem_u, sem_d
):
    blocks, _, capacity, part = moved.shape
    total, width = blocks * capacity, GROUPS * part
    arrive = [
        pltpu.make_async_copy(
            moved.at[:, group], rows.at[:, :, pl.ds(group * part, part)], sem_m.at[group]
        )
        for group in range(GROUPS)
    ]
    near, rest = slice(0, part), slice(part, gate_w.shape[1])
    copies = fetch_rows(order, gate_w, gate_b, sem_g, part, near)
    copies_rest = fetch_rows(order, gate_w, gate_b, sem_h, part, rest)
    copies_up = fetch_rows(order, up_w, up_b, sem_u, part)
    copies_down = fetch_columns(None, down_w, down_b, sem_d, part)
    start(arrive)
    start(copies)
    wait(arrive)
    start(copies_rest)
    wait(copies)
    start(copies_up)
    gate[:, near] = product(rows[...].reshape(total, width), gate_b[:, near], INNER)
    wait(copies_rest)
    gate[:, rest] = product(rows[...].reshape(total, width), gate_b[:, rest], INNER)
    start(copies_down)
    wait(copies_up)
    up[...] = product(rows[...].reshape(total, width), up_b[...], INNER)

    @pl.loop(0, blocks)
    def _(block):
        at = pl.ds(pl.multiple_of(block * STEP, STEP), STEP)
        value = gate[at, :]
        hidden[at, :] = (value * jax.nn.sigmoid(value) * up[at, :]).astype(jnp.bfloat16)

    for group in range(GROUPS):
        copies_down[group].wait()
        part_out = product(hidden[...], down_b[:, group * part : (group + 1) * part], INNER)
        out[:, group] = part_out.astype(jnp.bfloat16).reshape(blocks, capacity, part)
        hand_out(group, group, out, out_to, sem_o).start()
    for group in range(GROUPS):
        hand_out(group, group, out, out_to, sem_o).wait()


def weight_scratch(width, units):
    return [
        pltpu.VMEM((width, units), jnp.bfloat16),
        pltpu.VMEM((width, units), jnp.bfloat16),
        pltpu.VMEM((units, width), jnp.bfloat16),
    ]


def forward(order, moved, gate_w, up_w, down_w):
    blocks, _, capacity, part = moved.shape
    width, units = gate_w.shape
    total = blocks * capacity
    return pl.pallas_call(
        forward_kernel,
        out_shape=jax.ShapeDtypeStruct(moved.shape, jnp.bfloat16),
        in_specs=[SMEM] + [PLACE] * 4,
        out_specs=PLACE,
        scratch_shapes=[
            pltpu.VMEM((blocks, capacity, width), jnp.bfloat16),
            pltpu.VMEM(moved.shape, jnp.bfloat16),
        ]
        + weight_scratch(width, units)
        + [
            pltpu.VMEM((total, units), jnp.float32),
            pltpu.VMEM((total, units), jnp.float32),
            pltpu.VMEM((total, units), jnp.bfloat16),
        ]
        + [pltpu.SemaphoreType.DMA((GROUPS,))] * 6,
        compiler_params=pltpu.CompilerParams(vmem_limit_bytes=LIMIT),
        cost_estimate=pl.CostEstimate(
            flops=6 * total * width * units,
            bytes_accessed=6 * width * units + 4 * total * width,
            transcendentals=total * units,
        ),
    )(order, moved, gate_w, up_w, down_w)


def backward_kernel(*refs):
    order, own, other, table, gate_w, up_w, down_w = refs[:7]
    pieces_in = refs[7 : 7 + GROUPS]
    out_to, pieces = refs[7 + GROUPS], refs[8 + GROUPS : 8 + 2 * GROUPS]
    (
        out, gate_b, up_b, down_b, normed, cots, gate, up, grad, grad_gate, grad_up,
        scales, diffs, ones, twos, logits, sem_m, sem_o, sem_g, sem_u, sem_d,
    ) = refs[8 + 2 * GROUPS :]
    blocks, _, capacity, part = out.shape
    width = GROUPS * part
    arrive = [
        pltpu.make_async_copy(pieces_in[group], pieces[group], sem_m.at[group])
        for group in range(GROUPS)
    ]
    start(arrive)
    copies = fetch_rows(order, gate_w, gate_b, sem_g, part)
    copies_up = fetch_rows(order, up_w, up_b, sem_u, part)
    copies_down = fetch_columns(order, down_w, down_b, sem_d, part)
    start(copies)
    wait(arrive)

    def take(group, block):
        return pieces[group][block, 0:STEP, :]

    prepare(own[0], 0, take, other, table, normed, scales, diffs, logits, width, copies_up)

    @pl.loop(0, blocks)
    def _(block):
        at = pl.ds(pl.multiple_of(block * STEP, STEP), STEP)
        for group in range(GROUPS):
            cots[at, group * part : (group + 1) * part] = pieces[group][block, STEP : 2 * STEP, :]

    wait(copies)
    start(copies_down)
    gate[...] = product(normed[...], gate_b[...], INNER)
    wait(copies_up)
    up[...] = product(normed[...], up_b[...], INNER)
    wait(copies_down)
    grad[...] = product(cots[...], down_b[...], CONTRACT)

    @pl.loop(0, blocks)
    def _(block):
        at = pl.ds(pl.multiple_of(block * STEP, STEP), STEP)
        slope, value, lift = grad[at, :], gate[at, :], up[at, :]
        sig = jax.nn.sigmoid(value)
        silu = value * sig
        hidden = (silu * lift).astype(jnp.bfloat16).astype(jnp.float32)
        to_gate = (slope * lift * (sig * (1.0 + value * (1.0 - sig)))).astype(jnp.bfloat16)
        to_up = (slope * silu).astype(jnp.bfloat16)
        grad_gate[at, :] = to_gate
        grad_up[at, :] = to_up
        row_dot = even(lanes(slope * hidden))
        norm_dot = even(
            lanes(to_gate.astype(jnp.float32) * value + to_up.astype(jnp.float32) * lift)
        )
        scale, diff = scales[at, :], diffs[at, :]
        ours, theirs = jax.nn.sigmoid(diff), jax.nn.sigmoid(-diff)
        through = ours * theirs * row_dot
        ones[at, :] = scale * through
        twos[at, :] = scale * scale * ((ours * norm_dot + through * diff) / width)
        diffs[at, :] = scale * ours

    place = lax.broadcasted_iota(jnp.int32, (blocks * STEP, TABLE), 1)
    away = jnp.where((place < 24) & (lax.rem(place, 8) == own[0]), 1.0, 0.0)
    away = away - jnp.concatenate(
        [other[block, 0:STEP, 0:TABLE].astype(jnp.float32) for block in range(blocks)], axis=0
    )
    away = away.astype(jnp.bfloat16)
    for group in range(GROUPS):
        at = slice(group * part, (group + 1) * part)
        rows = product(grad_gate[...], gate_b[at, :], CONTRACT)
        rows = rows + product(grad_up[...], up_b[at, :], CONTRACT)
        turn = product(away, table[group], INNER)
        values = jnp.concatenate([take(group, block) for block in range(blocks)], axis=0)
        rows = (
            rows * (widen(diffs[...], part) * gains_of(table, group))
            + turn * widen(ones[...], part)
            - values.astype(jnp.float32) * widen(twos[...], part)
        )
        out[:, group] = rows.astype(jnp.bfloat16).reshape(blocks, capacity, part)
        hand_out(group, order[group], out, out_to, sem_o).start()
    for group in range(GROUPS):
        hand_out(group, order[group], out, out_to, sem_o).wait()


def backward(order, own, other, table, gate_w, up_w, down_w, pieces):
    blocks, double, part = pieces[0].shape
    capacity = double // 2
    width, units = gate_w.shape
    total = blocks * capacity
    small = pltpu.VMEM((total, 128), jnp.float32)
    return pl.pallas_call(
        backward_kernel,
        out_shape=jax.ShapeDtypeStruct((blocks, GROUPS, capacity, part), jnp.bfloat16),
        in_specs=[SMEM, SMEM, VMEM, VMEM, PLACE, PLACE, PLACE] + [PLACE] * GROUPS,
        out_specs=PLACE,
        scratch_shapes=[pltpu.VMEM((blocks, double, part), jnp.bfloat16)] * GROUPS
        + [pltpu.VMEM((blocks, GROUPS, capacity, part), jnp.bfloat16)]
        + weight_scratch(width, units)
        + [
            pltpu.VMEM((total, width), jnp.bfloat16),
            pltpu.VMEM((total, width), jnp.bfloat16),
            pltpu.VMEM((total, units), jnp.float32),
            pltpu.VMEM((total, units), jnp.float32),
            pltpu.VMEM((total, units), jnp.float32),
            pltpu.VMEM((total, units), jnp.bfloat16),
            pltpu.VMEM((total, units), jnp.bfloat16),
            small,
            small,
            small,
            small,
            pltpu.VMEM((total, TABLE), jnp.float32),
        ]
        + [pltpu.SemaphoreType.DMA((GROUPS,))] * 5,
        compiler_params=pltpu.CompilerParams(vmem_limit_bytes=LIMIT),
        cost_estimate=pl.CostEstimate(
            flops=10 * total * width * units,
            bytes_accessed=6 * width * units + 6 * total * width,
            transcendentals=total * units,
        ),
    )(order, own, other, table, gate_w, up_w, down_w, *pieces)


def finish_kernel(sel, home, base, out):
    blocks, groups, capacity, part = home.shape
    total = base[...].astype(jnp.float32)
    for group in range(groups):
        total = total + product(sel[...], home[:, group].reshape(blocks * capacity, part), INNER)
    out[...] = total.astype(jnp.bfloat16)


def finish(sel, home, base):
    return pl.pallas_call(
        finish_kernel,
        out_shape=jax.ShapeDtypeStruct(base.shape, jnp.bfloat16),
        in_specs=[VMEM] * 3,
        out_specs=VMEM,
        compiler_params=pltpu.CompilerParams(vmem_limit_bytes=LIMIT // 2),
    )(sel, home, base)


def finish_weighted_kernel(one_n, two_n, ones, twos, home, base, out):
    blocks, groups, capacity, part = home.shape
    first = jnp.zeros(base.shape, jnp.float32)
    second = jnp.zeros(base.shape, jnp.float32)
    for group in range(groups):
        rows = home[:, group].reshape(blocks * capacity, part)
        first = first + product(one_n[...], rows, INNER)
        second = second + product(two_n[...], rows, INNER)
    total = base[...].astype(jnp.float32) + first * widen(ones[...], part)
    out[...] = (total + second * widen(twos[...], part)).astype(jnp.bfloat16)


def finish_weighted(one_n, two_n, ones, twos, home, base):
    return pl.pallas_call(
        finish_weighted_kernel,
        out_shape=jax.ShapeDtypeStruct(base.shape, jnp.bfloat16),
        in_specs=[VMEM] * 6,
        out_specs=VMEM,
        compiler_params=pltpu.CompilerParams(vmem_limit_bytes=LIMIT // 2),
    )(one_n, two_n, ones, twos, home, base)


def send_home(pieces):
    experts, hids, capacity, part = pieces.shape
    home = swap(pieces.reshape(experts * hids, capacity, part), BOTH)
    return home.reshape(experts, hids, capacity, part)


def per_device(
    saved_input,
    cotangent,
    next_input,
    routes_saved,
    routes_next,
    norm_gain,
    router,
    expert_gate,
    expert_up,
    expert_down,
):
    gate_w, up_w, down_w = expert_gate[0, 0], expert_up[0, 0], expert_down[0, 0]
    tokens, part = saved_input.shape[1:]
    experts = lax.axis_size("expert")
    capacity = 3 * tokens // experts
    own = lax.axis_index("expert").astype(jnp.int32).reshape(1)
    order = arrival_order()

    tokens_next = with_table(next_input[0], norm_gain, router[0].T)
    tokens_next, routes = lax.optimization_barrier((tokens_next, (routes_saved[0].T, routes_next[0].T)))
    packed, sel_saved, one_next, two_next = pack(
        *routes, saved_input[0], cotangent[0], experts, capacity
    )
    near, packed = gather_near(tokens_next, packed)
    packed = swap(packed, "expert")
    moved_next, table, ones, twos = spread(
        routes[1], one_next, two_next, near + gather_far(near), experts
    )
    moved_next = swap(moved_next, "expert")
    other = packed[:, :, part:]
    near, _ = gather_near(packed[:, :, :part])
    near, moved_next = lax.optimization_barrier((near, moved_next))
    far = gather_far(near)
    out_next = forward(order, moved_next, gate_w, up_w, down_w)
    far, out_next = lax.optimization_barrier((far, out_next))
    pieces = near + far
    out_home = send_home(out_next)
    back_part = backward(order, own, other, table, gate_w, up_w, down_w, pieces)
    back_part, out_home = lax.optimization_barrier((back_part, out_home))
    back_home = send_home(back_part)

    forward_out = finish_weighted(one_next, two_next, ones, twos, out_home, next_input[0])
    grad_input = finish(sel_saved, back_home, cotangent[0])

    first_section = lax.axis_index("section") == 0
    outgoing = jnp.where(first_section, forward_out, grad_input)
    leaving = jnp.where(first_section, grad_input, forward_out)
    arriving = partner(outgoing, "section", 0)
    return (leaving[None], arriving[None])


def solution(mesh):
    placed = (
        P("section", "expert", "hid"),
        P("section", "expert", "hid"),
        P("section", "expert", "hid"),
        P("section", "expert", None),
        P("section", "expert", None),
        P("section", "hid"),
        P("section", "hid", None),
        P("section", "expert", None, "hid"),
        P("section", "expert", None, "hid"),
        P("section", "expert", "hid", None),
    )
    return jax.shard_map(
        per_device,
        mesh=mesh,
        in_specs=placed,
        out_specs=(P("section", "expert", "hid"), P("section", "expert", "hid")),
        check_vma=False,
    )
```
